32 devices in a mesh: dp: 8 (over z, x), mp: 4 (over y, core).
Axes of the slice: x: 2, y: 2, z: 4, core: 2. Of those that a mesh axis runs over, the one named last changes fastest.
Arguments:
- tokens: bfloat16 [2, 16384, 768], P(None, ('dp', 'mp')), may hold values from -6 to 6
- segment_ids: int32 [2, 16384], P(None, 'dp'), may hold values from 0 to 63, never falling along the last dimension, each value on 1 to 768 neighbouring positions
- norm1_gain: float32 [768], replicated, may hold values from 0.1 to 1.9
- norm1_bias: float32 [768], replicated, may hold values from -3 to 3
- w_qkv: bfloat16 [768, 3, 768], replicated, may hold values from -0.21875 to 0.21875
- conv_weight: float32 [3, 3, 768], P(None, None, 'mp'), may hold values from -3 to 3
- w_out: bfloat16 [768, 768], replicated, may hold values from -1.75 to 1.75
- norm2_gain: float32 [768], replicated, may hold values from 0.1 to 1.9
- norm2_bias: float32 [768], replicated, may hold values from -3 to 3
- w_in: bfloat16 [768, 3072], replicated, may hold values from -0.21875 to 0.21875
- w_down: bfloat16 [3072, 768], replicated, may hold values from -0.109375 to 0.109375
- cotangent: bfloat16 [2, 16384, 768], P(None, ('dp', 'mp')), may hold values from -6 to 6
Outputs:
- output: bfloat16 [2, 16384, 768], P(None, ('dp', 'mp'))
- input_grad: float32 [2, 16384, 768], P(None, ('dp', 'mp'))
- norm1_gain_grad: float32 [768], P('mp')
- norm1_bias_grad: float32 [768], P('mp')
- qkv_grad: float32 [768, 3, 768], P(None, None, 'mp')
- conv_grad: float32 [3, 3, 768], P(None, None, 'mp')
- out_grad: float32 [768, 768], P('mp')
- norm2_gain_grad: float32 [768], P('mp')
- norm2_bias_grad: float32 [768], P('mp')
- in_grad: float32 [768, 3072], replicated
- down_grad: float32 [3072, 768], replicated
The draws below stay inside these ranges and needn't reach their ends.
Inputs may be any that keep to these rules, and one draw needn't show every extreme that they name: `segment_ids`: segment numbers never fall along a row of 16384 tokens. A document may run on past the end of a sequence of 1024 tokens, but attention and the convolution still stop there, whatever the numbers.
All inputs are finite; a program needn't handle non-finite values.
Results may differ from the reference program's by a relative error of at most 0.015.
The reference program's roundings to bfloat16 on the way count: a program that leaves them out, or rounds other values in their place, can miss the bound.
Values may be sent and summed in bfloat16 or wider, within the bound.
No kernel may reach another device: no remote copies, remote signals or barrier semaphores. Data moves between devices by JAX's collectives and lax.ppermute only.
A program may use at most 256 MiB of HBM per device.

```python
import math
import jax
import jax.numpy as jnp
import numpy as np
from jax import lax

D = 768
HEADS = 12
FF = 3072
HEAD_DIM = 64
LEN = 1024
MB = 2
TOKENS_MB = 16384


def strengthened(values, key, source, target, parts, factor):
    def block_of(position):
        return (jnp.arange(values.shape[position]) // (values.shape[position] // parts)).reshape((-1,) + (1,) * (values.ndim - 1 - position))

    one_side = jax.random.permutation(key, parts)[block_of(target)]
    second = (block_of(target) + parts // 2) % parts
    return jnp.where((block_of(source) == one_side) | (block_of(source) == second), factor * values, values)


def steps_of(key, dims, cuts, least, high):
    def one(dim, blocks):
        steps = jax.random.uniform(jax.random.fold_in(jax.random.fold_in(key, 6), dim), (blocks,), jnp.float32, least / len(cuts), high / len(cuts))
        return jnp.repeat(jnp.exp(steps), dims[dim] // blocks).reshape((-1,) + (1,) * (len(dims) - dim - 1))

    loudness = one(*cuts[0])
    for cut in cuts[1:]:
        loudness = loudness * one(*cut)
    return loudness


def split_up(number_of, total, reach, lean):
    portions = [(1 << 20) // math.isqrt(grade ** lean) + 1 for grade in range(2, number_of + 1)]
    surplus, holding = total - reach - (number_of - 1), [1] * (number_of - 1)
    while surplus > 0:
        movable = [i for i in range(number_of - 1) if holding[i] < reach]
        whole, budget = sum([portions[i] for i in movable]), surplus
        for i in movable:
            more = min(reach - holding[i], max(1, budget * portions[i] // whole), surplus)
            holding[i] = holding[i] + more
            surplus = surplus - more
    return np.array([reach] + holding)


def uneven(own_key, number_of, total, reach, slope):
    if number_of == 2:
        one = jax.random.randint(own_key, (), max(1, total - reach), min(reach, total - 1) + 1)
        return jnp.stack([one, total - one])
    lengths = jnp.asarray(split_up(number_of, total, reach, slope), jnp.int32)
    pairs = (number_of - 1) // 2
    source_of, receiver = lengths[1:1 + 2 * pairs:2], lengths[2:2 + 2 * pairs:2]
    margin = jnp.minimum(source_of - 1, reach - receiver)
    moved = jax.random.randint(jax.random.fold_in(own_key, 1), (pairs,), 0, 1 << 20) % (margin + 1)
    lengths = lengths.at[1:1 + 2 * pairs:2].set(source_of - moved).at[2:2 + 2 * pairs:2].set(receiver + moved)
    return lengths[jax.random.permutation(jax.random.fold_in(own_key, 2), number_of)]


def gaussian(own_key, dims, spread, most, cuts=(), kind=jnp.bfloat16):
    gain = steps_of(own_key, dims, cuts, -0.22, 0.18) if cuts else 1.0
    values = jax.random.normal(own_key, dims, jnp.float32) * spread * gain
    return jnp.minimum(jnp.maximum(values, -most), most).astype(kind)


def gaussian_with(own_key, shape, width, bound, cuts, heavy, held_as=jnp.bfloat16):
    values = width * jax.random.normal(own_key, shape, jnp.float32)
    if cuts:
        values = values * steps_of(own_key, shape, cuts, -0.22, 0.18)
    return jnp.clip(strengthened(values, jax.random.fold_in(own_key, 3), *heavy), -bound, bound).astype(held_as)


def setup_inputs(seed: int = 0) -> dict:
    seeds = jax.random.split(jax.random.key(seed), 13)
    return {
        "tokens": gaussian(seeds[0], (MB, TOKENS_MB, D), 1.0, 6.0, ((1, 32),)),
        "segment_ids": jax.vmap(lambda own: jnp.searchsorted(jnp.cumsum(uneven(own, TOKENS_MB * 4 // LEN, TOKENS_MB, LEN * 3 // 4, 2)), jnp.arange(TOKENS_MB), side="right"))(jax.random.split(seeds[1], MB)).reshape((MB, TOKENS_MB)).astype(jnp.int32),
        "norm1_gain": jnp.clip(1.0 + 0.18 * jax.random.normal(seeds[2], (D,), jnp.float32), 0.1, 1.9),
        "norm1_bias": gaussian(seeds[3], (D,), 0.3, 3.0, (), jnp.float32),
        "w_qkv": gaussian(seeds[4], (D, 3, D), D ** -0.5, 0.21875),
        "conv_weight": gaussian(seeds[5], (3, 3, D), 0.6, 3.0, ((2, 4),), jnp.float32),
        "w_out": gaussian(seeds[6], (D, D), (D // 64) ** -0.5, 1.75),
        "norm2_gain": jnp.clip(1.0 + 0.18 * jax.random.normal(seeds[7], (D,), jnp.float32), 0.1, 1.9),
        "norm2_bias": gaussian(seeds[8], (D,), 0.3, 3.0, (), jnp.float32),
        "w_in": gaussian(seeds[9], (D, FF), D ** -0.5, 0.21875),
        "w_down": gaussian(seeds[10], (FF, D), FF ** -0.5, 0.109375),
        "cotangent": gaussian_with(seeds[11], (MB, TOKENS_MB, D), 1.0, 6.0, ((1, 32),), (1, 2, 32, 2.75)),
    }


HIGHEST = lax.Precision.HIGHEST
EPSILON = 1e-05
MASKED = -1e+30

@jax.custom_vjp
def low(v):
    return lax.optimization_barrier(v.astype(jnp.bfloat16)).astype(jnp.float32)

@jax.custom_vjp
def low_back(v):
    return v

def low_keep(v):
    return (low(v), None)

def low_pass(kept, grad):
    return (grad,)

def back_keep(v):
    return (v, None)

def back_low(kept, grad):
    return (low(grad),)
low.defvjp(low_keep, low_pass)
low_back.defvjp(back_keep, back_low)

def layer_norm(values, norm_gain, norm_bias):
    centred = values - lax.optimization_barrier(jnp.mean(values, axis=-1, keepdims=True))
    rstd_row = lax.rsqrt(lax.optimization_barrier(jnp.mean(centred * centred, axis=-1, keepdims=True)) + EPSILON)
    return centred * rstd_row * norm_gain + norm_bias

def delayed(values, shift_by):
    widths = [(0, 0), (shift_by, 0)] + [(0, 0)] * (values.ndim - 2)
    return jnp.pad(values, widths)[:, :LEN]

def attend(pieces):
    queries, keys_all, values_all, seg_row = pieces
    scaling = 1.0 / math.sqrt(HEAD_DIM)
    scores = low_back(jnp.einsum('qhd,khd->hqk', queries, keys_all, precision=HIGHEST) * scaling)
    places = lax.iota(jnp.int32, LEN)
    allowed = (places[None, :] <= places[:, None]) & (seg_row[None, :] == seg_row[:, None])
    scores = jnp.where(allowed[None], scores, MASKED)
    row_top = lax.optimization_barrier(jnp.max(scores, axis=-1, keepdims=True))
    weights = jnp.exp(scores - row_top)
    probabilities = weights / lax.optimization_barrier(jnp.sum(weights, axis=-1, keepdims=True))
    return jnp.einsum('hqk,khd->qhd', low(probabilities), values_all, precision=HIGHEST)

def forward(block, seg_block, gain_one, bias_one, qkv_weight, conv_taps, out_weight, gain_two, bias_two, in_weight, down_weight):
    batch = block.shape[0]
    normed_one = low(layer_norm(block, gain_one, bias_one))
    projected = low_back(low(jnp.einsum('bld,dce->blce', normed_one, qkv_weight, precision=HIGHEST)))
    places = lax.iota(jnp.int32, LEN)
    same_one = ((places >= 1)[None, :] & (delayed(seg_block, 1) == seg_block)).astype(projected.dtype)
    same_two = ((places >= 2)[None, :] & (delayed(seg_block, 2) == seg_block)).astype(projected.dtype)
    mixed = projected * conv_taps[:, 0] + delayed(projected, 1) * same_one[:, :, None, None] * conv_taps[:, 1] + delayed(projected, 2) * same_two[:, :, None, None] * conv_taps[:, 2]
    mixed = low(mixed)
    shaped = mixed.reshape(batch, LEN, 3, HEADS, HEAD_DIM)
    attended = lax.map(jax.checkpoint(attend), (shaped[:, :, 0], shaped[:, :, 1], shaped[:, :, 2], seg_block))
    attended = low_back(low(attended.reshape(batch, LEN, D)))
    branch = low_back(jnp.einsum('bld,de->ble', attended, out_weight, precision=HIGHEST))
    resid = block + branch
    normed_two = low(layer_norm(resid, gain_two, bias_two))
    hidden_pre = low_back(jnp.einsum('bld,df->blf', normed_two, in_weight, precision=HIGHEST))
    hidden = low(jnp.maximum(hidden_pre, 0.0) ** 2)
    return resid + jnp.einsum('blf,fd->bld', hidden, down_weight, precision=HIGHEST)

def reference(tokens, segment_ids, norm1_gain, norm1_bias, w_qkv, conv_weight, w_out, norm2_gain, norm2_bias, w_in, w_down, cotangent):
    seq_total = MB * TOKENS_MB // LEN
    group = math.gcd(seq_total, max(1, 4096 // LEN))
    blocks = seq_total // group
    token_blocks = tokens.astype(jnp.float32).reshape(blocks, group, LEN, D)
    seg_blocks = segment_ids.reshape(blocks, group, LEN)
    cot_blocks = cotangent.astype(jnp.float32).reshape(blocks, group, LEN, D)
    params = (norm1_gain, norm1_bias, w_qkv.astype(jnp.float32), conv_weight, w_out.astype(jnp.float32), norm2_gain, norm2_bias, w_in.astype(jnp.float32), w_down.astype(jnp.float32))

    def one_block(totals, item):
        block, seg_block, cot_block = item

        def apply_layer(block_in, gain_one, bias_one, qkv_weight, conv_taps, out_weight, gain_two, bias_two, in_weight, down_weight):
            return forward(block_in, seg_block, gain_one, bias_one, qkv_weight, conv_taps, out_weight, gain_two, bias_two, in_weight, down_weight)
        result, pull = jax.vjp(apply_layer, block, *params)
        grads = pull(cot_block)
        totals = tuple((total_part + grad_part for total_part, grad_part in zip(totals, grads[1:])))
        return (totals, (result.astype(jnp.bfloat16), grads[0]))
    start = tuple((jnp.zeros_like(param) for param in params))
    totals, (results, input_grads) = lax.scan(one_block, start, (token_blocks, seg_blocks, cot_blocks))
    return (results.reshape(MB, TOKENS_MB, D), input_grads.reshape(MB, TOKENS_MB, D), totals[0], totals[1], totals[2], totals[3], totals[4], totals[5], totals[6], totals[7], totals[8])
```

```python
import functools
import math

import jax
import jax.numpy as jnp
from jax import lax
from jax.experimental import pallas as pl
from jax.experimental.pallas import tpu as pltpu
from jax.sharding import PartitionSpec as P

HEAD_DIM = 64
LEN = 1024
LANES = 128
BLOCK = 256
EPSILON = 1e-05
MASKED = -1e30
F32 = jnp.float32
BF16 = jnp.bfloat16


def dot(a, b, dims):
    return lax.dot_general(a, b, (dims, ((), ())), preferred_element_type=F32)


def normalize(values, norm_gain, norm_bias):
    centred = values - jnp.mean(values, axis=-1, keepdims=True)
    rstd_row = lax.rsqrt(jnp.mean(centred * centred, axis=-1, keepdims=True) + EPSILON)
    scaled = centred * rstd_row
    return (scaled * norm_gain + norm_bias, scaled, rstd_row)


def normalize_back(gradient, scaled, rstd_row, norm_gain):
    grad_scaled = gradient * norm_gain
    inner_term = (
        grad_scaled
        - jnp.mean(grad_scaled, axis=-1, keepdims=True)
        - scaled * jnp.mean(grad_scaled * scaled, axis=-1, keepdims=True)
    )
    return (rstd_row * inner_term, jnp.sum(gradient * scaled, axis=0), jnp.sum(gradient, axis=0))


def attend_kernel(
    proj_q, proj_k, proj_v, taps, same, seg_col, seg_row, q_out, k_out, v_out, attended, lse, bias
):
    @pl.when(pl.program_id(0) == 0)
    def _():
        for first in range(0, LEN, BLOCK):
            width = first + BLOCK
            rows = first + lax.broadcasted_iota(jnp.int32, (BLOCK, width), 0)
            cols = lax.broadcasted_iota(jnp.int32, (BLOCK, width), 1)
            mine = jnp.concatenate([seg_col[first:width, :]] * (width // LANES), axis=1)
            allowed = (cols <= rows) & (mine == seg_row[0:1, :width])
            bias[first:width, :width] = jnp.where(allowed, 0.0, MASKED)

    same_one, same_two = same[0], same[1]
    for which, (source, target) in enumerate(((proj_q, q_out), (proj_k, k_out), (proj_v, v_out))):
        values = source[...].astype(F32)
        mixed = (
            values * taps[3 * which : 3 * which + 1, :]
            + pltpu.roll(values, 1, 0) * same_one * taps[3 * which + 1 : 3 * which + 2, :]
            + pltpu.roll(values, 2, 0) * same_two * taps[3 * which + 2 : 3 * which + 3, :]
        )
        target[...] = mixed.astype(BF16)
    scaling = 1.0 / math.sqrt(HEAD_DIM)
    lane = lax.broadcasted_iota(jnp.int32, (1, LANES), 1)
    for first in range(0, LEN, BLOCK):
        width = first + BLOCK
        queries = q_out[first:width, :] * jnp.asarray(scaling, BF16)
        parts = []
        for head in range(2):
            chosen = (lane >= HEAD_DIM) if head else (lane < HEAD_DIM)
            mine = jnp.where(chosen, queries, jnp.zeros_like(queries))
            scores = dot(mine, k_out[:width, :], ((1,), (1,))) + bias[first:width, :width]
            top = jnp.max(scores, axis=1, keepdims=True)
            weights = jnp.exp(scores - top)
            total = jnp.sum(weights, axis=1, keepdims=True)
            probs = (weights * (1.0 / total)).astype(BF16)
            parts.append((dot(probs, v_out[:width, :], ((1,), (0,))), top + jnp.log(total)))
        left = lane < HEAD_DIM
        attended[first:width, :] = jnp.where(left, parts[0][0], parts[1][0]).astype(BF16)
        logs = jnp.where(left, parts[0][1], parts[1][1])
        flipped = logs.T
        lse[0:1, first:width] = flipped[0:1, :]
        lse[1:2, first:width] = flipped[HEAD_DIM : HEAD_DIM + 1, :]


def attend_back_kernel(
    q_in,
    k_in,
    v_in,
    grads,
    attended,
    lse,
    proj_q,
    proj_k,
    proj_v,
    taps,
    same,
    seg_col,
    seg_row,
    back_q,
    back_k,
    back_v,
    tap_grads,
    bias,
    grad_k,
    grad_v,
    grad_qt,
):
    @pl.when(pl.program_id(0) == 0)
    def _():
        for first in range(0, LEN, BLOCK):
            width = first + BLOCK
            rows = lax.broadcasted_iota(jnp.int32, (width, BLOCK), 0)
            cols = first + lax.broadcasted_iota(jnp.int32, (width, BLOCK), 1)
            theirs = jnp.concatenate([seg_col[:width, :]] * (BLOCK // LANES), axis=1)
            allowed = (rows <= cols) & (theirs == seg_row[0:1, first:width])
            bias[:width, first:width] = jnp.where(allowed, 0.0, MASKED)

    scaling = 1.0 / math.sqrt(HEAD_DIM)
    lane = lax.broadcasted_iota(jnp.int32, (1, LANES), 1)
    keys_t = k_in[...].T
    inner = (grads[...].astype(F32) * attended[...].astype(F32)).T
    grad_k[...] = jnp.zeros_like(grad_k)
    grad_v[...] = jnp.zeros_like(grad_v)
    for head in range(2):
        low, high = head * HEAD_DIM, (head + 1) * HEAD_DIM
        chosen = (lane >= low) & (lane < high)
        inner_row = jnp.sum(inner[low:high, :], axis=0, keepdims=True)
        for first in range(0, LEN, BLOCK):
            width = first + BLOCK
            queries = q_in[first:width, :] * jnp.asarray(scaling, BF16)
            queries = jnp.where(chosen, queries, jnp.zeros_like(queries))
            outer = grads[first:width, :]
            outer = jnp.where(chosen, outer, jnp.zeros_like(outer))
            scores = dot(k_in[:width, :], queries, ((1,), (1,))) + bias[:width, first:width]
            probs = jnp.exp(scores - lse[head : head + 1, first:width])
            grad_probs = dot(v_in[:width, :], outer, ((1,), (1,)))
            grad_scores = (probs * (grad_probs - inner_row[:, first:width])).astype(BF16)
            grad_v[:width, :] += dot(probs.astype(BF16), outer, ((1,), (0,)))
            grad_k[:width, :] += dot(grad_scores, queries, ((1,), (0,)))
            grad_qt[low:high, first:width] = dot(
                keys_t[low:high, :width], grad_scores, ((1,), (0,))
            )
    same_one, same_two = same[0], same[1]
    grad_q = grad_qt[...].T * scaling
    for which, (gradient, source, target) in enumerate(
        ((grad_q, proj_q, back_q), (grad_k[...], proj_k, back_k), (grad_v[...], proj_v, back_v))
    ):
        values = source[...].astype(F32)
        weighted_one = gradient * same_one
        weighted_two = gradient * same_two
        row = 3 * which
        tap_grads[row : row + 1, :] = jnp.sum(gradient * values, axis=0, keepdims=True)
        tap_grads[row + 1 : row + 2, :] = jnp.sum(
            weighted_one * pltpu.roll(values, 1, 0), axis=0, keepdims=True
        )
        tap_grads[row + 2 : row + 3, :] = jnp.sum(
            weighted_two * pltpu.roll(values, 2, 0), axis=0, keepdims=True
        )
        target[...] = (
            gradient * taps[row : row + 1, :]
            + pltpu.roll(weighted_one, LEN - 1, 0) * taps[row + 1 : row + 2, :]
            + pltpu.roll(weighted_two, LEN - 2, 0) * taps[row + 2 : row + 3, :]
        ).astype(BF16)


def attend(projected, taps, same, seg_col, seg_row):
    width = projected.shape[1] // 3
    pairs = width // LANES

    def column(offset):
        return pl.BlockSpec((LEN, LANES), lambda h, offset=offset: (0, offset + h))

    def whole(shape):
        return pl.BlockSpec(shape, lambda h: (0,) * len(shape))

    return pl.pallas_call(
        attend_kernel,
        grid=(pairs,),
        in_specs=[
            column(0),
            column(pairs),
            column(2 * pairs),
            pl.BlockSpec((9, LANES), lambda h: (0, h)),
            whole((2, LEN, LANES)),
            whole((LEN, LANES)),
            whole((8, LEN)),
        ],
        out_specs=[column(0)] * 4 + [pl.BlockSpec((None, 2, LEN), lambda h: (h, 0, 0))],
        out_shape=[jax.ShapeDtypeStruct((LEN, width), BF16)] * 4
        + [jax.ShapeDtypeStruct((pairs, 2, LEN), F32)],
        scratch_shapes=[pltpu.VMEM((LEN, LEN), F32)],
        name="attend",
    )(projected, projected, projected, taps, same, seg_col, seg_row)


def attend_back(queries, keys, values, grads, attended, lse, projected, taps, same, seg_col, seg_row):
    width = queries.shape[1]
    pairs = width // LANES

    def column(offset):
        return pl.BlockSpec((LEN, LANES), lambda h, offset=offset: (0, offset + h))

    def whole(shape):
        return pl.BlockSpec(shape, lambda h: (0,) * len(shape))

    return pl.pallas_call(
        attend_back_kernel,
        grid=(pairs,),
        in_specs=[column(0)] * 5
        + [
            pl.BlockSpec((None, 2, LEN), lambda h: (h, 0, 0)),
            column(0),
            column(pairs),
            column(2 * pairs),
            pl.BlockSpec((9, LANES), lambda h: (0, h)),
            whole((2, LEN, LANES)),
            whole((LEN, LANES)),
            whole((8, LEN)),
        ],
        out_specs=[column(0)] * 3 + [pl.BlockSpec((9, LANES), lambda h: (0, h))],
        out_shape=[jax.ShapeDtypeStruct((LEN, width), BF16)] * 3
        + [jax.ShapeDtypeStruct((9, width), F32)],
        scratch_shapes=[
            pltpu.VMEM((LEN, LEN), F32),
            pltpu.VMEM((LEN, LANES), F32),
            pltpu.VMEM((LEN, LANES), F32),
            pltpu.VMEM((LANES, LEN), F32),
        ],
        name="attend_back",
    )(
        queries,
        keys,
        values,
        grads,
        attended,
        lse,
        projected,
        projected,
        projected,
        taps,
        same,
        seg_col,
        seg_row,
    )


def bit_of(axis, bit):
    return (lax.axis_index(axis) >> bit) & 1


def swap(values, axis, bit):
    count = lax.axis_size(axis)
    return lax.ppermute(values, axis, [(i, i ^ (1 << bit)) for i in range(count)])


def half_of(values, which, dim):
    size = values.shape[dim] // 2
    return lax.dynamic_slice_in_dim(values, which * size, size, dim)


def scatter_stage(values, axis, bit, dim):
    mine = bit_of(axis, bit)
    received = swap(half_of(values, 1 - mine, dim), axis, bit)
    return (half_of(values, mine, dim).astype(F32) + received.astype(F32)).astype(BF16)


def gather_stage(values, axis, bit, dim):
    low = bit_of(axis, bit) == 0
    received = swap(values, axis, bit)
    return jnp.concatenate(
        [jnp.where(low, values, received), jnp.where(low, received, values)], axis=dim
    )


def orders(dp_bits):
    dp = [("dp", bit) for bit in range(dp_bits)]
    y = ("mp", 1)
    first, second, rest = dp[0], dp[1:2], dp[2:]
    return (
        [first, y] + second + rest,
        [y] + second + [first] + rest,
        second + [first, y] + rest,
    )


def sum_everywhere(values, order, dims):
    for axis, bit in order:
        values = scatter_stage(values, axis, bit, dims[axis])
    return values


def spread(values, order, dims):
    for axis, bit in reversed(order):
        values = gather_stage(values, axis, bit, dims[axis])
    return values


def local(
    dp_bits,
    tokens,
    segment_ids,
    norm1_gain,
    norm1_bias,
    w_qkv,
    conv_weight,
    w_out,
    norm2_gain,
    norm2_bias,
    w_in,
    w_down,
    cotangent,
):
    width = tokens.shape[2]
    core = bit_of("mp", 0)
    group = lax.axis_index("mp")
    low = core == 0

    def own_sequence(pair):
        mine = lax.dynamic_index_in_dim(pair, core, 0, keepdims=False)
        theirs = swap(lax.dynamic_index_in_dim(pair, 1 - core, 0, keepdims=False), "mp", 0)
        return jnp.concatenate([jnp.where(low, mine, theirs), jnp.where(low, theirs, mine)], axis=0)

    def own_tokens(sequence, wire=BF16):
        rows = sequence.shape[0] // 2
        mine = lax.dynamic_slice_in_dim(sequence, core * rows, rows, 0)
        theirs = lax.dynamic_slice_in_dim(sequence, (1 - core) * rows, rows, 0)
        theirs = swap(theirs.astype(wire), "mp", 0).astype(sequence.dtype)
        return jnp.stack([jnp.where(low, mine, theirs), jnp.where(low, theirs, mine)], axis=0)

    taps_local = conv_weight.reshape(9, conv_weight.shape[2])
    pieces = [taps_local]
    for offset in range(1, 4):
        pieces.append(lax.ppermute(taps_local, "mp", [(i, i ^ offset) for i in range(4)]))
    stacked = jnp.stack(pieces, axis=0)
    taps = jnp.concatenate(
        [lax.dynamic_index_in_dim(stacked, group ^ i, 0, keepdims=False) for i in range(4)], axis=1
    )
    sequence_at = group >> 1
    seg = lax.dynamic_slice(segment_ids, (core, sequence_at * LEN), (1, LEN))[0]
    places = lax.iota(jnp.int32, LEN)
    same_one = (places >= 1) & (jnp.roll(seg, 1) == seg)
    same_two = (places >= 2) & (jnp.roll(seg, 2) == seg)
    same = jnp.broadcast_to(
        jnp.stack([same_one, same_two]).astype(F32)[:, :, None], (2, LEN, LANES)
    )
    seg_col = jnp.broadcast_to(seg[:, None], (LEN, LANES))
    seg_row = jnp.broadcast_to(seg[None, :], (8, LEN))

    token_rows = own_sequence(tokens).astype(F32)
    grad_output = own_sequence(cotangent)
    normed_one, scaled_one, rstd_one = normalize(token_rows, norm1_gain, norm1_bias)
    normed_one = normed_one.astype(BF16)
    qkv_flat = w_qkv.reshape(width, 3 * width)
    projected = dot(normed_one, qkv_flat, ((1,), (0,))).astype(BF16)
    queries, keys, values, attended, lse = attend(projected, taps, same, seg_col, seg_row)
    resid = token_rows + dot(attended, w_out, ((1,), (0,)))
    normed_two, scaled_two, rstd_two = normalize(resid, norm2_gain, norm2_bias)
    normed_two = normed_two.astype(BF16)
    active = jnp.maximum(dot(normed_two, w_in, ((1,), (0,))), 0.0)
    hidden = (active * active).astype(BF16)

    part_down = dot(hidden, grad_output, ((0,), (0,))).astype(BF16)
    grad_hidden = dot(grad_output, w_down, ((1,), (1,)))
    grad_pre = (grad_hidden * 2.0 * active).astype(BF16)
    part_in = dot(normed_two, grad_pre, ((0,), (0,))).astype(BF16)
    plans = orders(dp_bits)
    dims = {"dp": 0, "mp": 0}
    half_down = scatter_stage(part_down, "mp", 0, 0)
    half_in = scatter_stage(part_in, "mp", 0, 1)

    def all_sum(half):
        rows = half.shape[0] // 3
        done = []
        for index, order in enumerate(plans):
            piece = half[index * rows : (index + 1) * rows]
            piece = sum_everywhere(piece, order, dims)
            done.append(spread(piece, order, dims))
        return jnp.concatenate(done, axis=0)

    down_sum = all_sum(half_down)
    in_sum = all_sum(half_in)

    output = (resid + dot(hidden, w_down, ((1,), (0,)))).astype(BF16)
    grad_normed_two = dot(grad_pre, w_in, ((1,), (1,)))
    back_two, gain_two, bias_two = normalize_back(
        grad_normed_two, scaled_two, rstd_two, norm2_gain
    )
    grad_resid = grad_output.astype(F32) + back_two
    grad_branch = grad_resid.astype(BF16)
    part_out = dot(attended, grad_branch, ((0,), (0,))).astype(BF16)
    grad_attended = dot(grad_branch, w_out, ((1,), (1,))).astype(BF16)
    back_q, back_k, back_v, tap_grads = attend_back(
        queries, keys, values, grad_attended, attended, lse, projected, taps, same, seg_col, seg_row
    )
    grad_proj = jnp.concatenate([back_q, back_k, back_v], axis=1)
    part_qkv = dot(grad_proj, normed_one, ((0,), (0,))).astype(BF16)
    grad_normed_one = dot(grad_proj, qkv_flat, ((1,), (1,)))
    back_one, gain_one, bias_one = normalize_back(
        grad_normed_one, scaled_one, rstd_one, norm1_gain
    )
    input_grad = grad_resid + back_one

    share = width // 4
    by_owner = jnp.concatenate([part_qkv, part_out], axis=0).reshape(4, 2, 2, share, width)
    by_owner = by_owner.transpose(2, 1, 0, 3, 4).reshape(2, 2, 4 * share, width)
    half_heads = scatter_stage(by_owner, "mp", 0, 0)[0]
    rows = 4 * share // 3
    dims_heads = {"dp": 1, "mp": 0}
    done = []
    for index, order in enumerate(plans):
        piece = half_heads[:, index * rows : (index + 1) * rows]
        piece = sum_everywhere(piece, order, dims_heads)
        order_back = [stage for stage in order if stage[0] == "dp"]
        done.append(spread(piece, order_back, dims_heads))
    heads_sum = jnp.concatenate(done, axis=1)[0].astype(F32)
    qkv_grad = heads_sum[: 3 * share].T.reshape(width, 3, share)
    out_grad = heads_sum[3 * share :]

    small = jnp.concatenate(
        [tap_grads, gain_one[None], bias_one[None], gain_two[None], bias_two[None]], axis=0
    )
    for axis, bit in [("mp", 0), ("mp", 1)] + [("dp", bit) for bit in range(dp_bits)]:
        small = small + swap(small, axis, bit)
    small = lax.dynamic_slice_in_dim(small, group * share, share, 1)

    other_down = swap(down_sum, "mp", 0)
    other_in = swap(in_sum, "mp", 0)
    down_grad = jnp.concatenate(
        [jnp.where(low, down_sum, other_down), jnp.where(low, other_down, down_sum)], axis=0
    ).astype(F32)
    in_grad = jnp.concatenate(
        [jnp.where(low, in_sum, other_in), jnp.where(low, other_in, in_sum)], axis=1
    ).astype(F32)
    return (
        own_tokens(output),
        own_tokens(input_grad),
        small[9],
        small[10],
        qkv_grad,
        small[:9].reshape(3, 3, share),
        out_grad,
        small[11],
        small[12],
        in_grad,
        down_grad,
    )


def solution(mesh):
    placed = (
        P(None, ("dp", "mp"), None),
        P(None, "dp"),
        P(),
        P(),
        P(),
        P(None, None, "mp"),
        P(),
        P(),
        P(),
        P(),
        P(),
        P(None, ("dp", "mp"), None),
    )
    dp_bits = mesh.shape["dp"].bit_length() - 1
    return jax.shard_map(
        functools.partial(local, dp_bits),
        mesh=mesh,
        in_specs=placed,
        out_specs=(
            P(None, ("dp", "mp"), None),
            P(None, ("dp", "mp"), None),
            P("mp"),
            P("mp"),
            P(None, None, "mp"),
            P(None, None, "mp"),
            P("mp", None),
            P("mp"),
            P("mp"),
            P(),
            P(),
        ),
        check_vma=False,
    )
```

```python
import functools
import math

import jax
import jax.numpy as jnp
from jax import lax
from jax.experimental import pallas as pl
from jax.experimental.pallas import tpu as pltpu
from jax.sharding import PartitionSpec as P

HEAD_DIM = 64
LEN = 1024
LANES = 128
BLOCK = 256
EPSILON = 1e-05
MASKED = -1e30
F32 = jnp.float32
BF16 = jnp.bfloat16


def dot(a, b, dims):
    return lax.dot_general(a, b, (dims, ((), ())), preferred_element_type=F32)


def normalize(values, norm_gain, norm_bias):
    centred = values - jnp.mean(values, axis=-1, keepdims=True)
    rstd_row = lax.rsqrt(jnp.mean(centred * centred, axis=-1, keepdims=True) + EPSILON)
    scaled = centred * rstd_row
    return (scaled * norm_gain + norm_bias, scaled, rstd_row)


def normalize_back(gradient, scaled, rstd_row, norm_gain):
    grad_scaled = gradient * norm_gain
    inner_term = (
        grad_scaled
        - jnp.mean(grad_scaled, axis=-1, keepdims=True)
        - scaled * jnp.mean(grad_scaled * scaled, axis=-1, keepdims=True)
    )
    return (rstd_row * inner_term, jnp.sum(gradient * scaled, axis=0), jnp.sum(gradient, axis=0))


def attend_kernel(
    proj_q, proj_k, proj_v, taps, same, seg_col, seg_row, mixed_out, attended, lse, bias
):
    q_out, k_out, v_out = mixed_out.at[0], mixed_out.at[1], mixed_out.at[2]

    @pl.when(pl.program_id(0) == 0)
    def _():
        for first in range(0, LEN, BLOCK):
            width = first + BLOCK
            rows = first + lax.broadcasted_iota(jnp.int32, (BLOCK, width), 0)
            cols = lax.broadcasted_iota(jnp.int32, (BLOCK, width), 1)
            mine = jnp.concatenate([seg_col[first:width, :]] * (width // LANES), axis=1)
            allowed = (cols <= rows) & (mine == seg_row[0:1, :width])
            bias[first:width, :width] = jnp.where(allowed, 0.0, MASKED)

    same_one, same_two = same[0], same[1]
    for which, (source, target) in enumerate(((proj_q, q_out), (proj_k, k_out), (proj_v, v_out))):
        values = source[...].astype(F32)
        mixed = (
            values * taps[3 * which : 3 * which + 1, :]
            + pltpu.roll(values, 1, 0) * same_one * taps[3 * which + 1 : 3 * which + 2, :]
            + pltpu.roll(values, 2, 0) * same_two * taps[3 * which + 2 : 3 * which + 3, :]
        )
        target[...] = mixed.astype(BF16)
    scaling = 1.0 / math.sqrt(HEAD_DIM)
    lane = lax.broadcasted_iota(jnp.int32, (1, LANES), 1)
    for first in range(0, LEN, BLOCK):
        width = first + BLOCK
        queries = q_out[first:width, :] * jnp.asarray(scaling, BF16)
        parts = []
        for head in range(2):
            chosen = (lane >= HEAD_DIM) if head else (lane < HEAD_DIM)
            mine = jnp.where(chosen, queries, jnp.zeros_like(queries))
            scores = dot(mine, k_out[:width, :], ((1,), (1,))) + bias[first:width, :width]
            top = jnp.max(scores, axis=1, keepdims=True)
            weights = jnp.exp(scores - top)
            total = jnp.sum(weights, axis=1, keepdims=True)
            probs = (weights * (1.0 / total)).astype(BF16)
            parts.append((dot(probs, v_out[:width, :], ((1,), (0,))), top + jnp.log(total)))
        left = lane < HEAD_DIM
        attended[first:width, :] = jnp.where(left, parts[0][0], parts[1][0]).astype(BF16)
        logs = jnp.where(left, parts[0][1], parts[1][1])
        flipped = logs.T
        lse[0:1, first:width] = flipped[0:1, :]
        lse[1:2, first:width] = flipped[HEAD_DIM : HEAD_DIM + 1, :]


def attend_back_kernel(
    mixed_in,
    grads,
    attended,
    lse,
    proj_q,
    proj_k,
    proj_v,
    taps,
    same,
    seg_col,
    seg_row,
    back,
    tap_grads,
    bias,
    grad_k,
    grad_v,
    grad_qt,
):
    q_in, k_in, v_in = mixed_in.at[0], mixed_in.at[1], mixed_in.at[2]
    back_q, back_k, back_v = back.at[0], back.at[1], back.at[2]

    @pl.when(pl.program_id(0) == 0)
    def _():
        for first in range(0, LEN, BLOCK):
            width = first + BLOCK
            rows = lax.broadcasted_iota(jnp.int32, (width, BLOCK), 0)
            cols = first + lax.broadcasted_iota(jnp.int32, (width, BLOCK), 1)
            theirs = jnp.concatenate([seg_col[:width, :]] * (BLOCK // LANES), axis=1)
            allowed = (rows <= cols) & (theirs == seg_row[0:1, first:width])
            bias[:width, first:width] = jnp.where(allowed, 0.0, MASKED)

    scaling = 1.0 / math.sqrt(HEAD_DIM)
    lane = lax.broadcasted_iota(jnp.int32, (1, LANES), 1)
    keys_t = k_in[...].T
    inner = (grads[...].astype(F32) * attended[...].astype(F32)).T
    grad_k[...] = jnp.zeros_like(grad_k)
    grad_v[...] = jnp.zeros_like(grad_v)
    for head in range(2):
        low, high = head * HEAD_DIM, (head + 1) * HEAD_DIM
        chosen = (lane >= low) & (lane < high)
        inner_row = jnp.sum(inner[low:high, :], axis=0, keepdims=True)
        for first in range(0, LEN, BLOCK):
            width = first + BLOCK
            queries = q_in[first:width, :] * jnp.asarray(scaling, BF16)
            queries = jnp.where(chosen, queries, jnp.zeros_like(queries))
            outer = grads[first:width, :]
            outer = jnp.where(chosen, outer, jnp.zeros_like(outer))
            scores = dot(k_in[:width, :], queries, ((1,), (1,))) + bias[:width, first:width]
            probs = jnp.exp(scores - lse[head : head + 1, first:width])
            grad_probs = dot(v_in[:width, :], outer, ((1,), (1,)))
            grad_scores = (probs * (grad_probs - inner_row[:, first:width])).astype(BF16)
            grad_v[:width, :] += dot(probs.astype(BF16), outer, ((1,), (0,)))
            grad_k[:width, :] += dot(grad_scores, queries, ((1,), (0,)))
            grad_qt[low:high, first:width] = dot(
                keys_t[low:high, :width], grad_scores, ((1,), (0,))
            )
    same_one, same_two = same[0], same[1]
    grad_q = grad_qt[...].T * scaling
    for which, (gradient, source, target) in enumerate(
        ((grad_q, proj_q, back_q), (grad_k[...], proj_k, back_k), (grad_v[...], proj_v, back_v))
    ):
        values = source[...].astype(F32)
        weighted_one = gradient * same_one
        weighted_two = gradient * same_two
        row = 3 * which
        tap_grads[row : row + 1, :] = jnp.sum(gradient * values, axis=0, keepdims=True)
        tap_grads[row + 1 : row + 2, :] = jnp.sum(
            weighted_one * pltpu.roll(values, 1, 0), axis=0, keepdims=True
        )
        tap_grads[row + 2 : row + 3, :] = jnp.sum(
            weighted_two * pltpu.roll(values, 2, 0), axis=0, keepdims=True
        )
        target[...] = (
            gradient * taps[row : row + 1, :]
            + pltpu.roll(weighted_one, LEN - 1, 0) * taps[row + 1 : row + 2, :]
            + pltpu.roll(weighted_two, LEN - 2, 0) * taps[row + 2 : row + 3, :]
        ).astype(BF16)


def whole(shape):
    return pl.BlockSpec(shape, lambda *_: (0,) * len(shape))


def cost(flops, moved, exps=0):
    return pl.CostEstimate(flops=int(flops), transcendentals=int(exps), bytes_accessed=int(moved))


def attend(projected, taps, same, seg_col, seg_row):
    width = projected.shape[1] // 3
    pairs = width // LANES

    def column(offset):
        return pl.BlockSpec((LEN, LANES), lambda h, offset=offset: (0, offset + h))

    return pl.pallas_call(
        attend_kernel,
        grid=(pairs,),
        in_specs=[
            column(0),
            column(pairs),
            column(2 * pairs),
            pl.BlockSpec((9, LANES), lambda h: (0, h)),
            whole((2, LEN, LANES)),
            whole((LEN, LANES)),
            whole((8, LEN)),
        ],
        out_specs=[
            pl.BlockSpec((3, LEN, LANES), lambda h: (0, 0, h)),
            column(0),
            pl.BlockSpec((None, 2, LEN), lambda h: (h, 0, 0)),
        ],
        out_shape=[
            jax.ShapeDtypeStruct((3, LEN, width), BF16),
            jax.ShapeDtypeStruct((LEN, width), BF16),
            jax.ShapeDtypeStruct((pairs, 2, LEN), F32),
        ],
        scratch_shapes=[pltpu.VMEM((LEN, LEN), F32)],
        cost_estimate=cost(4 * LEN * LEN * width, 16 * LEN * width, LEN * LEN * pairs),
        name="attend",
    )(projected, projected, projected, taps, same, seg_col, seg_row)


def attend_back(first_pair, pairs, mixed, grads, attended, lse, projected, taps, same, seg_col, seg_row):
    all_pairs = grads.shape[1] // LANES

    def column(offset):
        return pl.BlockSpec((LEN, LANES), lambda h, offset=offset: (0, first_pair + offset + h))

    taken = pairs * LANES
    return pl.pallas_call(
        attend_back_kernel,
        grid=(pairs,),
        in_specs=[
            pl.BlockSpec((3, LEN, LANES), lambda h: (0, 0, first_pair + h)),
            column(0),
            column(0),
            pl.BlockSpec((None, 2, LEN), lambda h: (first_pair + h, 0, 0)),
            column(0),
            column(all_pairs),
            column(2 * all_pairs),
            pl.BlockSpec((9, LANES), lambda h: (0, first_pair + h)),
            whole((2, LEN, LANES)),
            whole((LEN, LANES)),
            whole((8, LEN)),
        ],
        out_specs=[
            pl.BlockSpec((3, LEN, LANES), lambda h: (0, 0, h)),
            pl.BlockSpec((9, LANES), lambda h: (0, h)),
        ],
        out_shape=[
            jax.ShapeDtypeStruct((3, LEN, taken), BF16),
            jax.ShapeDtypeStruct((9, taken), F32),
        ],
        scratch_shapes=[
            pltpu.VMEM((LEN, LEN), F32),
            pltpu.VMEM((LEN, LANES), F32),
            pltpu.VMEM((LEN, LANES), F32),
            pltpu.VMEM((LANES, LEN), F32),
        ],
        cost_estimate=cost(10 * LEN * LEN * taken, 22 * LEN * taken, LEN * LEN * pairs),
        name="attend_back",
    )(mixed, grads, attended, lse, projected, projected, projected, taps, same, seg_col, seg_row)


def front_kernel(core_ref, mine, theirs, gain, offset, weights, projected, normed, rows_out):
    @pl.when(pl.program_id(0) == 0)
    def _():
        core = core_ref[0]
        half = mine.shape[0]
        for source, at in ((mine, core), (theirs, 1 - core)):
            start = pl.multiple_of(at * half, half)
            rows_out[pl.ds(start, half), :] = source[...]
            value, _, _ = normalize(source[...].astype(F32), gain[...], offset[...])
            normed[pl.ds(start, half), :] = value.astype(BF16)

    projected[...] = dot(normed[...], weights[...], ((1,), (0,))).astype(BF16)


def front(core, tokens, theirs, gain, offset, weights):
    half, width = theirs.shape
    taken = width // 2
    return pl.pallas_call(
        front_kernel,
        grid_spec=pltpu.PrefetchScalarGridSpec(
            num_scalar_prefetch=1,
            grid=(6,),
            in_specs=[
                pl.BlockSpec((None, half, width), lambda j, c: (c[0], 0, 0)),
                whole((half, width)),
                whole((1, width)),
                whole((1, width)),
                pl.BlockSpec((None, width, taken), lambda j, c: (j // 2, 0, j % 2)),
            ],
            out_specs=[
                pl.BlockSpec((2 * half, taken), lambda j, c: (0, j)),
                whole((2 * half, width)),
                whole((2 * half, width)),
            ],
        ),
        out_shape=[
            jax.ShapeDtypeStruct((2 * half, 3 * width), BF16),
            jax.ShapeDtypeStruct((2 * half, width), BF16),
            jax.ShapeDtypeStruct((2 * half, width), BF16),
        ],
        cost_estimate=cost(12 * half * width * width, 14 * half * width + 6 * width * width),
        name="front",
    )(core, tokens, theirs, gain, offset, weights)


def feed_kernel(
    last, half_ref, normed, grads, in_block, down_block, out_in, back_in, part_down, part_in, out, back, out_sum, back_sum
):
    step = pl.program_id(0)

    @pl.when(step == 0)
    def _():
        out_sum[...] = out_in[...]
        back_sum[...] = back_in[...] if last else jnp.zeros_like(back_sum)

    active = jnp.maximum(dot(normed[...], in_block[...], ((1,), (0,))), 0.0)
    hidden = (active * active).astype(BF16)
    grad_hidden = dot(grads[...], down_block[...], ((1,), (1,)))
    grad_pre = (grad_hidden * 2.0 * active).astype(BF16)
    part_down[...] = dot(hidden, grads[...], ((0,), (0,))).astype(BF16)
    part_in[...] = dot(normed[...], grad_pre, ((0,), (0,))).astype(BF16)
    out_sum[...] += dot(hidden, down_block[...], ((1,), (0,)))
    back_sum[...] += dot(grad_pre, in_block[...], ((1,), (1,)))

    @pl.when(step == pl.num_programs(0) - 1)
    def _():
        out[...] = out_sum[...].astype(out.dtype)
        back[...] = back_sum[...]


def feed(half, last, normed, grads, w_in, w_down, out_in, back_in):
    rows, width = normed.shape
    units = w_in.shape[1]
    taken = 512
    steps = units // 2 // taken
    once = pl.Buffered(1)
    return pl.pallas_call(
        functools.partial(feed_kernel, last),
        grid_spec=pltpu.PrefetchScalarGridSpec(
            num_scalar_prefetch=1,
            grid=(steps,),
            in_specs=[
                whole((rows, width)),
                whole((rows, width)),
                pl.BlockSpec((width, taken), lambda j, h: (0, h[0] * steps + j)),
                pl.BlockSpec((taken, width), lambda j, h: (h[0] * steps + j, 0)),
                pl.BlockSpec((rows, width), lambda j, h: (0, 0), pipeline_mode=once),
                pl.BlockSpec(back_in.shape, lambda j, h: (0, 0), pipeline_mode=once),
            ],
            out_specs=[
                pl.BlockSpec((taken, width), lambda j, h: (j, 0)),
                pl.BlockSpec((width, taken), lambda j, h: (0, j)),
                pl.BlockSpec((rows, width), lambda j, h: (0, 0)),
                pl.BlockSpec((rows, width), lambda j, h: (0, 0)),
            ],
            scratch_shapes=[pltpu.VMEM((rows, width), F32), pltpu.VMEM((rows, width), F32)],
        ),
        out_shape=[
            jax.ShapeDtypeStruct((units // 2, width), BF16),
            jax.ShapeDtypeStruct((width, units // 2), BF16),
            jax.ShapeDtypeStruct((rows, width), BF16 if last else F32),
            jax.ShapeDtypeStruct((rows, width), F32),
        ],
        cost_estimate=cost(6 * rows * width * units, 16 * rows * width + 4 * width * units),
        name="feed",
    )(half, normed, grads, w_in, w_down, out_in, back_in)


def middle_kernel(
    resid, gradient, grads, attended, w_out, gain, grad_resid, grad_attended, part_out, norm_grads, total
):
    step = pl.program_id(0)
    _, scaled, rstd = normalize(resid[...], 1.0, 0.0)
    inner, gain_part, bias_part = normalize_back(gradient[...], scaled, rstd, gain[...])
    sums = jnp.concatenate([gain_part[None], bias_part[None]], axis=0)
    whole_grad = grads[...].astype(F32) + inner
    grad_resid[...] = whole_grad
    branch = whole_grad.astype(BF16)
    grad_attended[...] = dot(branch, w_out[...], ((1,), (1,))).astype(BF16)
    product = dot(attended[...], branch, ((0,), (0,)))

    @pl.when(step == 0)
    def _():
        total[...] = product
        norm_grads[...] = sums

    @pl.when(step > 0)
    def _():
        total[...] += product
        norm_grads[...] += sums

    @pl.when(step == pl.num_programs(0) - 1)
    def _():
        part_out[...] = total[...].astype(BF16)


def middle(resid, gradient, grads, attended, w_out, gain):
    rows, width = resid.shape
    block = pl.BlockSpec((BLOCK, width), lambda j: (j, 0))
    return pl.pallas_call(
        middle_kernel,
        grid=(rows // BLOCK,),
        in_specs=[block] * 4 + [whole((width, width)), whole((1, width))],
        out_specs=[block, block, whole((width, width)), whole((2, width))],
        out_shape=[
            jax.ShapeDtypeStruct((rows, width), F32),
            jax.ShapeDtypeStruct((rows, width), BF16),
            jax.ShapeDtypeStruct((width, width), BF16),
            jax.ShapeDtypeStruct((2, width), F32),
        ],
        scratch_shapes=[pltpu.VMEM((width, width), F32)],
        cost_estimate=cost(4 * rows * width * width, 18 * rows * width),
        name="middle",
    )(resid, gradient, grads, attended, w_out, gain)


def weight_kernel(back, normed, part):
    part[...] = dot(back[...], normed[...], ((0,), (0,))).astype(BF16)


def weight_grad(back, normed):
    _, rows, taken = back.shape
    width = normed.shape[1]
    return pl.pallas_call(
        weight_kernel,
        grid=(3,),
        in_specs=[pl.BlockSpec((None, rows, taken), lambda c: (c, 0, 0)), whole((rows, width))],
        out_specs=pl.BlockSpec((None, taken, width), lambda c: (c, 0, 0)),
        out_shape=jax.ShapeDtypeStruct((3, taken, width), BF16),
        cost_estimate=cost(6 * rows * width * taken, 8 * rows * taken),
        name="weight_grad",
    )(back, normed)


def last_kernel(*refs):
    backs, (weights, tokens, grad_resid, gain, input_grad, norm_grads) = refs[:-6], refs[-6:]
    step = pl.program_id(0)
    taken = backs[0].shape[2]
    gradient = None
    for index, back in enumerate(backs):
        for which in range(3):
            columns = slice(index * taken, (index + 1) * taken)
            product = dot(back[which], weights[which, :, columns], ((1,), (1,)))
            gradient = product if gradient is None else gradient + product
    _, scaled, rstd = normalize(tokens[...].astype(F32), 1.0, 0.0)
    inner, gain_part, bias_part = normalize_back(gradient, scaled, rstd, gain[...])
    sums = jnp.concatenate([gain_part[None], bias_part[None]], axis=0)
    input_grad[...] = grad_resid[...] + inner

    @pl.when(step == 0)
    def _():
        norm_grads[...] = sums

    @pl.when(step > 0)
    def _():
        norm_grads[...] += sums


def last(backs, weights, tokens, grad_resid, gain):
    rows, width = tokens.shape
    taken = backs[0].shape[2]
    block = pl.BlockSpec((BLOCK, width), lambda j: (j, 0))
    return pl.pallas_call(
        last_kernel,
        grid=(rows // BLOCK,),
        in_specs=[pl.BlockSpec((3, BLOCK, taken), lambda j: (0, j, 0))] * len(backs)
        + [whole((3, width, width)), block, block, whole((1, width))],
        out_specs=[block, whole((2, width))],
        out_shape=[
            jax.ShapeDtypeStruct((rows, width), F32),
            jax.ShapeDtypeStruct((2, width), F32),
        ],
        cost_estimate=cost(6 * rows * width * width, 16 * rows * width + 6 * width * width),
        name="last",
    )(*backs, weights, tokens, grad_resid, gain)


def bit_of(axis, bit):
    return (lax.axis_index(axis) >> bit) & 1


def swap(values, axis, bit):
    count = lax.axis_size(axis)
    return lax.ppermute(values, axis, [(i, i ^ (1 << bit)) for i in range(count)])


def half_of(values, which, dim):
    size = values.shape[dim] // 2
    return lax.dynamic_slice_in_dim(values, which * size, size, dim)


def added(left, right):
    return (left.astype(F32) + right.astype(F32)).astype(BF16)


def joined(mine, theirs, bit, dim):
    shape = mine.shape[:dim] + (2,) + mine.shape[dim:]
    at = lax.broadcasted_iota(jnp.int32, (2,) + (1,) * (mine.ndim - dim), 0)
    both = jnp.where(at == bit, jnp.expand_dims(mine, dim), jnp.expand_dims(theirs, dim))
    return jnp.broadcast_to(both, shape).reshape(
        mine.shape[:dim] + (2 * mine.shape[dim],) + mine.shape[dim + 1 :]
    )


class Stage:
    def __init__(self, dp_bits, even, odd, dims):
        self.dims = dims[even], dims[odd]
        count = 4 << dp_bits
        self.pairs = []
        flips = [1 << (bit + 2 if axis == "dp" else bit) for axis, bit in (even, odd)]
        for index in range(count):
            self.pairs.append((index, index ^ flips[index & 1]))
        self.bit = jnp.where(bit_of("mp", 0) == 0, bit_of(*even), bit_of(*odd))

    def send(self, values):
        return lax.ppermute(values, ("dp", "mp"), self.pairs)


class Sum:
    def __init__(self, values, stages, back):
        self.stages = list(stages)
        self.back = list(back)
        self.value = values
        self.outgoing = self.kept = None
        self.split()

    def split(self):
        if self.stages:
            stage = self.stages[0]
            dim = stage.dims[0]
            self.outgoing = half_of(self.value, 1 - stage.bit, dim)
            self.kept = half_of(self.value, stage.bit, dim)
        else:
            self.outgoing = self.kept = self.value

    def done(self):
        return not (self.stages or self.back)

    def state(self):
        return (self.outgoing, self.kept)

    def start(self):
        stage = self.stages[0] if self.stages else self.back[0]
        self.received = stage.send(self.outgoing)

    def finish(self):
        if self.stages:
            self.stages.pop(0)
            self.value = added(self.kept, self.received)
        else:
            stage = self.back.pop(0)
            self.value = joined(self.kept, self.received, stage.bit, stage.dims[0])
        self.split()


def local(
    dp_bits,
    tokens,
    segment_ids,
    norm1_gain,
    norm1_bias,
    w_qkv,
    conv_weight,
    w_out,
    norm2_gain,
    norm2_bias,
    w_in,
    w_down,
    cotangent,
):
    width = tokens.shape[2]
    core = bit_of("mp", 0)
    group = lax.axis_index("mp")
    rows = tokens.shape[1]

    def theirs_of(pair):
        return swap(lax.dynamic_index_in_dim(pair, 1 - core, 0, keepdims=False), "mp", 0)

    def own_tokens(sequence):
        mine = lax.dynamic_slice_in_dim(sequence, core * rows, rows, 0)
        theirs = lax.dynamic_slice_in_dim(sequence, (1 - core) * rows, rows, 0)
        theirs = swap(theirs.astype(BF16), "mp", 0).astype(sequence.dtype)
        at = lax.broadcasted_iota(jnp.int32, (2, 1, 1), 0)
        return jnp.where(at == core, mine[None], theirs[None])

    taps_local = conv_weight.reshape(9, conv_weight.shape[2])
    pieces = [taps_local]
    for offset in range(1, 4):
        pieces.append(lax.ppermute(taps_local, "mp", [(i, i ^ offset) for i in range(4)]))
    stacked = jnp.stack(pieces, axis=0)
    taps = jnp.concatenate(
        [lax.dynamic_index_in_dim(stacked, group ^ i, 0, keepdims=False) for i in range(4)], axis=1
    )
    seg = lax.dynamic_slice(segment_ids, (core, (group >> 1) * LEN), (1, LEN))[0]
    places = lax.iota(jnp.int32, LEN)
    same_one = (places >= 1) & (jnp.roll(seg, 1) == seg)
    same_two = (places >= 2) & (jnp.roll(seg, 2) == seg)
    same = jnp.broadcast_to(
        jnp.stack([same_one, same_two]).astype(F32)[:, :, None], (2, LEN, LANES)
    )
    seg_col = jnp.broadcast_to(seg[:, None], (LEN, LANES))
    seg_row = jnp.broadcast_to(seg[None, :], (8, LEN))
    masks = (taps, same, seg_col, seg_row)

    weights = w_qkv.transpose(1, 0, 2)
    grad_output = joined(
        lax.dynamic_index_in_dim(cotangent, core, 0, keepdims=False), theirs_of(cotangent), core, 0
    )
    projected, normed_one, token_rows = front(
        core[None], tokens, theirs_of(tokens), norm1_gain[None], norm1_bias[None], weights
    )
    mixed, attended, lse = attend(projected, *masks)
    resid = token_rows.astype(F32) + dot(attended, w_out, ((1,), (0,)))
    normed_two, _, _ = normalize(resid, norm2_gain, norm2_bias)
    normed_two = normed_two.astype(BF16)

    nothing = jnp.zeros((8, LANES), F32)
    down_other, in_other, out_sum, back_sum = feed(
        1 - core[None], False, normed_two, grad_output, w_in, w_down, resid, nothing
    )
    down_core, in_core = swap(down_other, "mp", 0), swap(in_other, "mp", 0)
    down_own, in_own, output, back_sum = feed(
        core[None], True, normed_two, grad_output, w_in, w_down, out_sum, back_sum
    )

    dp = [("dp", bit) for bit in range(dp_bits)]
    y = ("mp", 1)

    def stages(dims):
        return [Stage(dp_bits, dp[0], y, dims), Stage(dp_bits, y, dp[0], dims)] + [
            Stage(dp_bits, axis, axis, dims) for axis in dp[1:]
        ]

    flat = {axis: 0 for axis in dp + [y]}
    plan = stages(flat)
    down = Sum(added(down_own, down_core), plan, plan[::-1])
    into = Sum(added(in_own, in_core), plan, plan[::-1])

    results = {}
    backs, taps_grads, parts = [], [], []

    def chunk_middle(held):
        back_sum, resid, attended = held
        grad_resid, grad_attended, part_out, norm_two = middle(
            resid, back_sum, grad_output, attended, w_out, norm2_gain[None]
        )
        results.update(grad_resid=grad_resid, part_out=part_out, norm_two=norm_two)
        return (grad_attended,)

    def chunk_attend(first_pair, pairs):
        def run(held):
            (grad_attended,) = held
            back, tap_grads = attend_back(
                first_pair, pairs, mixed, grad_attended, attended, lse, projected, *masks
            )
            backs.append(back)
            taps_grads.append(tap_grads)
            return (grad_attended,)

        return run

    heads_at = {}

    chunks = [chunk_middle, chunk_attend(0, 2), chunk_attend(2, 2), chunk_attend(4, 2)]
    held = (back_sum, resid, attended)
    active = [down]
    waiting = [into]
    heads = None
    tick = 0
    while active or waiting or heads is None:
        if tick == len(chunks):
            parts = jnp.concatenate([weight_grad(back, normed_one) for back in backs], axis=1)
            share = width // 4
            by_owner = jnp.concatenate([parts, results["part_out"][None]], axis=0)
            by_owner = by_owner.reshape(4, 2, 2, share, width)
            dims_heads = {axis: 3 for axis in dp}
            dims_heads[y] = 1
            dims_heads[("mp", 0)] = 2
            cores = ("mp", 0)
            head_dp = [Stage(dp_bits, axis, axis, dims_heads) for axis in dp]
            plan_heads = [
                Stage(dp_bits, cores, cores, dims_heads),
                Stage(dp_bits, y, y, dims_heads),
            ] + head_dp
            heads = Sum(by_owner, plan_heads, head_dp[::-1])
            active.append(heads)
        state = tuple(unit.state() for unit in active)
        state, held = lax.optimization_barrier((state, held))
        for unit, (outgoing, kept) in zip(active, state):
            unit.outgoing, unit.kept = outgoing, kept
            unit.start()
        if tick < len(chunks):
            held = chunks[tick](held)
            if tick == len(chunks) - 1:
                held = (backs[-1],)
        for unit in active:
            unit.finish()
        active = [unit for unit in active if not unit.done()]
        active += waiting
        waiting = []
        tick += 1

    input_grad, norm_one = last(backs, weights, token_rows, results["grad_resid"], norm1_gain[None])
    heads_sum = heads.value.reshape(4, width // 4, width).astype(F32)
    qkv_grad = heads_sum[:3].transpose(2, 0, 1)
    out_grad = heads_sum[3]

    share = width // 4
    small = jnp.concatenate(
        [jnp.concatenate(taps_grads, axis=1), norm_one, results["norm_two"]], axis=0
    )
    for axis, bit in [("mp", 0), ("mp", 1)] + dp:
        small = small + swap(small, axis, bit)
    small = lax.dynamic_slice_in_dim(small, group * share, share, 1)

    down_grad = joined(down.value, swap(down.value, "mp", 0), core, 0).astype(F32)
    other_in = swap(into.value, "mp", 0)
    low = core == 0
    in_grad = jnp.concatenate(
        [jnp.where(low, into.value, other_in), jnp.where(low, other_in, into.value)], axis=1
    ).astype(F32)
    return (
        own_tokens(output),
        own_tokens(input_grad),
        small[9],
        small[10],
        qkv_grad,
        small[:9].reshape(3, 3, share),
        out_grad,
        small[11],
        small[12],
        in_grad,
        down_grad,
    )


def solution(mesh):
    placed = (
        P(None, ("dp", "mp"), None),
        P(None, "dp"),
        P(),
        P(),
        P(),
        P(None, None, "mp"),
        P(),
        P(),
        P(),
        P(),
        P(),
        P(None, ("dp", "mp"), None),
    )
    dp_bits = mesh.shape["dp"].bit_length() - 1
    return jax.shard_map(
        functools.partial(local, dp_bits),
        mesh=mesh,
        in_specs=placed,
        out_specs=(
            P(None, ("dp", "mp"), None),
            P(None, ("dp", "mp"), None),
            P("mp"),
            P("mp"),
            P(None, None, "mp"),
            P(None, None, "mp"),
            P("mp", None),
            P("mp"),
            P("mp"),
            P(),
            P(),
        ),
        check_vma=False,
    )
```

```python
import functools
import math

import jax
import jax.numpy as jnp
from jax import lax
from jax.experimental import pallas as pl
from jax.experimental.pallas import tpu as pltpu
from jax.sharding import PartitionSpec as P

HEAD_DIM = 64
LEN = 1024
LANES = 128
BLOCK = 256
EPSILON = 1e-05
MASKED = -1e30
F32 = jnp.float32
BF16 = jnp.bfloat16


def dot(a, b, dims):
    return lax.dot_general(a, b, (dims, ((), ())), preferred_element_type=F32)


def normalize(values, norm_gain, norm_bias):
    centred = values - jnp.mean(values, axis=-1, keepdims=True)
    rstd_row = lax.rsqrt(jnp.mean(centred * centred, axis=-1, keepdims=True) + EPSILON)
    scaled = centred * rstd_row
    return (scaled * norm_gain + norm_bias, scaled, rstd_row)


def normalize_back(gradient, scaled, rstd_row, norm_gain):
    grad_scaled = gradient * norm_gain
    inner_term = (
        grad_scaled
        - jnp.mean(grad_scaled, axis=-1, keepdims=True)
        - scaled * jnp.mean(grad_scaled * scaled, axis=-1, keepdims=True)
    )
    return (rstd_row * inner_term, jnp.sum(gradient * scaled, axis=0), jnp.sum(gradient, axis=0))


def attend_kernel(
    proj_q, proj_k, proj_v, taps, same, seg_col, seg_row, mixed_out, attended, lse, bias
):
    q_out, k_out, v_out = mixed_out.at[0], mixed_out.at[1], mixed_out.at[2]

    @pl.when(pl.program_id(0) == 0)
    def _():
        for first in range(0, LEN, BLOCK):
            width = first + BLOCK
            rows = first + lax.broadcasted_iota(jnp.int32, (BLOCK, width), 0)
            cols = lax.broadcasted_iota(jnp.int32, (BLOCK, width), 1)
            mine = jnp.concatenate([seg_col[first:width, :]] * (width // LANES), axis=1)
            allowed = (cols <= rows) & (mine == seg_row[0:1, :width])
            bias[first:width, :width] = jnp.where(allowed, 0.0, MASKED)

    same_one, same_two = same[0], same[1]
    for which, (source, target) in enumerate(((proj_q, q_out), (proj_k, k_out), (proj_v, v_out))):
        values = source[...].astype(F32)
        mixed = (
            values * taps[3 * which : 3 * which + 1, :]
            + pltpu.roll(values, 1, 0) * same_one * taps[3 * which + 1 : 3 * which + 2, :]
            + pltpu.roll(values, 2, 0) * same_two * taps[3 * which + 2 : 3 * which + 3, :]
        )
        target[...] = mixed.astype(BF16)
    scaling = 1.0 / math.sqrt(HEAD_DIM)
    lane = lax.broadcasted_iota(jnp.int32, (1, LANES), 1)
    for first in range(0, LEN, BLOCK):
        width = first + BLOCK
        queries = q_out[first:width, :] * jnp.asarray(scaling, BF16)
        parts = []
        for head in range(2):
            chosen = (lane >= HEAD_DIM) if head else (lane < HEAD_DIM)
            mine = jnp.where(chosen, queries, jnp.zeros_like(queries))
            scores = dot(mine, k_out[:width, :], ((1,), (1,))) + bias[first:width, :width]
            top = jnp.max(scores, axis=1, keepdims=True)
            weights = jnp.exp(scores - top)
            total = jnp.sum(weights, axis=1, keepdims=True)
            product = dot(weights.astype(BF16), v_out[:width, :], ((1,), (0,)))
            parts.append((product * (1.0 / total), top + jnp.log(total)))
        left = lane < HEAD_DIM
        attended[first:width, :] = jnp.where(left, parts[0][0], parts[1][0]).astype(BF16)
        logs = jnp.where(left, parts[0][1], parts[1][1])
        flipped = logs.T
        lse[0:1, first:width] = flipped[0:1, :]
        lse[1:2, first:width] = flipped[HEAD_DIM : HEAD_DIM + 1, :]


def attend_back_kernel(
    continued,
    *refs,
):
    attend_back_body(*(refs[2:] if continued else refs))


def attend_back_body(
    mixed_in,
    grads,
    attended,
    lse,
    proj_q,
    proj_k,
    proj_v,
    taps,
    same,
    seg_col,
    seg_row,
    back,
    tap_grads,
    bias,
    grad_k,
    grad_v,
    grad_qt,
):
    q_in, k_in, v_in = mixed_in.at[0], mixed_in.at[1], mixed_in.at[2]
    back_q, back_k, back_v = back.at[0], back.at[1], back.at[2]

    @pl.when(pl.program_id(0) == 0)
    def _():
        for first in range(0, LEN, BLOCK):
            width = first + BLOCK
            rows = lax.broadcasted_iota(jnp.int32, (width, BLOCK), 0)
            cols = first + lax.broadcasted_iota(jnp.int32, (width, BLOCK), 1)
            theirs = jnp.concatenate([seg_col[:width, :]] * (BLOCK // LANES), axis=1)
            allowed = (rows <= cols) & (theirs == seg_row[0:1, first:width])
            bias[:width, first:width] = jnp.where(allowed, 0.0, MASKED)

    scaling = 1.0 / math.sqrt(HEAD_DIM)
    lane = lax.broadcasted_iota(jnp.int32, (1, LANES), 1)
    keys_t = k_in[...].T
    inner = (grads[...].astype(F32) * attended[...].astype(F32)).T
    grad_k[...] = jnp.zeros_like(grad_k)
    grad_v[...] = jnp.zeros_like(grad_v)
    for head in range(2):
        low, high = head * HEAD_DIM, (head + 1) * HEAD_DIM
        chosen = (lane >= low) & (lane < high)
        inner_row = jnp.sum(inner[low:high, :], axis=0, keepdims=True)
        for first in range(0, LEN, BLOCK):
            width = first + BLOCK
            queries = q_in[first:width, :] * jnp.asarray(scaling, BF16)
            queries = jnp.where(chosen, queries, jnp.zeros_like(queries))
            outer = grads[first:width, :]
            outer = jnp.where(chosen, outer, jnp.zeros_like(outer))
            scores = dot(k_in[:width, :], queries, ((1,), (1,))) + bias[:width, first:width]
            probs = jnp.exp(scores - lse[head : head + 1, first:width])
            grad_probs = dot(v_in[:width, :], outer, ((1,), (1,)))
            grad_scores = (probs * (grad_probs - inner_row[:, first:width])).astype(BF16)
            grad_v[:width, :] += dot(probs.astype(BF16), outer, ((1,), (0,)))
            grad_k[:width, :] += dot(grad_scores, queries, ((1,), (0,)))
            grad_qt[low:high, first:width] = dot(
                keys_t[low:high, :width], grad_scores, ((1,), (0,))
            )
    same_one, same_two = same[0], same[1]
    grad_q = grad_qt[...].T * scaling
    for which, (gradient, source, target) in enumerate(
        ((grad_q, proj_q, back_q), (grad_k[...], proj_k, back_k), (grad_v[...], proj_v, back_v))
    ):
        values = source[...].astype(F32)
        row = 3 * which
        after_one = pltpu.roll(gradient * same_one, LEN - 1, 0)
        after_two = pltpu.roll(gradient * same_two, LEN - 2, 0)
        tap_grads[row : row + 1, :] = jnp.sum(gradient * values, axis=0, keepdims=True)
        tap_grads[row + 1 : row + 2, :] = jnp.sum(after_one * values, axis=0, keepdims=True)
        tap_grads[row + 2 : row + 3, :] = jnp.sum(after_two * values, axis=0, keepdims=True)
        target[...] = (
            gradient * taps[row : row + 1, :]
            + after_one * taps[row + 1 : row + 2, :]
            + after_two * taps[row + 2 : row + 3, :]
        ).astype(BF16)


def whole(shape):
    return pl.BlockSpec(shape, lambda *_: (0,) * len(shape))


def cost(flops, moved, exps=0):
    return pl.CostEstimate(flops=int(flops), transcendentals=int(exps), bytes_accessed=int(moved))


def attend(projected, taps, same, seg_col, seg_row):
    width = projected.shape[1] // 3
    pairs = width // LANES

    def column(offset):
        return pl.BlockSpec((LEN, LANES), lambda h, offset=offset: (0, offset + h))

    return pl.pallas_call(
        attend_kernel,
        grid=(pairs,),
        in_specs=[
            column(0),
            column(pairs),
            column(2 * pairs),
            pl.BlockSpec((9, LANES), lambda h: (0, h)),
            whole((2, LEN, LANES)),
            whole((LEN, LANES)),
            whole((8, LEN)),
        ],
        out_specs=[
            pl.BlockSpec((3, LEN, LANES), lambda h: (0, 0, h)),
            column(0),
            pl.BlockSpec((None, 2, LEN), lambda h: (h, 0, 0)),
        ],
        out_shape=[
            jax.ShapeDtypeStruct((3, LEN, width), BF16),
            jax.ShapeDtypeStruct((LEN, width), BF16),
            jax.ShapeDtypeStruct((pairs, 2, LEN), F32),
        ],
        scratch_shapes=[pltpu.VMEM((LEN, LEN), F32)],
        cost_estimate=cost(4 * LEN * LEN * width, 16 * LEN * width, LEN * LEN * pairs),
        name="attend",
    )(projected, projected, projected, taps, same, seg_col, seg_row)


def attend_back(first_pair, pairs, so_far, mixed, grads, attended, lse, projected, taps, same, seg_col, seg_row):
    width = grads.shape[1]
    all_pairs = width // LANES

    def column(offset):
        return pl.BlockSpec((LEN, LANES), lambda h, offset=offset: (0, first_pair + offset + h))

    stack = pl.BlockSpec((3, LEN, LANES), lambda h: (0, 0, first_pair + h))
    rows = pl.BlockSpec((9, LANES), lambda h: (0, first_pair + h))
    there = [pl.BlockSpec(memory_space=pl.ANY)] * 2 if so_far else []
    taken = pairs * LANES
    return pl.pallas_call(
        functools.partial(attend_back_kernel, bool(so_far)),
        grid=(pairs,),
        in_specs=there
        + [
            stack,
            column(0),
            column(0),
            pl.BlockSpec((None, 2, LEN), lambda h: (first_pair + h, 0, 0)),
            column(0),
            column(all_pairs),
            column(2 * all_pairs),
            rows,
            whole((2, LEN, LANES)),
            whole((LEN, LANES)),
            whole((8, LEN)),
        ],
        out_specs=[stack, rows],
        out_shape=[
            jax.ShapeDtypeStruct((3, LEN, width), BF16),
            jax.ShapeDtypeStruct((9, width), F32),
        ],
        scratch_shapes=[
            pltpu.VMEM((LEN, LEN), F32),
            pltpu.VMEM((LEN, LANES), F32),
            pltpu.VMEM((LEN, LANES), F32),
            pltpu.VMEM((LANES, LEN), F32),
        ],
        input_output_aliases={0: 0, 1: 1} if so_far else {},
        cost_estimate=cost(10 * LEN * LEN * taken, 22 * LEN * taken, LEN * LEN * pairs),
        name="attend_back",
    )(*so_far, mixed, grads, attended, lse, projected, projected, projected, taps, same, seg_col, seg_row)


def front_kernel(continued, place, *refs):
    tokens, gain, offset, weights, projected, normed, rows_out = refs[3:] if continued else refs

    @pl.when(pl.program_id(0) == 0)
    def _():
        rows_out[...] = tokens[...]
        value, _, _ = normalize(tokens[...].astype(F32), gain[...], offset[...])
        normed[...] = value.astype(BF16)

    projected[...] = dot(normed[...], weights[...], ((1,), (0,))).astype(BF16)


def front(place, tokens, gain, offset, weights, so_far):
    half, width = tokens.shape[-2:]
    if tokens.ndim == 3:
        source = pl.BlockSpec((None, half, width), lambda j, s: (s[0], 0, 0))
    else:
        source = whole((half, width))
    mine = pl.BlockSpec((half, width), lambda j, s: (s[0], 0))
    return pl.pallas_call(
        functools.partial(front_kernel, bool(so_far)),
        grid_spec=pltpu.PrefetchScalarGridSpec(
            num_scalar_prefetch=1,
            grid=(3,),
            in_specs=[pl.BlockSpec(memory_space=pl.ANY)] * len(so_far)
            + [
                source,
                whole((1, width)),
                whole((1, width)),
                pl.BlockSpec((None, width, width), lambda j, s: (j, 0, 0)),
            ],
            out_specs=[pl.BlockSpec((half, width), lambda j, s: (s[0], j)), mine, mine],
        ),
        out_shape=[
            jax.ShapeDtypeStruct((2 * half, 3 * width), BF16),
            jax.ShapeDtypeStruct((2 * half, width), BF16),
            jax.ShapeDtypeStruct((2 * half, width), BF16),
        ],
        input_output_aliases={1: 0, 2: 1, 3: 2} if so_far else {},
        cost_estimate=cost(6 * half * width * width, 14 * half * width + 6 * width * width),
        name="front",
    )(place, *so_far, tokens, gain, offset, weights)


def feed_kernel(first, last, place, *refs):
    step = pl.program_id(0)
    here = place[1]
    if first:
        tokens, attended, w_out, gain, offset, grads, in_block, down_block = refs[:8]
        resid_out, normed_out, parts, out, back, down_sum, in_sum = refs[8:]
        out_in = tokens[...].astype(F32) + dot(attended[...], w_out[...], ((1,), (0,)))
        resid_out[...] = out_in
        normed, _, _ = normalize(out_in, gain[...], offset[...])
        normed = normed.astype(BF16)
        normed_out[...] = normed
    else:
        normed_in, out_so_far, back_so_far, grads, in_block, down_block = refs[:6]
        normed = normed_in[...]
        out_in = out_so_far[...]
        if last:
            parts, out_theirs, out_mine, back, down_sum, in_sum = refs[6:]
        else:
            parts, out, back, down_sum, in_sum = refs[6:]
    gradient = grads[...]
    active = jnp.maximum(dot(normed, in_block[...], ((1,), (0,))), 0.0)
    hidden = (active * active).astype(BF16)
    grad_hidden = dot(gradient, down_block[...], ((1,), (1,)))
    grad_pre = (grad_hidden * 2.0 * active).astype(BF16)
    down = dot(hidden, gradient, ((0,), (0,)))
    into = dot(normed, grad_pre, ((0,), (0,)))

    @pl.when(step == 0)
    def _():
        down_sum[...] = down
        in_sum[...] = into

    @pl.when(step > 0)
    def _():
        down_sum[...] += down
        in_sum[...] += into

    result = out_in + dot(hidden, down_block[...], ((1,), (0,)))
    grad_normed = dot(grad_pre, in_block[...], ((1,), (1,)))
    back[...] = grad_normed if first else back_so_far[...] + grad_normed
    if last:
        half = pl.num_programs(0) // 2

        @pl.when(step < half)
        def _():
            out_theirs[...] = result.astype(BF16)

        @pl.when(step >= half)
        def _():
            out_mine[...] = result.astype(BF16)
    else:
        out[...] = result

    @pl.when(step == pl.num_programs(0) - 1)
    def _():
        blocks, _, rows, _ = parts.shape
        for index in range(blocks):
            parts[index ^ here, 0, :, :] = down_sum[index * rows : (index + 1) * rows, :].astype(BF16)
            parts[index ^ here, 1, :, :] = in_sum[index * rows : (index + 1) * rows, :].astype(BF16)


def feed(square, here, core, last, ahead, grads, w_in, w_down):
    rows, width = grads.shape
    first = len(ahead) == 5
    steps = rows // BLOCK
    half = steps // 2

    def turn(j, s):
        return (j + half * (1 - s[2])) % steps

    block = pl.BlockSpec((BLOCK, width), lambda j, s: (turn(j, s), 0))
    fixed = whole((width, width))
    row = whole((1, width))
    if first:
        ahead_specs = [block, block, fixed, row, row]
    else:
        ahead_specs = [block, block, block]
    sums = jax.ShapeDtypeStruct((rows, width), F32)
    low = jax.ShapeDtypeStruct((rows, width), BF16)
    out_specs = [pl.BlockSpec((8, 2, width // 8, width), lambda j, s: (0, 0, 0, 0))]
    out_shape = [jax.ShapeDtypeStruct((8, 2, width // 8, width), BF16)]
    if first:
        out_specs = [block, block] + out_specs
        out_shape = [sums, low] + out_shape
    if last:
        out_specs += [
            pl.BlockSpec((BLOCK, width), lambda j, s: (jnp.minimum(j, half - 1), 0)),
            pl.BlockSpec((BLOCK, width), lambda j, s: (jnp.maximum(j - half, 0), 0)),
        ]
        out_shape += [jax.ShapeDtypeStruct((rows // 2, width), BF16)] * 2
    else:
        out_specs.append(block)
        out_shape.append(sums)
    return pl.pallas_call(
        functools.partial(feed_kernel, first, last),
        grid_spec=pltpu.PrefetchScalarGridSpec(
            num_scalar_prefetch=1,
            grid=(steps,),
            in_specs=ahead_specs
            + [
                block,
                pl.BlockSpec((width, width), lambda j, s: (0, s[0])),
                pl.BlockSpec((width, width), lambda j, s: (s[0], 0)),
            ],
            out_specs=out_specs + [block],
            scratch_shapes=[pltpu.VMEM((width, width), F32), pltpu.VMEM((width, width), F32)],
        ),
        out_shape=out_shape + [sums],
        cost_estimate=cost(12 * rows * width * width, 16 * rows * width + 8 * width * width),
        name="feed",
    )(jnp.stack([square, here, core]), *ahead, grads, w_in, w_down)


def middle_kernel(
    resid, gradient, grads, w_out, gain, grad_resid, branch_out, grad_attended, norm_grads
):
    _, scaled, rstd = normalize(resid[...], 1.0, 0.0)
    inner, gain_part, bias_part = normalize_back(gradient[...], scaled, rstd, gain[...])
    sums = jnp.concatenate([gain_part[None], bias_part[None]], axis=0)
    whole_grad = grads[...].astype(F32) + inner
    grad_resid[...] = whole_grad
    branch = whole_grad.astype(BF16)
    branch_out[...] = branch
    grad_attended[...] = dot(branch, w_out[...], ((1,), (1,))).astype(BF16)
    before = jnp.where(pl.program_id(0) == 0, 0.0, norm_grads[...])
    norm_grads[...] = jnp.where(pl.program_id(0) == 0, sums, before + sums)


def middle(resid, gradient, grads, w_out, gain):
    rows, width = resid.shape
    block = pl.BlockSpec((BLOCK, width), lambda j: (j, 0))
    return pl.pallas_call(
        middle_kernel,
        grid=(rows // BLOCK,),
        in_specs=[block] * 3 + [whole((width, width)), whole((1, width))],
        out_specs=[block, block, block, whole((2, width))],
        out_shape=[
            jax.ShapeDtypeStruct((rows, width), F32),
            jax.ShapeDtypeStruct((rows, width), BF16),
            jax.ShapeDtypeStruct((rows, width), BF16),
            jax.ShapeDtypeStruct((2, width), F32),
        ],
        cost_estimate=cost(2 * rows * width * width, 18 * rows * width),
        name="middle",
    )(resid, gradient, grads, w_out, gain)


def weight_kernel(place, back, normed, attended, branch, mine, theirs):
    step = pl.program_id(0)
    core = place[0]

    def write(left, right):
        product = dot(left[...], right[...], ((0,), (0,))).astype(BF16)
        share = product.shape[0] // 4
        for half in range(2):
            for target, owner, here in ((mine, core, place[1]), (theirs, 1 - core, place[2])):
                high, low = step >> 1, step & 1
                even, odd = 4 * high + 2 * half + low, 4 * half + 2 * high + low
                at = ((1 - owner) * even + owner * odd) ^ here
                first = product[2 * half * share : (2 * half + 1) * share]
                second = product[(2 * half + 1) * share : (2 * half + 2) * share]
                target[at, :, :] = jnp.where(owner == 0, first, second)

    pl.when(step < 3)(lambda: write(back, normed))
    pl.when(step >= 3)(lambda: write(attended, branch))


def weight_grad(core, here_mine, here_theirs, back, normed, attended, branch):
    _, rows, width = back.shape
    share = width // 4
    return pl.pallas_call(
        weight_kernel,
        grid_spec=pltpu.PrefetchScalarGridSpec(
            num_scalar_prefetch=1,
            grid=(4,),
            in_specs=[pl.BlockSpec((None, rows, width), lambda t, s: (jnp.minimum(t, 2), 0, 0))]
            + [whole((rows, width))] * 3,
            out_specs=[whole((8, share, width))] * 2,
        ),
        out_shape=[jax.ShapeDtypeStruct((8, share, width), BF16)] * 2,
        cost_estimate=cost(8 * rows * width * width, 20 * rows * width),
        name="weight_grad",
    )(jnp.stack([core, here_mine, here_theirs]), back, normed, attended, branch)


def spread_kernel(place, *refs):
    pieces, (down, into) = refs[:4], refs[-2:]
    step = pl.program_id(0)
    rows = pieces[0].shape[2]
    odd = place[1 + step // 4] & 1
    for number, piece in enumerate(pieces):

        @pl.when(step // 2 == number)
        def _():
            for index in range(2):
                at = pl.multiple_of((index ^ odd) * rows, rows)
                down[pl.ds(at, rows), :] = piece[index, 0].astype(F32)
                into[pl.ds(at, rows), :] = piece[index, 1].astype(F32)


def spread(core, here_mine, here_theirs, square, units, pieces, so_far):
    _, _, rows, width = pieces[0].shape

    def taken(number):
        return pl.BlockSpec(
            (2, 2, rows, width), lambda t, s: (jnp.clip(t - 2 * number, 0, 1), 0, 0, 0)
        )

    def pair(t, s):
        return (t & 3) ^ (jnp.where(t < 4, s[1], s[2]) >> 1)

    def column(t, s):
        return 2 * square + (s[0] ^ (t >> 2))

    return pl.pallas_call(
        spread_kernel,
        grid_spec=pltpu.PrefetchScalarGridSpec(
            num_scalar_prefetch=1,
            grid=(8,),
            in_specs=[taken(number) for number in range(4)]
            + [pl.BlockSpec(memory_space=pl.ANY)] * len(so_far),
            out_specs=[
                pl.BlockSpec((2 * rows, width), lambda t, s: (4 * column(t, s) + pair(t, s), 0)),
                pl.BlockSpec((2 * rows, width), lambda t, s: (pair(t, s), column(t, s))),
            ],
        ),
        out_shape=[
            jax.ShapeDtypeStruct((units, width), F32),
            jax.ShapeDtypeStruct((width, units), F32),
        ],
        input_output_aliases={5: 0, 6: 1} if so_far else {},
        cost_estimate=cost(0, 24 * width * width),
        name="spread",
    )(jnp.stack([core, here_mine, here_theirs]), *pieces, *so_far)


def last_kernel(place, back, weights, tokens, grad_resid, gain, theirs, mine, norm_grads):
    step = pl.program_id(0)
    gradient = dot(back[0], weights[0], ((1,), (1,)))
    gradient += dot(back[1], weights[1], ((1,), (1,)))
    gradient += dot(back[2], weights[2], ((1,), (1,)))
    _, scaled, rstd = normalize(tokens[...].astype(F32), 1.0, 0.0)
    inner, gain_part, bias_part = normalize_back(gradient, scaled, rstd, gain[...])
    sums = jnp.concatenate([gain_part[None], bias_part[None]], axis=0)
    result = grad_resid[...] + inner
    half = pl.num_programs(0) // 2

    @pl.when(step < half)
    def _():
        theirs[...] = result.astype(BF16)

    @pl.when(step >= half)
    def _():
        mine[...] = result

    before = jnp.where(step == 0, 0.0, norm_grads[...])
    norm_grads[...] = jnp.where(step == 0, sums, before + sums)


def last(core, back, weights, tokens, grad_resid, gain):
    rows, width = tokens.shape
    steps = rows // BLOCK
    half = steps // 2

    def turn(j, s):
        return (j + half * (1 - s[0])) % steps

    block = pl.BlockSpec((BLOCK, width), lambda j, s: (turn(j, s), 0))
    return pl.pallas_call(
        last_kernel,
        grid_spec=pltpu.PrefetchScalarGridSpec(
            num_scalar_prefetch=1,
            grid=(steps,),
            in_specs=[
                pl.BlockSpec((3, BLOCK, width), lambda j, s: (0, turn(j, s), 0)),
                whole((3, width, width)),
                block,
                block,
                whole((1, width)),
            ],
            out_specs=[
                pl.BlockSpec((BLOCK, width), lambda j, s: (jnp.minimum(j, half - 1), 0)),
                pl.BlockSpec((BLOCK, width), lambda j, s: (jnp.maximum(j - half, 0), 0)),
                whole((2, width)),
            ],
        ),
        out_shape=[
            jax.ShapeDtypeStruct((rows // 2, width), BF16),
            jax.ShapeDtypeStruct((rows // 2, width), F32),
            jax.ShapeDtypeStruct((2, width), F32),
        ],
        cost_estimate=cost(6 * rows * width * width, 16 * rows * width + 6 * width * width),
        name="last",
    )(core[None], back, weights, tokens, grad_resid, gain)


def bit_of(axis, bit):
    return (lax.axis_index(axis) >> bit) & 1


def swap(values, axis, bit):
    count = lax.axis_size(axis)
    return lax.ppermute(values, axis, [(i, i ^ (1 << bit)) for i in range(count)])


def joined(mine, theirs, bit, dim):
    shape = mine.shape[:dim] + (2,) + mine.shape[dim:]
    at = lax.broadcasted_iota(jnp.int32, (2,) + (1,) * (mine.ndim - dim), 0)
    both = jnp.where(at == bit, jnp.expand_dims(mine, dim), jnp.expand_dims(theirs, dim))
    return jnp.broadcast_to(both, shape).reshape(
        mine.shape[:dim] + (2 * mine.shape[dim],) + mine.shape[dim + 1 :]
    )


class Stage:
    def __init__(self, dp_bits, even, odd):
        flips = [1 << (bit + 2 if axis == "dp" else bit) for axis, bit in (even, odd)]
        self.pairs = [(index, index ^ flips[index & 1]) for index in range(4 << dp_bits)]

    def send(self, values):
        return lax.ppermute(values, ("dp", "mp"), self.pairs)


class Sum:
    def __init__(self, terms, halving, adding, doubling):
        self.terms = terms
        self.count = terms[0].shape[0]
        self.halving, self.adding, self.doubling = list(halving), list(adding), list(doubling)
        self.pieces = None
        self.prepare()

    def total(self, low, high):
        result = None
        for term in self.terms:
            term = term[low:high].astype(F32)
            result = term if result is None else result + term
        return result.astype(BF16)

    def prepare(self):
        if self.halving:
            self.outgoing = self.total(self.count // 2, self.count)
        elif self.terms:
            self.outgoing = self.total(0, self.count)

    def start(self):
        stage = (self.halving or self.adding or self.doubling)[0]
        self.received = stage.send(self.outgoing)

    def finish(self):
        if self.halving:
            self.halving.pop(0)
            self.count //= 2
            self.terms.append(self.received)
            self.prepare()
        elif self.adding:
            self.adding.pop(0)
            self.terms = [self.outgoing, self.received]
            self.prepare()
            if self.adding:
                self.start()
                self.finish()
        else:
            self.doubling.pop(0)
            self.terms = []
            self.pieces = [self.outgoing, self.received]
            if self.doubling:
                self.outgoing = jnp.concatenate(self.pieces, axis=0)


class Whole:
    def __init__(self, values, stages):
        self.outgoing, self.stages = values, list(stages)

    def start(self):
        self.received = self.stages.pop(0).send(self.outgoing)

    def finish(self):
        self.outgoing = self.outgoing + self.received


class Once:
    def __init__(self, values, stage):
        self.outgoing, self.stage = values, stage

    def start(self):
        self.received = self.stage.send(self.outgoing)

    def finish(self):
        pass


def local(
    dp_bits,
    tokens,
    segment_ids,
    norm1_gain,
    norm1_bias,
    w_qkv,
    conv_weight,
    w_out,
    norm2_gain,
    norm2_bias,
    w_in,
    w_down,
    cotangent,
):
    width = tokens.shape[2]
    core = bit_of("mp", 0)
    group = lax.axis_index("mp")
    rows = tokens.shape[1]

    def theirs_of(pair):
        return swap(lax.dynamic_index_in_dim(pair, 1 - core, 0, keepdims=False), "mp", 0)

    def own_tokens(mine, theirs):
        at = lax.broadcasted_iota(jnp.int32, (2, 1, 1), 0)
        return jnp.where(at == core, mine[None], theirs.astype(mine.dtype)[None])

    their_tokens = theirs_of(tokens)
    taps_local = conv_weight.reshape(9, conv_weight.shape[2])
    pieces = [taps_local]
    for offset in range(1, 4):
        pieces.append(lax.ppermute(taps_local, "mp", [(i, i ^ offset) for i in range(4)]))
    stacked = jnp.stack(pieces, axis=0)
    taps = jnp.concatenate(
        [lax.dynamic_index_in_dim(stacked, group ^ i, 0, keepdims=False) for i in range(4)], axis=1
    )
    seg = lax.dynamic_slice(segment_ids, (core, (group >> 1) * LEN), (1, LEN))[0]
    places = lax.iota(jnp.int32, LEN)
    same_one = (places >= 1) & (jnp.roll(seg, 1) == seg)
    same_two = (places >= 2) & (jnp.roll(seg, 2) == seg)
    same = jnp.broadcast_to(
        jnp.stack([same_one, same_two]).astype(F32)[:, :, None], (2, LEN, LANES)
    )
    seg_col = jnp.broadcast_to(seg[:, None], (LEN, LANES))
    seg_row = jnp.broadcast_to(seg[None, :], (8, LEN))
    masks = (taps, same, seg_col, seg_row)

    weights = w_qkv.transpose(1, 0, 2)
    their_cotangent = theirs_of(cotangent)
    so_far = front(core[None], tokens, norm1_gain[None], norm1_bias[None], weights, ())
    so_far, their_tokens, masks = lax.optimization_barrier((so_far, their_tokens, masks))
    projected, normed_one, token_rows = front(
        1 - core[None], their_tokens, norm1_gain[None], norm1_bias[None], weights, so_far
    )
    mixed, attended, lse = attend(projected, *masks)
    grad_output = joined(
        lax.dynamic_index_in_dim(cotangent, core, 0, keepdims=False), their_cotangent, core, 0
    )

    dp = [("dp", bit) for bit in range(dp_bits)]
    y, cores = ("mp", 1), ("mp", 0)
    swap_cores = Stage(dp_bits, cores, cores)
    first, second = Stage(dp_bits, dp[0], y), Stage(dp_bits, y, dp[0])
    third = Stage(dp_bits, dp[1], dp[1])
    across = Stage(dp_bits, dp[0], dp[0])
    adding = [Stage(dp_bits, axis, axis) for axis in dp[2:]]
    x_bit, y_bit, z_bit = bit_of(*dp[0]), bit_of(*y), bit_of(*dp[1])
    here_even, here_odd = 4 * x_bit + 2 * y_bit + z_bit, 4 * y_bit + 2 * x_bit + z_bit
    here = jnp.where(core == 0, here_even, here_odd)
    here_theirs = jnp.where(core == 0, here_odd, here_even)
    place = (core, here, here_theirs)

    def feed_square(number, other, ahead):
        owner = 1 - core if other else core
        final = number == squares - 1 and not other
        return feed(
            2 * number + owner,
            here_theirs if other else here,
            core,
            final,
            ahead,
            grad_output,
            w_in,
            w_down,
        )

    squares = w_in.shape[1] // width // 2
    names = "abcdefgh"[:squares]
    found, units = {}, {}
    resid, normed_two, other, *ahead = feed_square(
        0, True, (token_rows, attended, w_out, norm2_gain[None], norm2_bias[None])
    )
    units["core" + names[0]] = Once(other, swap_cores)

    def chunk_own(number):
        name = names[number]

        def run(ahead):
            own, *ahead = feed_square(number, False, (normed_two, *ahead))
            units[name] = Sum(
                [own, units["core" + name].received], [first, second, third], adding, [third, second, first]
            )
            if number == squares - 1:
                theirs, found["output"], *ahead = ahead
                units["out"] = Once(theirs, swap_cores)
            return ahead

        return run

    def chunk_other(number):
        def run(ahead):
            other, *ahead = feed_square(number, True, (normed_two, *ahead))
            units["core" + names[number]] = Once(other, swap_cores)
            return ahead

        return run

    def chunk_middle(ahead):
        back_sum = ahead[-1]
        grad_resid, branch, grad_attended, norm_two = middle(
            resid, back_sum, grad_output, w_out, norm2_gain[None]
        )
        found.update(grad_resid=grad_resid, branch=branch, norm_two=norm_two, back=())
        return grad_attended

    def chunk_attend(first_pair):
        def run(held):
            grads = held[0] if isinstance(held, tuple) else held
            found["back"] = attend_back(
                first_pair, 2, found["back"], mixed, grads, attended, lse, projected, *masks
            )
            found["grads"] = grads
            return (grads, found["back"][0])

        return run

    def chunk_weights(held):
        mine, theirs = weight_grad(*place, held[1], normed_one, attended, found["branch"])
        found["mine"] = mine
        units["core"] = Once(theirs, swap_cores)
        return held[1]

    def chunk_last(back):
        theirs, found["input_grad"], found["norm_one"] = last(
            core, back, weights, token_rows, found["grad_resid"], norm1_gain[None]
        )
        units["h"] = Sum(
            [found["mine"], units["core"].received], [first, second, third], adding, [third, across]
        )
        small = jnp.concatenate([found["back"][1], found["norm_one"], found["norm_two"]], axis=0)
        units["small"] = Whole(small, [Stage(dp_bits, axis, axis) for axis in [cores, y] + dp])
        units["in"] = Once(theirs, swap_cores)
        return found["input_grad"]

    def chunk_spread(square, name):
        def run(held):
            pieces = list(units[name].pieces) + [units[name + str(i)].received for i in range(2)]
            found["spread"] = spread(
                *place, square, w_in.shape[1], pieces, found.get("spread", ())
            )
            return found["spread"]

        return run

    plan = [
        (("corea",), (), chunk_own(0)),
        (("a",), (), chunk_other(1)),
        (("a", "coreb"), (), chunk_own(1)),
        (("a", "b", "out"), (), chunk_middle),
        (("a", "b"), ("out",), chunk_attend(0)),
        (("a", "b"), (), chunk_attend(2)),
        (("a", "b"), (), chunk_attend(4)),
        (("a", "b"), (), chunk_weights),
        (("core", "b", "a0"), (), chunk_last),
        (("h", "b", "a1", "small", "in"), ("a0",), None),
        (("h", "b0", "small"), ("a1", "in"), chunk_spread(0, "a")),
        (("h", "b1", "small"), ("b0",), None),
        (("h", "small"), ("b1",), chunk_spread(1, "b")),
        (("h", "small"), (), None),
        (("h",), (), None),
    ]
    held = ahead
    for sent, arrived, chunk in plan:
        for name in sent:
            if name not in units:
                units[name] = Once(units[name[0]].pieces[int(name[1])], swap_cores)
        active, landed = [units[name] for name in sent], [units[name] for name in arrived]
        outgoing, received, held = lax.optimization_barrier(
            (tuple(unit.outgoing for unit in active), tuple(unit.received for unit in landed), held)
        )
        for unit, values in zip(landed, received):
            unit.received = values
        for unit, values in zip(active, outgoing):
            unit.outgoing = values
            unit.start()
        if chunk:
            held = chunk(held)
        for unit in active:
            unit.finish()

    small = units["small"]
    while small.stages:
        small.start()
        small.finish()
    share = width // 4
    small = lax.dynamic_slice_in_dim(small.outgoing, group * share, share, 1)
    heads = jnp.concatenate(units["h"].pieces, axis=0)
    heads = [
        lax.dynamic_index_in_dim(heads, index ^ (2 * x_bit + z_bit), 0, keepdims=False).astype(F32)
        for index in range(4)
    ]
    qkv_grad = jnp.stack(heads[:3]).transpose(2, 0, 1)
    out_grad = heads[3]
    down_grad, in_grad = found["spread"]
    return (
        own_tokens(found["output"], units["out"].received),
        own_tokens(found["input_grad"], units["in"].received),
        small[9],
        small[10],
        qkv_grad,
        small[:9].reshape(3, 3, share),
        out_grad,
        small[11],
        small[12],
        in_grad,
        down_grad,
    )


def solution(mesh):
    placed = (
        P(None, ("dp", "mp"), None),
        P(None, "dp"),
        P(),
        P(),
        P(),
        P(None, None, "mp"),
        P(),
        P(),
        P(),
        P(),
        P(),
        P(None, ("dp", "mp"), None),
    )
    dp_bits = mesh.shape["dp"].bit_length() - 1
    return jax.shard_map(
        functools.partial(local, dp_bits),
        mesh=mesh,
        in_specs=placed,
        out_specs=(
            P(None, ("dp", "mp"), None),
            P(None, ("dp", "mp"), None),
            P("mp"),
            P("mp"),
            P(None, None, "mp"),
            P(None, None, "mp"),
            P("mp", None),
            P("mp"),
            P("mp"),
            P(),
            P(),
        ),
        check_vma=False,
    )
```

```python
import functools
import math

import jax
import jax.numpy as jnp
from jax import lax
from jax.experimental import pallas as pl
from jax.experimental.pallas import tpu as pltpu
from jax.sharding import PartitionSpec as P

HEAD_DIM = 64
LEN = 1024
LANES = 128
BLOCK = 256
FEED_ROWS = 256
EPSILON = 1e-05
MASKED = -1e30
F32 = jnp.float32
BF16 = jnp.bfloat16


def dot(a, b, dims):
    return lax.dot_general(a, b, (dims, ((), ())), preferred_element_type=F32)


def normalize(values, norm_gain, norm_bias):
    centred = values - jnp.mean(values, axis=-1, keepdims=True)
    rstd_row = lax.rsqrt(jnp.mean(centred * centred, axis=-1, keepdims=True) + EPSILON)
    scaled = centred * rstd_row
    return (scaled * norm_gain + norm_bias, scaled, rstd_row)


def normalize_back(gradient, scaled, rstd_row, norm_gain):
    grad_scaled = gradient * norm_gain
    inner_term = (
        grad_scaled
        - jnp.mean(grad_scaled, axis=-1, keepdims=True)
        - scaled * jnp.mean(grad_scaled * scaled, axis=-1, keepdims=True)
    )
    return (rstd_row * inner_term, jnp.sum(gradient * scaled, axis=0), jnp.sum(gradient, axis=0))


def attend_kernel(
    place, proj_q, proj_k, proj_v, taps, segments, mixed_out, attended, lse, same, seg_col, seg_row, bias
):
    q_out, k_out, v_out = mixed_out.at[0], mixed_out.at[1], mixed_out.at[2]

    @pl.when(pl.program_id(0) == 0)
    def _():
        numbers = jnp.where(place[0] == 0, segments[0:1, :], segments[1:2, :])
        seg_row[...] = jnp.broadcast_to(numbers, seg_row.shape)
        column = jnp.broadcast_to(numbers.astype(F32), (LANES, LEN)).T
        seg_col[...] = column.astype(jnp.int32)
        at = lax.broadcasted_iota(jnp.int32, (LEN, LANES), 0)
        for shift in (1, 2):
            equal = (at >= shift) & (pltpu.roll(column, shift, 0) == column)
            same[shift - 1] = jnp.where(equal, 1.0, 0.0)
        for first in range(0, LEN, BLOCK):
            width = first + BLOCK
            rows = first + lax.broadcasted_iota(jnp.int32, (BLOCK, width), 0)
            cols = lax.broadcasted_iota(jnp.int32, (BLOCK, width), 1)
            mine = jnp.concatenate([seg_col[first:width, :]] * (width // LANES), axis=1)
            allowed = (cols <= rows) & (mine == seg_row[0:1, :width])
            bias[first:width, :width] = jnp.where(allowed, 0.0, MASKED)

    same_one, same_two = same[0], same[1]
    for which, (source, target) in enumerate(((proj_q, q_out), (proj_k, k_out), (proj_v, v_out))):
        values = source[...].astype(F32)
        mixed = (
            values * taps[3 * which : 3 * which + 1, :]
            + pltpu.roll(values, 1, 0) * same_one * taps[3 * which + 1 : 3 * which + 2, :]
            + pltpu.roll(values, 2, 0) * same_two * taps[3 * which + 2 : 3 * which + 3, :]
        )
        target[...] = mixed.astype(BF16)
    scaling = 1.0 / math.sqrt(HEAD_DIM)
    lane = lax.broadcasted_iota(jnp.int32, (1, LANES), 1)
    for first in range(0, LEN, BLOCK):
        width = first + BLOCK
        queries = q_out[first:width, :] * jnp.asarray(scaling, BF16)
        parts = []
        for head in range(2):
            chosen = (lane >= HEAD_DIM) if head else (lane < HEAD_DIM)
            mine = jnp.where(chosen, queries, jnp.zeros_like(queries))
            scores = dot(mine, k_out[:width, :], ((1,), (1,))) + bias[first:width, :width]
            top = jnp.max(scores, axis=1, keepdims=True)
            weights = jnp.exp(scores - top)
            total = jnp.sum(weights, axis=1, keepdims=True)
            product = dot(weights.astype(BF16), v_out[:width, :], ((1,), (0,)))
            parts.append((product * (1.0 / total), top + jnp.log(total)))
        left = lane < HEAD_DIM
        attended[first:width, :] = jnp.where(left, parts[0][0], parts[1][0]).astype(BF16)
        logs = jnp.where(left, parts[0][1], parts[1][1])
        flipped = logs.T
        lse[0:1, first:width] = flipped[0:1, :]
        lse[1:2, first:width] = flipped[HEAD_DIM : HEAD_DIM + 1, :]


def attend_back_kernel(
    continued,
    *refs,
):
    attend_back_body(*(refs[2:] if continued else refs))


def attend_back_body(
    mixed_in,
    grads,
    attended,
    lse,
    proj_q,
    proj_k,
    proj_v,
    taps,
    same,
    seg_col,
    seg_row,
    back,
    tap_grads,
    bias,
    grad_k,
    grad_v,
    grad_qt,
    keys_t,
    inner,
):
    q_in, k_in, v_in = mixed_in.at[0], mixed_in.at[1], mixed_in.at[2]
    back_q, back_k, back_v = back.at[0], back.at[1], back.at[2]

    @pl.when(pl.program_id(0) == 0)
    def _():
        for first in range(0, LEN, BLOCK):
            width = first + BLOCK
            rows = lax.broadcasted_iota(jnp.int32, (width, BLOCK), 0)
            cols = first + lax.broadcasted_iota(jnp.int32, (width, BLOCK), 1)
            theirs = jnp.concatenate([seg_col[:width, :]] * (BLOCK // LANES), axis=1)
            allowed = (rows <= cols) & (theirs == seg_row[0:1, first:width])
            bias[:width, first:width] = jnp.where(allowed, 0.0, MASKED)

    scaling = 1.0 / math.sqrt(HEAD_DIM)
    lane = lax.broadcasted_iota(jnp.int32, (1, LANES), 1)
    keys_t[...] = k_in[...].T
    inner[...] = (grads[...].astype(F32) * attended[...].astype(F32)).T
    grad_k[...] = jnp.zeros_like(grad_k)
    grad_v[...] = jnp.zeros_like(grad_v)

    def one_head(head, _):
        low = pl.multiple_of(head * HEAD_DIM, HEAD_DIM)
        mine = pl.ds(low, HEAD_DIM)
        chosen = (lane >= low) & (lane < low + HEAD_DIM)
        inner_row = jnp.sum(inner[mine, :], axis=0, keepdims=True)
        for first in range(0, LEN, BLOCK):
            width = first + BLOCK
            queries = q_in[first:width, :] * jnp.asarray(scaling, BF16)
            queries = jnp.where(chosen, queries, jnp.zeros_like(queries))
            outer = grads[first:width, :]
            outer = jnp.where(chosen, outer, jnp.zeros_like(outer))
            scores = dot(k_in[:width, :], queries, ((1,), (1,))) + bias[:width, first:width]
            probs = jnp.exp(scores - lse[pl.ds(head, 1), first:width])
            grad_probs = dot(v_in[:width, :], outer, ((1,), (1,)))
            grad_scores = (probs * (grad_probs - inner_row[:, first:width])).astype(BF16)
            grad_v[:width, :] += dot(probs.astype(BF16), outer, ((1,), (0,)))
            grad_k[:width, :] += dot(grad_scores, queries, ((1,), (0,)))
            grad_qt[mine, first:width] = dot(keys_t[mine, :width], grad_scores, ((1,), (0,)))
        return 0

    lax.fori_loop(0, 2, one_head, 0)
    same_one, same_two = same[0], same[1]
    grad_q = grad_qt[...].T * scaling
    for which, (gradient, source, target) in enumerate(
        ((grad_q, proj_q, back_q), (grad_k[...], proj_k, back_k), (grad_v[...], proj_v, back_v))
    ):
        values = source[...].astype(F32)
        row = 3 * which
        after_one = pltpu.roll(gradient * same_one, LEN - 1, 0)
        after_two = pltpu.roll(gradient * same_two, LEN - 2, 0)
        tap_grads[row : row + 1, :] = jnp.sum(gradient * values, axis=0, keepdims=True)
        tap_grads[row + 1 : row + 2, :] = jnp.sum(after_one * values, axis=0, keepdims=True)
        tap_grads[row + 2 : row + 3, :] = jnp.sum(after_two * values, axis=0, keepdims=True)
        target[...] = (
            gradient * taps[row : row + 1, :]
            + after_one * taps[row + 1 : row + 2, :]
            + after_two * taps[row + 2 : row + 3, :]
        ).astype(BF16)


def whole(shape):
    return pl.BlockSpec(shape, lambda *_: (0,) * len(shape))


def cost(flops, moved, exps=0):
    return pl.CostEstimate(flops=int(flops), transcendentals=int(exps), bytes_accessed=int(moved))


def attend(place, projected, taps, segments):
    width = projected.shape[1] // 3
    pairs = width // LANES

    def column(offset):
        return pl.BlockSpec((LEN, LANES), lambda h, s, offset=offset: (0, offset + h))

    return pl.pallas_call(
        attend_kernel,
        grid_spec=pltpu.PrefetchScalarGridSpec(
            num_scalar_prefetch=1,
            grid=(pairs,),
            in_specs=[
                column(0),
                column(pairs),
                column(2 * pairs),
                pl.BlockSpec((9, LANES), lambda h, s: (0, h)),
                pl.BlockSpec((2, LEN), lambda h, s: (0, s[3])),
            ],
            out_specs=[
                pl.BlockSpec((3, LEN, LANES), lambda h, s: (0, 0, h)),
                column(0),
                pl.BlockSpec((None, 2, LEN), lambda h, s: (h, 0, 0)),
                whole((2, LEN, LANES)),
                whole((LEN, LANES)),
                whole((8, LEN)),
            ],
            scratch_shapes=[pltpu.VMEM((LEN, LEN), F32)],
        ),
        out_shape=[
            jax.ShapeDtypeStruct((3, LEN, width), BF16),
            jax.ShapeDtypeStruct((LEN, width), BF16),
            jax.ShapeDtypeStruct((pairs, 2, LEN), F32),
            jax.ShapeDtypeStruct((2, LEN, LANES), F32),
            jax.ShapeDtypeStruct((LEN, LANES), jnp.int32),
            jax.ShapeDtypeStruct((8, LEN), jnp.int32),
        ],
        cost_estimate=cost(4 * LEN * LEN * width, 16 * LEN * width, LEN * LEN * pairs),
        name="attend",
    )(place, projected, projected, projected, taps, segments)


def attend_back(first_pair, pairs, so_far, mixed, grads, attended, lse, projected, taps, same, seg_col, seg_row):
    width = grads.shape[1]
    all_pairs = width // LANES

    def column(offset):
        return pl.BlockSpec((LEN, LANES), lambda h, offset=offset: (0, first_pair + offset + h))

    stack = pl.BlockSpec((3, LEN, LANES), lambda h: (0, 0, first_pair + h))
    rows = pl.BlockSpec((9, LANES), lambda h: (0, first_pair + h))
    there = [pl.BlockSpec(memory_space=pl.ANY)] * 2 if so_far else []
    taken = pairs * LANES
    return pl.pallas_call(
        functools.partial(attend_back_kernel, bool(so_far)),
        grid=(pairs,),
        in_specs=there
        + [
            stack,
            column(0),
            column(0),
            pl.BlockSpec((None, 2, LEN), lambda h: (first_pair + h, 0, 0)),
            column(0),
            column(all_pairs),
            column(2 * all_pairs),
            rows,
            whole((2, LEN, LANES)),
            whole((LEN, LANES)),
            whole((8, LEN)),
        ],
        out_specs=[stack, rows],
        out_shape=[
            jax.ShapeDtypeStruct((3, LEN, width), BF16),
            jax.ShapeDtypeStruct((9, width), F32),
        ],
        scratch_shapes=[
            pltpu.VMEM((LEN, LEN), F32),
            pltpu.VMEM((LEN, LANES), F32),
            pltpu.VMEM((LEN, LANES), F32),
            pltpu.VMEM((LANES, LEN), F32),
            pltpu.VMEM((LANES, LEN), BF16),
            pltpu.VMEM((LANES, LEN), F32),
        ],
        input_output_aliases={0: 0, 1: 1} if so_far else {},
        cost_estimate=cost(10 * LEN * LEN * taken, 22 * LEN * taken, LEN * LEN * pairs),
        name="attend_back",
    )(*so_far, mixed, grads, attended, lse, projected, projected, projected, taps, same, seg_col, seg_row)


def front_kernel(continued, place, *refs):
    tokens, gain, offset, weights, projected, normed, rows_out = refs[3:] if continued else refs

    @pl.when(pl.program_id(0) == 0)
    def _():
        rows_out[...] = tokens[...]
        value, _, _ = normalize(tokens[...].astype(F32), row_of(gain), row_of(offset))
        normed[...] = value.astype(BF16)

    projected[...] = dot(normed[...], weights[...], ((1,), (0,))).astype(BF16)


def row_of(vector):
    return vector[...].reshape(1, vector.shape[0])


def front(place, tokens, gain, offset, weights, so_far):
    _, half, width = tokens.shape
    other = int(bool(so_far))
    mine = pl.BlockSpec((half, width), lambda j, s: (s[0] ^ other, 0))
    return pl.pallas_call(
        functools.partial(front_kernel, bool(so_far)),
        grid_spec=pltpu.PrefetchScalarGridSpec(
            num_scalar_prefetch=1,
            grid=(3,),
            in_specs=[pl.BlockSpec(memory_space=pl.ANY)] * len(so_far)
            + [
                pl.BlockSpec((None, half, width), lambda j, s: (s[0], 0, 0)),
                whole((width,)),
                whole((width,)),
                pl.BlockSpec((None, width, width), lambda j, s: (j, 0, 0)),
            ],
            out_specs=[pl.BlockSpec((half, width), lambda j, s: (s[0] ^ other, j)), mine, mine],
        ),
        out_shape=[
            jax.ShapeDtypeStruct((2 * half, 3 * width), BF16),
            jax.ShapeDtypeStruct((2 * half, width), BF16),
            jax.ShapeDtypeStruct((2 * half, width), BF16),
        ],
        input_output_aliases={1: 0, 2: 1, 3: 2} if so_far else {},
        cost_estimate=cost(6 * half * width * width, 14 * half * width + 6 * width * width),
        name="front",
    )(place, *so_far, tokens, gain, offset, weights)


def feed_kernel(number, other, first, last, place, *refs):
    core, here = place[0], place[1 + other]
    square = 2 * number + (core ^ other)
    if first:
        gain, offset, tokens, attended, w_out, mine, theirs, w_in, w_down = refs[:9]
        resid_out, normed_out, grads_out, parts_out, out, back_out = refs[9:15]
        tokens_held, attended_held, weights_held = refs[-3:]
        scratch = refs[15:-3]
    else:
        normed_in, out_in, back_in, grads_in, w_in, w_down = refs[:6]
        if last:
            parts_out, out_theirs, out_mine, back_out = refs[6:10]
            result_low = refs[-1]
            scratch = refs[10:-1]
        else:
            parts_out, out, back_out = refs[6:9]
            scratch = refs[9:]
    lefts, rights, in_block, down_block, total, back, parts, sems = scratch
    hidden, normed, grads, grad_pre = lefts.at[0], lefts.at[1], rights.at[0], rights.at[1]
    count = normed.shape[0]
    width = in_block.shape[1]
    half = normed.shape[0] // 2
    columns = pl.ds(pl.multiple_of(square * width, width), width)
    my_rows = pl.ds(pl.multiple_of(core * half, half), half)
    their_rows = pl.ds(pl.multiple_of((1 - core) * half, half), half)
    flights = []

    def copy(source, target):
        flight = pltpu.make_async_copy(source, target, sems.at[len(flights)])
        flights.append(flight)
        flight.start()
        return flight

    if first:
        early = [copy(attended, attended_held), copy(w_out, weights_held), copy(tokens, tokens_held)]
        later = [copy(w_in.at[:, columns], in_block)]
        last_in = [
            copy(mine.at[core], grads.at[my_rows, :]),
            copy(theirs.at[core], grads.at[their_rows, :]),
            copy(w_down.at[columns, :], down_block),
        ]
    else:
        early = [copy(normed_in, normed)]
        later = [copy(w_in.at[:, columns], in_block)]
        last_in = [copy(grads_in, grads), copy(w_down.at[columns, :], down_block)]
        total_in = copy(out_in, total)
        back_so_far = copy(back_in, back)
    for flight in early:
        flight.wait()
    writes = []
    if first:

        def begin(step, _):
            at = pl.ds(pl.multiple_of(step * BLOCK, BLOCK), BLOCK)
            product = dot(attended_held[at, :], weights_held[...], ((1,), (0,)))
            value = tokens_held[at, :].astype(F32) + product
            total[at, :] = value
            value, _, _ = normalize(value, row_of(gain), row_of(offset))
            normed[at, :] = value.astype(BF16)
            return 0

        lax.fori_loop(0, count // BLOCK, begin, 0)
        resid_flight = copy(total, resid_out)
        writes.append(copy(normed, normed_out))
    for flight in later + last_in:
        flight.wait()
    if first:
        writes.append(copy(grads, grads_out))
    size = FEED_ROWS

    def inner(step, _):
        at = pl.ds(pl.multiple_of(step * size, size), size)
        active = jnp.maximum(dot(normed[at, :], in_block[...], ((1,), (0,))), 0.0)
        hidden[at, :] = (active * active).astype(BF16)
        grad_hidden = dot(grads[at, :], down_block[...], ((1,), (1,)))
        grad_pre[at, :] = (grad_hidden * 2.0 * active).astype(BF16)
        return 0

    lax.fori_loop(0, count // size, inner, 0)
    blocks, _, rows, _ = parts.shape
    taken = width // 2

    def weigh(step, _):
        which, half_at = step // 2, step % 2
        at = pl.ds(pl.multiple_of(half_at * taken, taken), taken)
        product = dot(lefts[which, :, at], rights[which], ((0,), (0,))).astype(BF16)
        for index in range(blocks // 2):
            target = (half_at * (blocks // 2) + index) ^ here
            parts[target, which, :, :] = product[index * rows : (index + 1) * rows, :]
        return 0

    lax.fori_loop(0, 4, weigh, 0)
    writes.append(copy(parts, parts_out))
    if first:
        resid_flight.wait()
    else:
        total_in.wait()
        back_so_far.wait()

    def outer(step, _):
        at = pl.ds(pl.multiple_of(step * size, size), size)
        value = total[at, :] + dot(hidden[at, :], down_block[...], ((1,), (0,)))
        if last:
            result_low[at, :] = value.astype(BF16)
        else:
            total[at, :] = value
        product = dot(grad_pre[at, :], in_block[...], ((1,), (1,)))
        back[at, :] = product if first else back[at, :] + product
        return 0

    lax.fori_loop(0, count // size, outer, 0)
    if last:
        writes.append(copy(result_low.at[their_rows, :], out_theirs))
        writes.append(copy(result_low.at[my_rows, :], out_mine))
    else:
        writes.append(copy(total, out))
    writes.append(copy(back, back_out))
    for flight in writes:
        flight.wait()


def feed(number, other, last, place, ahead, w_in, w_down):
    first = len(ahead) == 7
    rows, width = ahead[2].shape
    sums = jax.ShapeDtypeStruct((rows, width), F32)
    low = jax.ShapeDtypeStruct((rows, width), BF16)
    half = jax.ShapeDtypeStruct((rows // 2, width), BF16)
    out_shape = [jax.ShapeDtypeStruct((8, 2, width // 8, width), BF16)]
    if first:
        out_shape = [sums, low, low] + out_shape
    out_shape += [half, half, sums] if last else [sums, sums]
    anywhere = pl.BlockSpec(memory_space=pl.ANY)
    in_specs = [anywhere] * (len(ahead) + 2)
    if first:
        in_specs[:2] = [whole((width,))] * 2
    held = [
        pltpu.VMEM((2, rows, width), BF16),
        pltpu.VMEM((2, rows, width), BF16),
        pltpu.VMEM((width, width), BF16),
        pltpu.VMEM((width, width), BF16),
        pltpu.VMEM((rows, width), F32),
        pltpu.VMEM((rows, width), F32),
        pltpu.VMEM((8, 2, width // 8, width), BF16),
        pltpu.SemaphoreType.DMA((16,)),
    ]
    if first:
        held += [
            pltpu.VMEM((rows, width), BF16),
            pltpu.VMEM((rows, width), BF16),
            pltpu.VMEM((width, width), BF16),
        ]
    if last:
        held.append(pltpu.VMEM((rows, width), BF16))
    return pl.pallas_call(
        functools.partial(feed_kernel, number, int(other), first, last),
        grid_spec=pltpu.PrefetchScalarGridSpec(
            num_scalar_prefetch=1,
            grid=(1,),
            in_specs=in_specs,
            out_specs=[anywhere] * len(out_shape),
            scratch_shapes=held,
        ),
        out_shape=out_shape,
        cost_estimate=cost(12 * rows * width * width, 16 * rows * width + 8 * width * width),
        name="feed",
    )(place, *ahead, w_in, w_down)


def middle_kernel(
    resid, gradient, grads, w_out, gain, grad_resid, branch_out, grad_attended, norm_grads
):
    _, scaled, rstd = normalize(resid[...], 1.0, 0.0)
    inner, gain_part, bias_part = normalize_back(gradient[...], scaled, rstd, row_of(gain))
    sums = jnp.concatenate([gain_part[None], bias_part[None]], axis=0)
    whole_grad = grads[...].astype(F32) + inner
    grad_resid[...] = whole_grad
    branch = whole_grad.astype(BF16)
    branch_out[...] = branch
    grad_attended[...] = dot(branch, w_out[...], ((1,), (1,))).astype(BF16)
    before = jnp.where(pl.program_id(0) == 0, 0.0, norm_grads[...])
    norm_grads[...] = jnp.where(pl.program_id(0) == 0, sums, before + sums)


def middle(resid, gradient, grads, w_out, gain):
    rows, width = resid.shape
    block = pl.BlockSpec((BLOCK, width), lambda j: (j, 0))
    return pl.pallas_call(
        middle_kernel,
        grid=(rows // BLOCK,),
        in_specs=[block] * 3 + [whole((width, width)), whole((width,))],
        out_specs=[block, block, block, whole((2, width))],
        out_shape=[
            jax.ShapeDtypeStruct((rows, width), F32),
            jax.ShapeDtypeStruct((rows, width), BF16),
            jax.ShapeDtypeStruct((rows, width), BF16),
            jax.ShapeDtypeStruct((2, width), F32),
        ],
        cost_estimate=cost(2 * rows * width * width, 18 * rows * width),
        name="middle",
    )(resid, gradient, grads, w_out, gain)


def weight_kernel(place, back, normed, attended, branch, mine, theirs):
    step = pl.program_id(0)
    core = place[0]

    def write(left, right):
        product = dot(left[...], right[...], ((0,), (0,))).astype(BF16)
        share = product.shape[0] // 4
        for half in range(2):
            for target, owner, here in ((mine, core, place[1]), (theirs, 1 - core, place[2])):
                high, low = step >> 1, step & 1
                even, odd = 4 * high + 2 * half + low, 4 * half + 2 * high + low
                at = ((1 - owner) * even + owner * odd) ^ here
                first = product[2 * half * share : (2 * half + 1) * share]
                second = product[(2 * half + 1) * share : (2 * half + 2) * share]
                target[at, :, :] = jnp.where(owner == 0, first, second)

    pl.when(step < 3)(lambda: write(back, normed))
    pl.when(step >= 3)(lambda: write(attended, branch))


def weight_grad(place, back, normed, attended, branch):
    _, rows, width = back.shape
    share = width // 4
    return pl.pallas_call(
        weight_kernel,
        grid_spec=pltpu.PrefetchScalarGridSpec(
            num_scalar_prefetch=1,
            grid=(4,),
            in_specs=[pl.BlockSpec((None, rows, width), lambda t, s: (jnp.minimum(t, 2), 0, 0))]
            + [whole((rows, width))] * 3,
            out_specs=[whole((8, share, width))] * 2,
        ),
        out_shape=[jax.ShapeDtypeStruct((8, share, width), BF16)] * 2,
        cost_estimate=cost(8 * rows * width * width, 20 * rows * width),
        name="weight_grad",
    )(place, back, normed, attended, branch)


def spread_kernel(place, *refs):
    pieces, (down, into) = refs[:4], refs[-2:]
    step = pl.program_id(0)
    rows = pieces[0].shape[2]
    odd = place[1 + step // 4] & 1
    parts = 2
    size = rows // parts
    for number, piece in enumerate(pieces):

        @pl.when(step // 2 == number)
        def _():
            def move(number, _):
                index, part = number // parts, number % parts
                source = pl.ds(pl.multiple_of(part * size, size), size)
                target = pl.ds(pl.multiple_of((index ^ odd) * rows + part * size, size), size)
                down[target, :] = piece[index, 0, source, :].astype(F32)
                into[target, :] = piece[index, 1, source, :].astype(F32)
                return 0

            lax.fori_loop(0, 2 * parts, move, 0)


def spread(place, square, units, pieces, so_far):
    _, _, rows, width = pieces[0].shape

    def taken(number):
        return pl.BlockSpec(
            (2, 2, rows, width), lambda t, s: (jnp.clip(t - 2 * number, 0, 1), 0, 0, 0)
        )

    def pair(t, s):
        return (t & 3) ^ (jnp.where(t < 4, s[1], s[2]) >> 1)

    def column(t, s):
        return 2 * square + (s[0] ^ (t >> 2))

    return pl.pallas_call(
        spread_kernel,
        grid_spec=pltpu.PrefetchScalarGridSpec(
            num_scalar_prefetch=1,
            grid=(8,),
            in_specs=[taken(number) for number in range(4)]
            + [pl.BlockSpec(memory_space=pl.ANY)] * len(so_far),
            out_specs=[
                pl.BlockSpec((2 * rows, width), lambda t, s: (4 * column(t, s) + pair(t, s), 0)),
                pl.BlockSpec((2 * rows, width), lambda t, s: (pair(t, s), column(t, s))),
            ],
        ),
        out_shape=[
            jax.ShapeDtypeStruct((units, width), F32),
            jax.ShapeDtypeStruct((width, units), F32),
        ],
        input_output_aliases={5: 0, 6: 1} if so_far else {},
        cost_estimate=cost(0, 24 * width * width),
        name="spread",
    )(place, *pieces, *so_far)


def last_kernel(place, back, weights, tokens, grad_resid, gain, theirs, mine, norm_grads):
    step = pl.program_id(0)
    gradient = dot(back[0], weights[0], ((1,), (1,)))
    gradient += dot(back[1], weights[1], ((1,), (1,)))
    gradient += dot(back[2], weights[2], ((1,), (1,)))
    _, scaled, rstd = normalize(tokens[...].astype(F32), 1.0, 0.0)
    inner, gain_part, bias_part = normalize_back(gradient, scaled, rstd, row_of(gain))
    sums = jnp.concatenate([gain_part[None], bias_part[None]], axis=0)
    result = grad_resid[...] + inner
    half = pl.num_programs(0) // 2

    @pl.when(step < half)
    def _():
        theirs[...] = result.astype(BF16)

    @pl.when(step >= half)
    def _():
        mine[...] = result

    before = jnp.where(step == 0, 0.0, norm_grads[...])
    norm_grads[...] = jnp.where(step == 0, sums, before + sums)


def last(place, back, weights, tokens, grad_resid, gain):
    rows, width = tokens.shape
    steps = rows // BLOCK
    half = steps // 2

    def turn(j, s):
        return (j + half * (1 - s[0])) % steps

    block = pl.BlockSpec((BLOCK, width), lambda j, s: (turn(j, s), 0))
    return pl.pallas_call(
        last_kernel,
        grid_spec=pltpu.PrefetchScalarGridSpec(
            num_scalar_prefetch=1,
            grid=(steps,),
            in_specs=[
                pl.BlockSpec((3, BLOCK, width), lambda j, s: (0, turn(j, s), 0)),
                whole((3, width, width)),
                block,
                block,
                whole((width,)),
            ],
            out_specs=[
                pl.BlockSpec((BLOCK, width), lambda j, s: (jnp.minimum(j, half - 1), 0)),
                pl.BlockSpec((BLOCK, width), lambda j, s: (jnp.maximum(j - half, 0), 0)),
                whole((2, width)),
            ],
        ),
        out_shape=[
            jax.ShapeDtypeStruct((rows // 2, width), BF16),
            jax.ShapeDtypeStruct((rows // 2, width), F32),
            jax.ShapeDtypeStruct((2, width), F32),
        ],
        cost_estimate=cost(6 * rows * width * width, 16 * rows * width + 6 * width * width),
        name="last",
    )(place, back, weights, tokens, grad_resid, gain)


def bit_of(axis, bit):
    return (lax.axis_index(axis) >> bit) & 1


def swap(values, axis, bit):
    count = lax.axis_size(axis)
    return lax.ppermute(values, axis, [(i, i ^ (1 << bit)) for i in range(count)])


class Stage:
    def __init__(self, dp_bits, even, odd):
        flips = [1 << (bit + 2 if axis == "dp" else bit) for axis, bit in (even, odd)]
        self.pairs = [(index, index ^ flips[index & 1]) for index in range(4 << dp_bits)]

    def send(self, values):
        return lax.ppermute(values, ("dp", "mp"), self.pairs)


class Sum:
    def __init__(self, terms, halving, adding, doubling):
        self.terms = terms
        self.count = terms[0].shape[0]
        self.halving, self.adding, self.doubling = list(halving), list(adding), list(doubling)
        self.pieces = None
        self.prepare()

    def total(self, low, high):
        result = None
        for term in self.terms:
            term = term[low:high].astype(F32)
            result = term if result is None else result + term
        return result.astype(BF16)

    def land(self, values):
        self.received = self.pieces[1] = values

    def prepare(self):
        if self.halving:
            self.outgoing = self.total(self.count // 2, self.count)
        elif self.terms:
            self.outgoing = self.total(0, self.count)

    def start(self):
        stage = (self.halving or self.adding or self.doubling)[0]
        self.received = stage.send(self.outgoing)

    def finish(self):
        if self.halving:
            self.halving.pop(0)
            self.count //= 2
            self.terms.append(self.received)
            self.prepare()
        elif self.adding:
            self.adding.pop(0)
            self.terms = [self.outgoing, self.received]
            self.prepare()
            if self.adding:
                self.start()
                self.finish()
        else:
            self.doubling.pop(0)
            self.terms = []
            self.pieces = [self.outgoing, self.received]
            if self.doubling:
                self.outgoing = jnp.concatenate(self.pieces, axis=0)


class Whole:
    def __init__(self, values, stages):
        self.outgoing, self.stages = values, list(stages)

    def start(self):
        self.received = self.stages.pop(0).send(self.outgoing)

    def finish(self):
        self.outgoing = self.outgoing + self.received


class Once:
    def __init__(self, values, stage):
        self.outgoing, self.stage = values, stage

    def start(self):
        self.received = self.stage.send(self.outgoing)

    def finish(self):
        pass

    def land(self, values):
        self.received = values


def local(
    dp_bits,
    tokens,
    segment_ids,
    norm1_gain,
    norm1_bias,
    w_qkv,
    conv_weight,
    w_out,
    norm2_gain,
    norm2_bias,
    w_in,
    w_down,
    cotangent,
):
    width = tokens.shape[2]
    core = bit_of("mp", 0)
    group = lax.axis_index("mp")
    rows = tokens.shape[1]

    def own_tokens(mine, theirs):
        at = lax.broadcasted_iota(jnp.int32, (2, 1, 1), 0)
        return jnp.where(at == core, mine[None], theirs.astype(mine.dtype)[None])

    dp = [("dp", bit) for bit in range(dp_bits)]
    y, cores = ("mp", 1), ("mp", 0)
    swap_cores = Stage(dp_bits, cores, cores)
    first, second = Stage(dp_bits, dp[0], y), Stage(dp_bits, y, dp[0])
    third = Stage(dp_bits, dp[1], dp[1])
    across = Stage(dp_bits, dp[0], dp[0])
    adding = [Stage(dp_bits, axis, axis) for axis in dp[2:]]
    x_bit, y_bit, z_bit = bit_of(*dp[0]), bit_of(*y), bit_of(*dp[1])
    here_even, here_odd = 4 * x_bit + 2 * y_bit + z_bit, 4 * y_bit + 2 * x_bit + z_bit
    here = jnp.where(core == 0, here_even, here_odd)
    here_theirs = jnp.where(core == 0, here_odd, here_even)
    place = jnp.stack([core, here, here_theirs, y_bit])

    their_tokens = swap(tokens, "mp", 0)
    taps_local, their_tokens = lax.optimization_barrier(
        (conv_weight.reshape(9, conv_weight.shape[2]), their_tokens)
    )
    their_cotangent = swap(cotangent, "mp", 0)
    pieces = [taps_local]
    for offset in range(1, 4):
        pieces.append(lax.ppermute(taps_local, "mp", [(i, i ^ offset) for i in range(4)]))
    stacked = jnp.stack(pieces, axis=0)
    taps = jnp.concatenate(
        [lax.dynamic_index_in_dim(stacked, group ^ i, 0, keepdims=False) for i in range(4)], axis=1
    )

    weights = w_qkv.transpose(1, 0, 2)
    so_far = front(place, tokens, norm1_gain, norm1_bias, weights, ())
    projected, normed_one, token_rows = front(
        place, their_tokens, norm1_gain, norm1_bias, weights, so_far
    )
    mixed, attended, lse, *masks = attend(place, projected, taps, segment_ids)
    masks = (taps, *masks)

    def feed_square(number, other, ahead):
        final = number == squares - 1 and not other
        return feed(number, other, final, place, ahead, w_in, w_down)

    squares = w_in.shape[1] // width // 2
    names = "abcdefgh"[:squares]
    found, units = {}, {}
    resid, normed_two, grad_output, other, *ahead = feed_square(
        0, True, (norm2_gain, norm2_bias, token_rows, attended, w_out, cotangent, their_cotangent)
    )
    units["core" + names[0]] = Once(other, swap_cores)

    def chunk_own(number):
        name = names[number]

        def run(ahead):
            own, *ahead = feed_square(number, False, (normed_two, *ahead, grad_output))
            units[name] = Sum(
                [own, units["core" + name].received], [first, second, third], adding, [third, second, first]
            )
            if number == squares - 1:
                theirs, found["output"], *ahead = ahead
                units["out"] = Once(theirs, swap_cores)
            return ahead

        return run

    def chunk_other(number):
        def run(ahead):
            other, *ahead = feed_square(number, True, (normed_two, *ahead, grad_output))
            units["core" + names[number]] = Once(other, swap_cores)
            return ahead

        return run

    def chunk_middle(ahead):
        back_sum = ahead[-1]
        grad_resid, branch, grad_attended, norm_two = middle(
            resid, back_sum, grad_output, w_out, norm2_gain
        )
        found.update(grad_resid=grad_resid, branch=branch, norm_two=norm_two, back=())
        return grad_attended

    def chunk_attend(first_pair, pairs):
        def run(held):
            grads = held[0] if isinstance(held, tuple) else held
            found["back"] = attend_back(
                first_pair, pairs, found["back"], mixed, grads, attended, lse, projected, *masks
            )
            found["grads"] = grads
            return (grads, found["back"][0])

        return run

    def chunk_weights(held):
        mine, theirs = weight_grad(place, held[1], normed_one, attended, found["branch"])
        found["mine"] = mine
        units["core"] = Once(theirs, swap_cores)
        return held[1]

    def chunk_last(back):
        theirs, found["input_grad"], found["norm_one"] = last(
            place, back, weights, token_rows, found["grad_resid"], norm1_gain
        )
        units["h"] = Sum(
            [found["mine"], units["core"].received], [first, second, third], adding, [third, across]
        )
        small = jnp.concatenate([found["back"][1], found["norm_one"], found["norm_two"]], axis=0)
        units["small"] = Whole(small, [Stage(dp_bits, axis, axis) for axis in [cores, y] + dp])
        units["in"] = Once(theirs, swap_cores)
        return found["input_grad"]

    def chunk_spread(square, name):
        def run(held):
            pieces = list(units[name].pieces) + [units[name + str(i)].received for i in range(2)]
            found["spread"] = spread(
                place, square, w_in.shape[1], pieces, found.get("spread", ())
            )
            return found["spread"]

        return run

    plan = [
        (("corea",), (), chunk_own(0)),
        (("a",), (), chunk_other(1)),
        (("a", "coreb"), (), chunk_own(1)),
        (("a", "b", "out"), (), chunk_middle),
        (("a", "b"), ("out",), chunk_attend(0, width // LANES // 2)),
        (("a", "b"), (), chunk_attend(width // LANES // 2, width // LANES // 2)),
        (("a", "b"), (), chunk_weights),
        (("core", "a", "b"), (), chunk_last),
        (("h", "a0", "in", "small"), ("a",), None),
        (("h", "a1", "small"), ("a0", "in"), None),
        (("h", "b", "small"), ("a1",), chunk_spread(0, "a")),
        (("h", "b", "small"), (), None),
        (("h", "b0", "b1", "small"), ("b",), None),
        (("h",), ("b0", "b1"), chunk_spread(1, "b")),
    ]
    held = ahead
    for sent, arrived, chunk in plan:
        for name in sent:
            if name not in units:
                units[name] = Once(units[name[0]].pieces[int(name[1])], swap_cores)
        active, landed = [units[name] for name in sent], [units[name] for name in arrived]
        outgoing, received, held = lax.optimization_barrier(
            (tuple(unit.outgoing for unit in active), tuple(unit.received for unit in landed), held)
        )
        for unit, values in zip(landed, received):
            unit.land(values)
        for unit, values in zip(active, outgoing):
            unit.outgoing = values
            unit.start()
        if chunk:
            held = chunk(held)
        for unit in active:
            unit.finish()

    small = units["small"]
    while small.stages:
        small.start()
        small.finish()
    share = width // 4
    small = lax.dynamic_slice_in_dim(small.outgoing, group * share, share, 1)
    heads = jnp.concatenate(units["h"].pieces, axis=0)
    heads = [
        lax.dynamic_index_in_dim(heads, index ^ (2 * x_bit + z_bit), 0, keepdims=False).astype(F32)
        for index in range(4)
    ]
    qkv_grad = jnp.stack(heads[:3]).transpose(2, 0, 1)
    out_grad = heads[3]
    down_grad, in_grad = found["spread"]
    return (
        own_tokens(found["output"], units["out"].received),
        own_tokens(found["input_grad"], units["in"].received),
        small[9],
        small[10],
        qkv_grad,
        small[:9].reshape(3, 3, share),
        out_grad,
        small[11],
        small[12],
        in_grad,
        down_grad,
    )


def solution(mesh):
    placed = (
        P(None, ("dp", "mp"), None),
        P(None, "dp"),
        P(),
        P(),
        P(),
        P(None, None, "mp"),
        P(),
        P(),
        P(),
        P(),
        P(),
        P(None, ("dp", "mp"), None),
    )
    dp_bits = mesh.shape["dp"].bit_length() - 1
    return jax.shard_map(
        functools.partial(local, dp_bits),
        mesh=mesh,
        in_specs=placed,
        out_specs=(
            P(None, ("dp", "mp"), None),
            P(None, ("dp", "mp"), None),
            P("mp"),
            P("mp"),
            P(None, None, "mp"),
            P(None, None, "mp"),
            P("mp", None),
            P("mp"),
            P("mp"),
            P(),
            P(),
        ),
        check_vma=False,
    )
```

```python
import functools
import math

import jax
import jax.numpy as jnp
from jax import lax
from jax.experimental import pallas as pl
from jax.experimental.pallas import tpu as pltpu
from jax.sharding import PartitionSpec as P

HEAD_DIM = 64
LEN = 1024
LANES = 128
BLOCK = 256
FEED_ROWS = 256
EPSILON = 1e-05
MASKED = -1e30
F32 = jnp.float32
BF16 = jnp.bfloat16


def dot(a, b, dims):
    return lax.dot_general(a, b, (dims, ((), ())), preferred_element_type=F32)


def normalize(values, norm_gain, norm_bias):
    centred = values - jnp.mean(values, axis=-1, keepdims=True)
    rstd_row = lax.rsqrt(jnp.mean(centred * centred, axis=-1, keepdims=True) + EPSILON)
    scaled = centred * rstd_row
    return (scaled * norm_gain + norm_bias, scaled, rstd_row)


def normalize_back(gradient, scaled, rstd_row, norm_gain):
    grad_scaled = gradient * norm_gain
    inner_term = (
        grad_scaled
        - jnp.mean(grad_scaled, axis=-1, keepdims=True)
        - scaled * jnp.mean(grad_scaled * scaled, axis=-1, keepdims=True)
    )
    return (rstd_row * inner_term, jnp.sum(gradient * scaled, axis=0), jnp.sum(gradient, axis=0))


def attend_kernel(
    place, proj_q, proj_k, proj_v, taps, segments, mixed_out, attended, lse, same, seg_col, seg_row, bias
):
    q_out, k_out, v_out = mixed_out.at[0], mixed_out.at[1], mixed_out.at[2]

    @pl.when(pl.program_id(0) == 0)
    def _():
        numbers = jnp.where(place[0] == 0, segments[0:1, :], segments[1:2, :])
        seg_row[...] = jnp.broadcast_to(numbers, seg_row.shape)
        column = jnp.broadcast_to(numbers.astype(F32), (LANES, LEN)).T
        seg_col[...] = column.astype(jnp.int32)
        at = lax.broadcasted_iota(jnp.int32, (LEN, LANES), 0)
        for shift in (1, 2):
            equal = (at >= shift) & (pltpu.roll(column, shift, 0) == column)
            same[shift - 1] = jnp.where(equal, 1.0, 0.0)
        for first in range(0, LEN, BLOCK):
            width = first + BLOCK
            rows = first + lax.broadcasted_iota(jnp.int32, (BLOCK, width), 0)
            cols = lax.broadcasted_iota(jnp.int32, (BLOCK, width), 1)
            mine = jnp.concatenate([seg_col[first:width, :]] * (width // LANES), axis=1)
            allowed = (cols <= rows) & (mine == seg_row[0:1, :width])
            bias[first:width, :width] = jnp.where(allowed, 0.0, MASKED)

    same_one, same_two = same[0], same[1]
    for which, (source, target) in enumerate(((proj_q, q_out), (proj_k, k_out), (proj_v, v_out))):
        values = source[...].astype(F32)
        mixed = (
            values * taps[3 * which : 3 * which + 1, :]
            + pltpu.roll(values, 1, 0) * same_one * taps[3 * which + 1 : 3 * which + 2, :]
            + pltpu.roll(values, 2, 0) * same_two * taps[3 * which + 2 : 3 * which + 3, :]
        )
        target[...] = mixed.astype(BF16)
    scaling = 1.0 / math.sqrt(HEAD_DIM)
    lane = lax.broadcasted_iota(jnp.int32, (1, LANES), 1)
    for first in range(0, LEN, BLOCK):
        width = first + BLOCK
        queries = q_out[first:width, :] * jnp.asarray(scaling, BF16)
        parts = []
        for head in range(2):
            chosen = (lane >= HEAD_DIM) if head else (lane < HEAD_DIM)
            mine = jnp.where(chosen, queries, jnp.zeros_like(queries))
            scores = dot(mine, k_out[:width, :], ((1,), (1,))) + bias[first:width, :width]
            top = jnp.max(scores, axis=1, keepdims=True)
            weights = jnp.exp(scores - top)
            total = jnp.sum(weights, axis=1, keepdims=True)
            product = dot(weights.astype(BF16), v_out[:width, :], ((1,), (0,)))
            parts.append((product * (1.0 / total), top + jnp.log(total)))
        left = lane < HEAD_DIM
        attended[first:width, :] = jnp.where(left, parts[0][0], parts[1][0]).astype(BF16)
        logs = jnp.where(left, parts[0][1], parts[1][1])
        flipped = logs.T
        lse[0:1, first:width] = flipped[0:1, :]
        lse[1:2, first:width] = flipped[HEAD_DIM : HEAD_DIM + 1, :]


def attend_back_kernel(
    continued,
    *refs,
):
    attend_back_body(*(refs[2:] if continued else refs))


def attend_back_body(
    mixed_in,
    grads,
    attended,
    lse,
    proj_q,
    proj_k,
    proj_v,
    taps,
    same,
    seg_col,
    seg_row,
    back,
    tap_grads,
    bias,
    grad_k,
    grad_v,
    grad_qt,
    keys_t,
    inner,
):
    q_in, k_in, v_in = mixed_in.at[0], mixed_in.at[1], mixed_in.at[2]
    back_q, back_k, back_v = back.at[0], back.at[1], back.at[2]

    @pl.when(pl.program_id(0) == 0)
    def _():
        for first in range(0, LEN, BLOCK):
            width = first + BLOCK
            rows = lax.broadcasted_iota(jnp.int32, (width, BLOCK), 0)
            cols = first + lax.broadcasted_iota(jnp.int32, (width, BLOCK), 1)
            theirs = jnp.concatenate([seg_col[:width, :]] * (BLOCK // LANES), axis=1)
            allowed = (rows <= cols) & (theirs == seg_row[0:1, first:width])
            bias[:width, first:width] = jnp.where(allowed, 0.0, MASKED)

    scaling = 1.0 / math.sqrt(HEAD_DIM)
    lane = lax.broadcasted_iota(jnp.int32, (1, LANES), 1)
    keys_t[...] = k_in[...].T
    inner[...] = (grads[...].astype(F32) * attended[...].astype(F32)).T
    grad_k[...] = jnp.zeros_like(grad_k)
    grad_v[...] = jnp.zeros_like(grad_v)

    def one_head(head, _):
        low = pl.multiple_of(head * HEAD_DIM, HEAD_DIM)
        mine = pl.ds(low, HEAD_DIM)
        chosen = (lane >= low) & (lane < low + HEAD_DIM)
        inner_row = jnp.sum(inner[mine, :], axis=0, keepdims=True)
        for first in range(0, LEN, BLOCK):
            width = first + BLOCK
            queries = q_in[first:width, :] * jnp.asarray(scaling, BF16)
            queries = jnp.where(chosen, queries, jnp.zeros_like(queries))
            outer = grads[first:width, :]
            outer = jnp.where(chosen, outer, jnp.zeros_like(outer))
            scores = dot(k_in[:width, :], queries, ((1,), (1,))) + bias[:width, first:width]
            probs = jnp.exp(scores - lse[pl.ds(head, 1), first:width])
            grad_probs = dot(v_in[:width, :], outer, ((1,), (1,)))
            grad_scores = (probs * (grad_probs - inner_row[:, first:width])).astype(BF16)
            grad_v[:width, :] += dot(probs.astype(BF16), outer, ((1,), (0,)))
            grad_k[:width, :] += dot(grad_scores, queries, ((1,), (0,)))
            grad_qt[mine, first:width] = dot(keys_t[mine, :width], grad_scores, ((1,), (0,)))
        return 0

    lax.fori_loop(0, 2, one_head, 0)
    same_one, same_two = same[0], same[1]
    grad_q = grad_qt[...].T * scaling
    for which, (gradient, source, target) in enumerate(
        ((grad_q, proj_q, back_q), (grad_k[...], proj_k, back_k), (grad_v[...], proj_v, back_v))
    ):
        values = source[...].astype(F32)
        row = 3 * which
        after_one = pltpu.roll(gradient * same_one, LEN - 1, 0)
        after_two = pltpu.roll(gradient * same_two, LEN - 2, 0)
        tap_grads[row : row + 1, :] = jnp.sum(gradient * values, axis=0, keepdims=True)
        tap_grads[row + 1 : row + 2, :] = jnp.sum(after_one * values, axis=0, keepdims=True)
        tap_grads[row + 2 : row + 3, :] = jnp.sum(after_two * values, axis=0, keepdims=True)
        target[...] = (
            gradient * taps[row : row + 1, :]
            + after_one * taps[row + 1 : row + 2, :]
            + after_two * taps[row + 2 : row + 3, :]
        ).astype(BF16)


def whole(shape):
    return pl.BlockSpec(shape, lambda *_: (0,) * len(shape))


def cost(flops, moved, exps=0):
    return pl.CostEstimate(flops=int(flops), transcendentals=int(exps), bytes_accessed=int(moved))


def attend(place, projected, taps, segments):
    width = projected.shape[1] // 3
    pairs = width // LANES

    def column(offset):
        return pl.BlockSpec((LEN, LANES), lambda h, s, offset=offset: (0, offset + h))

    return pl.pallas_call(
        attend_kernel,
        grid_spec=pltpu.PrefetchScalarGridSpec(
            num_scalar_prefetch=1,
            grid=(pairs,),
            in_specs=[
                column(0),
                column(pairs),
                column(2 * pairs),
                pl.BlockSpec((9, LANES), lambda h, s: (0, h)),
                pl.BlockSpec((2, LEN), lambda h, s: (0, s[3])),
            ],
            out_specs=[
                pl.BlockSpec((3, LEN, LANES), lambda h, s: (0, 0, h)),
                column(0),
                pl.BlockSpec((None, 2, LEN), lambda h, s: (h, 0, 0)),
                whole((2, LEN, LANES)),
                whole((LEN, LANES)),
                whole((8, LEN)),
            ],
            scratch_shapes=[pltpu.VMEM((LEN, LEN), F32)],
        ),
        out_shape=[
            jax.ShapeDtypeStruct((3, LEN, width), BF16),
            jax.ShapeDtypeStruct((LEN, width), BF16),
            jax.ShapeDtypeStruct((pairs, 2, LEN), F32),
            jax.ShapeDtypeStruct((2, LEN, LANES), F32),
            jax.ShapeDtypeStruct((LEN, LANES), jnp.int32),
            jax.ShapeDtypeStruct((8, LEN), jnp.int32),
        ],
        cost_estimate=cost(4 * LEN * LEN * width, 16 * LEN * width, LEN * LEN * pairs),
        name="attend",
    )(place, projected, projected, projected, taps, segments)


def attend_back(first_pair, pairs, so_far, mixed, grads, attended, lse, projected, taps, same, seg_col, seg_row):
    width = grads.shape[1]
    all_pairs = width // LANES

    def column(offset):
        return pl.BlockSpec((LEN, LANES), lambda h, offset=offset: (0, first_pair + offset + h))

    stack = pl.BlockSpec((3, LEN, LANES), lambda h: (0, 0, first_pair + h))
    rows = pl.BlockSpec((9, LANES), lambda h: (0, first_pair + h))
    there = [pl.BlockSpec(memory_space=pl.ANY)] * 2 if so_far else []
    taken = pairs * LANES
    return pl.pallas_call(
        functools.partial(attend_back_kernel, bool(so_far)),
        grid=(pairs,),
        in_specs=there
        + [
            stack,
            column(0),
            column(0),
            pl.BlockSpec((None, 2, LEN), lambda h: (first_pair + h, 0, 0)),
            column(0),
            column(all_pairs),
            column(2 * all_pairs),
            rows,
            whole((2, LEN, LANES)),
            whole((LEN, LANES)),
            whole((8, LEN)),
        ],
        out_specs=[stack, rows],
        out_shape=[
            jax.ShapeDtypeStruct((3, LEN, width), BF16),
            jax.ShapeDtypeStruct((9, width), F32),
        ],
        scratch_shapes=[
            pltpu.VMEM((LEN, LEN), F32),
            pltpu.VMEM((LEN, LANES), F32),
            pltpu.VMEM((LEN, LANES), F32),
            pltpu.VMEM((LANES, LEN), F32),
            pltpu.VMEM((LANES, LEN), BF16),
            pltpu.VMEM((LANES, LEN), F32),
        ],
        input_output_aliases={0: 0, 1: 1} if so_far else {},
        cost_estimate=cost(10 * LEN * LEN * taken, 22 * LEN * taken, LEN * LEN * pairs),
        name="attend_back",
    )(*so_far, mixed, grads, attended, lse, projected, projected, projected, taps, same, seg_col, seg_row)


def front_kernel(continued, place, *refs):
    tokens, gain, offset, weights, projected, normed, rows_out = refs[3:] if continued else refs

    @pl.when(pl.program_id(0) == 0)
    def _():
        rows_out[...] = tokens[...]
        value, _, _ = normalize(tokens[...].astype(F32), row_of(gain), row_of(offset))
        normed[...] = value.astype(BF16)

    projected[...] = dot(normed[...], weights[...], ((1,), (0,))).astype(BF16)


def row_of(vector):
    return vector[...].reshape(1, vector.shape[0])


def front(place, tokens, gain, offset, weights, so_far):
    _, half, width = tokens.shape
    other = int(bool(so_far))
    mine = pl.BlockSpec((half, width), lambda j, s: (s[0] ^ other, 0))
    return pl.pallas_call(
        functools.partial(front_kernel, bool(so_far)),
        grid_spec=pltpu.PrefetchScalarGridSpec(
            num_scalar_prefetch=1,
            grid=(3,),
            in_specs=[pl.BlockSpec(memory_space=pl.ANY)] * len(so_far)
            + [
                pl.BlockSpec((None, half, width), lambda j, s: (s[0], 0, 0)),
                whole((width,)),
                whole((width,)),
                pl.BlockSpec((None, width, width), lambda j, s: (j, 0, 0)),
            ],
            out_specs=[pl.BlockSpec((half, width), lambda j, s: (s[0] ^ other, j)), mine, mine],
        ),
        out_shape=[
            jax.ShapeDtypeStruct((2 * half, 3 * width), BF16),
            jax.ShapeDtypeStruct((2 * half, width), BF16),
            jax.ShapeDtypeStruct((2 * half, width), BF16),
        ],
        input_output_aliases={1: 0, 2: 1, 3: 2} if so_far else {},
        cost_estimate=cost(6 * half * width * width, 14 * half * width + 6 * width * width),
        name="front",
    )(place, *so_far, tokens, gain, offset, weights)


def feed_kernel(number, other, first, last, place, *refs):
    core, here = place[0], place[1 + other]
    square = 2 * number + (core ^ other)
    if first:
        gain, offset, tokens, attended, w_out, mine, theirs, w_in, w_down = refs[:9]
        resid_out, normed_out, grads_out, parts_out, out, back_out = refs[9:15]
        tokens_held, attended_held, weights_held = refs[-3:]
        scratch = refs[15:-3]
    else:
        normed_in, out_in, back_in, grads_in, w_in, w_down = refs[:6]
        if last:
            parts_out, out_theirs, out_mine, back_out = refs[6:10]
            result_low = refs[-1]
            scratch = refs[10:-1]
        else:
            parts_out, out, back_out = refs[6:9]
            scratch = refs[9:]
    lefts, rights, in_block, down_block, total, back, parts, sems, row_sems = scratch
    hidden, normed, grads, grad_pre = lefts.at[0], lefts.at[1], rights.at[0], rights.at[1]
    count = normed.shape[0]
    width = in_block.shape[1]
    half = normed.shape[0] // 2
    columns = pl.ds(pl.multiple_of(square * width, width), width)
    my_rows = pl.ds(pl.multiple_of(core * half, half), half)
    their_rows = pl.ds(pl.multiple_of((1 - core) * half, half), half)
    flights = []

    def copy(source, target):
        flight = pltpu.make_async_copy(source, target, sems.at[len(flights)])
        flights.append(flight)
        flight.start()
        return flight

    if first:
        early = [copy(attended, attended_held), copy(w_out, weights_held), copy(tokens, tokens_held)]
        for flight in early:
            flight.wait()
        later = [
            copy(w_in.at[:, columns], in_block),
            copy(mine.at[core], grads.at[my_rows, :]),
            copy(theirs.at[core], grads.at[their_rows, :]),
            copy(w_down.at[columns, :], down_block),
        ]
    else:
        later = [
            copy(normed_in, normed),
            copy(w_in.at[:, columns], in_block),
            copy(grads_in, grads),
            copy(w_down.at[columns, :], down_block),
        ]
    writes = []
    if first:

        def begin(step, _):
            at = pl.ds(pl.multiple_of(step * BLOCK, BLOCK), BLOCK)
            product = dot(attended_held[at, :], weights_held[...], ((1,), (0,)))
            value = tokens_held[at, :].astype(F32) + product
            total[at, :] = value
            value, _, _ = normalize(value, row_of(gain), row_of(offset))
            normed[at, :] = value.astype(BF16)
            return 0

        lax.fori_loop(0, count // BLOCK, begin, 0)
        resid_flight = copy(total, resid_out)
        writes.append(copy(normed, normed_out))
    for flight in later:
        flight.wait()
    if not first:
        total_in = copy(out_in, total)
        back_so_far = copy(back_in, back)
    if first:
        writes.append(copy(grads, grads_out))
    size = FEED_ROWS

    def inner(step, _):
        at = pl.ds(pl.multiple_of(step * size, size), size)
        active = jnp.maximum(dot(normed[at, :], in_block[...], ((1,), (0,))), 0.0)
        hidden[at, :] = (active * active).astype(BF16)
        grad_hidden = dot(grads[at, :], down_block[...], ((1,), (1,)))
        grad_pre[at, :] = (grad_hidden * 2.0 * active).astype(BF16)
        return 0

    lax.fori_loop(0, count // size, inner, 0)
    blocks, _, rows, _ = parts.shape
    taken = width // 2

    def weigh(step, _):
        which, half_at = step // 2, step % 2
        at = pl.ds(pl.multiple_of(half_at * taken, taken), taken)
        product = dot(lefts[which, :, at], rights[which], ((0,), (0,))).astype(BF16)
        for index in range(blocks // 2):
            target = (half_at * (blocks // 2) + index) ^ here
            parts[target, which, :, :] = product[index * rows : (index + 1) * rows, :]
        return 0

    lax.fori_loop(0, 4, weigh, 0)
    writes.append(copy(parts, parts_out))
    if first:
        resid_flight.wait()
    else:
        total_in.wait()
        back_so_far.wait()

    def row_copies(step):
        at = pl.ds(pl.multiple_of(step * size, size), size)
        flights = [pltpu.make_async_copy(back.at[at, :], back_out.at[at, :], row_sems.at[0, step])]
        if not last:
            flights.append(pltpu.make_async_copy(total.at[at, :], out.at[at, :], row_sems.at[1, step]))
        return flights

    def outer(step, _):
        at = pl.ds(pl.multiple_of(step * size, size), size)
        value = total[at, :] + dot(hidden[at, :], down_block[...], ((1,), (0,)))
        if last:
            result_low[at, :] = value.astype(BF16)
        else:
            total[at, :] = value
        product = dot(grad_pre[at, :], in_block[...], ((1,), (1,)))
        back[at, :] = product if first else back[at, :] + product
        for flight in row_copies(step):
            flight.start()
        return 0

    lax.fori_loop(0, count // size, outer, 0)
    if last:
        writes.append(copy(result_low.at[their_rows, :], out_theirs))
        writes.append(copy(result_low.at[my_rows, :], out_mine))
    for step in range(count // size):
        for flight in row_copies(step):
            flight.wait()
    for flight in writes:
        flight.wait()


def feed(number, other, last, place, ahead, w_in, w_down):
    first = len(ahead) == 7
    rows, width = ahead[2].shape
    sums = jax.ShapeDtypeStruct((rows, width), F32)
    low = jax.ShapeDtypeStruct((rows, width), BF16)
    half = jax.ShapeDtypeStruct((rows // 2, width), BF16)
    out_shape = [jax.ShapeDtypeStruct((8, 2, width // 8, width), BF16)]
    if first:
        out_shape = [sums, low, low] + out_shape
    out_shape += [half, half, sums] if last else [sums, sums]
    anywhere = pl.BlockSpec(memory_space=pl.ANY)
    in_specs = [anywhere] * (len(ahead) + 2)
    if first:
        in_specs[:2] = [whole((width,))] * 2
    held = [
        pltpu.VMEM((2, rows, width), BF16),
        pltpu.VMEM((2, rows, width), BF16),
        pltpu.VMEM((width, width), BF16),
        pltpu.VMEM((width, width), BF16),
        pltpu.VMEM((rows, width), F32),
        pltpu.VMEM((rows, width), F32),
        pltpu.VMEM((8, 2, width // 8, width), BF16),
        pltpu.SemaphoreType.DMA((16,)),
        pltpu.SemaphoreType.DMA((2, rows // FEED_ROWS)),
    ]
    if first:
        held += [
            pltpu.VMEM((rows, width), BF16),
            pltpu.VMEM((rows, width), BF16),
            pltpu.VMEM((width, width), BF16),
        ]
    if last:
        held.append(pltpu.VMEM((rows, width), BF16))
    return pl.pallas_call(
        functools.partial(feed_kernel, number, int(other), first, last),
        grid_spec=pltpu.PrefetchScalarGridSpec(
            num_scalar_prefetch=1,
            grid=(1,),
            in_specs=in_specs,
            out_specs=[anywhere] * len(out_shape),
            scratch_shapes=held,
        ),
        out_shape=out_shape,
        cost_estimate=cost(12 * rows * width * width, 16 * rows * width + 8 * width * width),
        name="feed",
    )(place, *ahead, w_in, w_down)


def middle_kernel(
    resid, gradient, grads, w_out, gain, grad_resid, branch_out, grad_attended, norm_grads
):
    _, scaled, rstd = normalize(resid[...], 1.0, 0.0)
    inner, gain_part, bias_part = normalize_back(gradient[...], scaled, rstd, row_of(gain))
    sums = jnp.concatenate([gain_part[None], bias_part[None]], axis=0)
    whole_grad = grads[...].astype(F32) + inner
    grad_resid[...] = whole_grad
    branch = whole_grad.astype(BF16)
    branch_out[...] = branch
    grad_attended[...] = dot(branch, w_out[...], ((1,), (1,))).astype(BF16)
    before = jnp.where(pl.program_id(0) == 0, 0.0, norm_grads[...])
    norm_grads[...] = jnp.where(pl.program_id(0) == 0, sums, before + sums)


def middle(resid, gradient, grads, w_out, gain):
    rows, width = resid.shape
    block = pl.BlockSpec((BLOCK, width), lambda j: (j, 0))
    return pl.pallas_call(
        middle_kernel,
        grid=(rows // BLOCK,),
        in_specs=[block] * 3 + [whole((width, width)), whole((width,))],
        out_specs=[block, block, block, whole((2, width))],
        out_shape=[
            jax.ShapeDtypeStruct((rows, width), F32),
            jax.ShapeDtypeStruct((rows, width), BF16),
            jax.ShapeDtypeStruct((rows, width), BF16),
            jax.ShapeDtypeStruct((2, width), F32),
        ],
        cost_estimate=cost(2 * rows * width * width, 18 * rows * width),
        name="middle",
    )(resid, gradient, grads, w_out, gain)


def weight_kernel(place, back, normed, attended, branch, mine, theirs):
    step = pl.program_id(0)
    core = place[0]

    def write(left, right):
        product = dot(left[...], right[...], ((0,), (0,))).astype(BF16)
        share = product.shape[0] // 4
        for half in range(2):
            for target, owner, here in ((mine, core, place[1]), (theirs, 1 - core, place[2])):
                high, low = step >> 1, step & 1
                even, odd = 4 * high + 2 * half + low, 4 * half + 2 * high + low
                at = ((1 - owner) * even + owner * odd) ^ here
                first = product[2 * half * share : (2 * half + 1) * share]
                second = product[(2 * half + 1) * share : (2 * half + 2) * share]
                target[at, :, :] = jnp.where(owner == 0, first, second)

    pl.when(step < 3)(lambda: write(back, normed))
    pl.when(step >= 3)(lambda: write(attended, branch))


def weight_grad(place, back, normed, attended, branch):
    _, rows, width = back.shape
    share = width // 4
    return pl.pallas_call(
        weight_kernel,
        grid_spec=pltpu.PrefetchScalarGridSpec(
            num_scalar_prefetch=1,
            grid=(4,),
            in_specs=[pl.BlockSpec((None, rows, width), lambda t, s: (jnp.minimum(t, 2), 0, 0))]
            + [whole((rows, width))] * 3,
            out_specs=[whole((8, share, width))] * 2,
        ),
        out_shape=[jax.ShapeDtypeStruct((8, share, width), BF16)] * 2,
        cost_estimate=cost(8 * rows * width * width, 20 * rows * width),
        name="weight_grad",
    )(place, back, normed, attended, branch)


def spread_kernel(place, *refs):
    pieces, (down, into) = refs[:4], refs[-2:]
    step = pl.program_id(0)
    rows = pieces[0].shape[2]
    odd = place[1 + step // 4] & 1
    parts = 2
    size = rows // parts
    for number, piece in enumerate(pieces):

        @pl.when(step // 2 == number)
        def _():
            def move(number, _):
                index, part = number // parts, number % parts
                source = pl.ds(pl.multiple_of(part * size, size), size)
                target = pl.ds(pl.multiple_of((index ^ odd) * rows + part * size, size), size)
                down[target, :] = piece[index, 0, source, :].astype(F32)
                into[target, :] = piece[index, 1, source, :].astype(F32)
                return 0

            lax.fori_loop(0, 2 * parts, move, 0)


def spread(place, square, units, pieces, so_far):
    _, _, rows, width = pieces[0].shape

    def taken(number):
        return pl.BlockSpec(
            (2, 2, rows, width), lambda t, s: (jnp.clip(t - 2 * number, 0, 1), 0, 0, 0)
        )

    def pair(t, s):
        return (t & 3) ^ (jnp.where(t < 4, s[1], s[2]) >> 1)

    def column(t, s):
        return 2 * square + (s[0] ^ (t >> 2))

    return pl.pallas_call(
        spread_kernel,
        grid_spec=pltpu.PrefetchScalarGridSpec(
            num_scalar_prefetch=1,
            grid=(8,),
            in_specs=[taken(number) for number in range(4)]
            + [pl.BlockSpec(memory_space=pl.ANY)] * len(so_far),
            out_specs=[
                pl.BlockSpec((2 * rows, width), lambda t, s: (4 * column(t, s) + pair(t, s), 0)),
                pl.BlockSpec((2 * rows, width), lambda t, s: (pair(t, s), column(t, s))),
            ],
        ),
        out_shape=[
            jax.ShapeDtypeStruct((units, width), F32),
            jax.ShapeDtypeStruct((width, units), F32),
        ],
        input_output_aliases={5: 0, 6: 1} if so_far else {},
        cost_estimate=cost(0, 24 * width * width),
        name="spread",
    )(place, *pieces, *so_far)


def last_kernel(place, back, weights, tokens, grad_resid, gain, theirs, mine, norm_grads):
    step = pl.program_id(0)
    gradient = dot(back[0], weights[0], ((1,), (1,)))
    gradient += dot(back[1], weights[1], ((1,), (1,)))
    gradient += dot(back[2], weights[2], ((1,), (1,)))
    _, scaled, rstd = normalize(tokens[...].astype(F32), 1.0, 0.0)
    inner, gain_part, bias_part = normalize_back(gradient, scaled, rstd, row_of(gain))
    sums = jnp.concatenate([gain_part[None], bias_part[None]], axis=0)
    result = grad_resid[...] + inner
    half = pl.num_programs(0) // 2

    @pl.when(step < half)
    def _():
        theirs[...] = result.astype(BF16)

    @pl.when(step >= half)
    def _():
        mine[...] = result

    before = jnp.where(step == 0, 0.0, norm_grads[...])
    norm_grads[...] = jnp.where(step == 0, sums, before + sums)


def last(place, back, weights, tokens, grad_resid, gain):
    rows, width = tokens.shape
    steps = rows // BLOCK
    half = steps // 2

    def turn(j, s):
        return (j + half * (1 - s[0])) % steps

    block = pl.BlockSpec((BLOCK, width), lambda j, s: (turn(j, s), 0))
    return pl.pallas_call(
        last_kernel,
        grid_spec=pltpu.PrefetchScalarGridSpec(
            num_scalar_prefetch=1,
            grid=(steps,),
            in_specs=[
                pl.BlockSpec((3, BLOCK, width), lambda j, s: (0, turn(j, s), 0)),
                whole((3, width, width)),
                block,
                block,
                whole((width,)),
            ],
            out_specs=[
                pl.BlockSpec((BLOCK, width), lambda j, s: (jnp.minimum(j, half - 1), 0)),
                pl.BlockSpec((BLOCK, width), lambda j, s: (jnp.maximum(j - half, 0), 0)),
                whole((2, width)),
            ],
        ),
        out_shape=[
            jax.ShapeDtypeStruct((rows // 2, width), BF16),
            jax.ShapeDtypeStruct((rows // 2, width), F32),
            jax.ShapeDtypeStruct((2, width), F32),
        ],
        cost_estimate=cost(6 * rows * width * width, 16 * rows * width + 6 * width * width),
        name="last",
    )(place, back, weights, tokens, grad_resid, gain)


def bit_of(axis, bit):
    return (lax.axis_index(axis) >> bit) & 1


def swap(values, axis, bit):
    count = lax.axis_size(axis)
    return lax.ppermute(values, axis, [(i, i ^ (1 << bit)) for i in range(count)])


class Stage:
    def __init__(self, dp_bits, even, odd):
        flips = [1 << (bit + 2 if axis == "dp" else bit) for axis, bit in (even, odd)]
        self.pairs = [(index, index ^ flips[index & 1]) for index in range(4 << dp_bits)]

    def send(self, values):
        return lax.ppermute(values, ("dp", "mp"), self.pairs)


class Sum:
    def __init__(self, terms, halving, adding, doubling):
        self.terms = terms
        self.count = terms[0].shape[0]
        self.halving, self.adding, self.doubling = list(halving), list(adding), list(doubling)
        self.pieces = None
        self.prepare()

    def total(self, low, high):
        if len(self.terms) == 2:
            return self.terms[0][low:high] + self.terms[1][low:high]
        result = None
        for term in self.terms:
            term = term[low:high].astype(F32)
            result = term if result is None else result + term
        return result.astype(BF16)

    def land(self, values):
        self.received = self.pieces[1] = values

    def prepare(self):
        if self.halving:
            self.outgoing = self.total(self.count // 2, self.count)
        elif self.terms:
            self.outgoing = self.total(0, self.count)

    def start(self):
        stage = (self.halving or self.adding or self.doubling)[0]
        self.received = stage.send(self.outgoing)

    def finish(self):
        if self.halving:
            self.halving.pop(0)
            self.count //= 2
            self.terms.append(self.received)
            self.prepare()
        elif self.adding:
            self.adding.pop(0)
            self.terms = [self.outgoing, self.received]
            self.prepare()
            if self.adding:
                self.start()
                self.finish()
        else:
            self.doubling.pop(0)
            self.terms = []
            self.pieces = [self.outgoing, self.received]
            if self.doubling:
                self.outgoing = jnp.concatenate(self.pieces, axis=0)


class Whole:
    def __init__(self, values, stages):
        self.outgoing, self.stages = values, list(stages)

    def start(self):
        self.received = self.stages.pop(0).send(self.outgoing)

    def finish(self):
        self.outgoing = self.outgoing + self.received


class Once:
    def __init__(self, values, stage):
        self.outgoing, self.stage = values, stage

    def start(self):
        self.received = self.stage.send(self.outgoing)

    def finish(self):
        pass

    def land(self, values):
        self.received = values


def local(
    dp_bits,
    tokens,
    segment_ids,
    norm1_gain,
    norm1_bias,
    w_qkv,
    conv_weight,
    w_out,
    norm2_gain,
    norm2_bias,
    w_in,
    w_down,
    cotangent,
):
    width = tokens.shape[2]
    core = bit_of("mp", 0)
    group = lax.axis_index("mp")
    rows = tokens.shape[1]

    def own_tokens(mine, theirs):
        at = lax.broadcasted_iota(jnp.int32, (2, 1, 1), 0)
        return jnp.where(at == core, mine[None], theirs.astype(mine.dtype)[None])

    dp = [("dp", bit) for bit in range(dp_bits)]
    y, cores = ("mp", 1), ("mp", 0)
    swap_cores = Stage(dp_bits, cores, cores)
    first, second = Stage(dp_bits, dp[0], y), Stage(dp_bits, y, dp[0])
    third = Stage(dp_bits, dp[1], dp[1])
    across = Stage(dp_bits, dp[0], dp[0])
    adding = [Stage(dp_bits, axis, axis) for axis in dp[2:]]
    x_bit, y_bit, z_bit = bit_of(*dp[0]), bit_of(*y), bit_of(*dp[1])
    here_even, here_odd = 4 * x_bit + 2 * y_bit + z_bit, 4 * y_bit + 2 * x_bit + z_bit
    here = jnp.where(core == 0, here_even, here_odd)
    here_theirs = jnp.where(core == 0, here_odd, here_even)
    place = jnp.stack([core, here, here_theirs, y_bit])

    their_tokens = swap(tokens, "mp", 0)
    taps_local, their_tokens = lax.optimization_barrier(
        (conv_weight.reshape(9, conv_weight.shape[2]), their_tokens)
    )
    their_cotangent = swap(cotangent, "mp", 0)
    pieces = [taps_local]
    for offset in range(1, 4):
        pieces.append(lax.ppermute(taps_local, "mp", [(i, i ^ offset) for i in range(4)]))
    stacked = jnp.stack(pieces, axis=0)
    taps = jnp.concatenate(
        [lax.dynamic_index_in_dim(stacked, group ^ i, 0, keepdims=False) for i in range(4)], axis=1
    )

    weights = w_qkv.transpose(1, 0, 2)
    so_far = front(place, tokens, norm1_gain, norm1_bias, weights, ())
    projected, normed_one, token_rows = front(
        place, their_tokens, norm1_gain, norm1_bias, weights, so_far
    )
    projected, their_cotangent = lax.optimization_barrier((projected, their_cotangent))
    mixed, attended, lse, *masks = attend(place, projected, taps, segment_ids)
    masks = (taps, *masks)

    def feed_square(number, other, ahead):
        final = number == squares - 1 and not other
        return feed(number, other, final, place, ahead, w_in, w_down)

    squares = w_in.shape[1] // width // 2
    names = "abcdefgh"[:squares]
    found, units = {}, {}
    resid, normed_two, grad_output, other, *ahead = feed_square(
        0, True, (norm2_gain, norm2_bias, token_rows, attended, w_out, cotangent, their_cotangent)
    )
    units["core" + names[0]] = Once(other, swap_cores)

    def chunk_own(number):
        name = names[number]

        def run(ahead):
            own, *ahead = feed_square(number, False, (normed_two, *ahead, grad_output))
            units[name] = Sum(
                [own, units["core" + name].received], [first, second, third], adding, [third, second, first]
            )
            if number == squares - 1:
                theirs, found["output"], *ahead = ahead
                units["out"] = Once(theirs, swap_cores)
            return ahead

        return run

    def chunk_other(number):
        def run(ahead):
            other, *ahead = feed_square(number, True, (normed_two, *ahead, grad_output))
            units["core" + names[number]] = Once(other, swap_cores)
            return ahead

        return run

    def chunk_middle(ahead):
        back_sum = ahead[-1]
        grad_resid, branch, grad_attended, norm_two = middle(
            resid, back_sum, grad_output, w_out, norm2_gain
        )
        found.update(grad_resid=grad_resid, branch=branch, norm_two=norm_two, back=())
        return grad_attended

    def chunk_attend(first_pair, pairs):
        def run(held):
            grads = held[0] if isinstance(held, tuple) else held
            found["back"] = attend_back(
                first_pair, pairs, found["back"], mixed, grads, attended, lse, projected, *masks
            )
            found["grads"] = grads
            return (grads, found["back"][0])

        return run

    def chunk_weights(held):
        mine, theirs = weight_grad(place, held[1], normed_one, attended, found["branch"])
        found["mine"] = mine
        units["core"] = Once(theirs, swap_cores)
        return held[1]

    def chunk_last(back):
        theirs, found["input_grad"], found["norm_one"] = last(
            place, back, weights, token_rows, found["grad_resid"], norm1_gain
        )
        units["h"] = Sum(
            [found["mine"], units["core"].received], [first, second, third], adding, [third, across]
        )
        small = jnp.concatenate([found["back"][1], found["norm_one"], found["norm_two"]], axis=0)
        units["small"] = Whole(small, [Stage(dp_bits, axis, axis) for axis in [cores, y] + dp])
        units["in"] = Once(theirs, swap_cores)
        return found["input_grad"]

    def chunk_spread(square, name):
        def run(held):
            pieces = list(units[name].pieces) + [units[name + str(i)].received for i in range(2)]
            found["spread"] = spread(
                place, square, w_in.shape[1], pieces, found.get("spread", ())
            )
            return found["spread"]

        return run

    plan = [
        (("corea",), (), chunk_own(0)),
        (("a",), (), chunk_other(1)),
        (("a", "coreb"), (), chunk_own(1)),
        (("a", "b", "out"), (), chunk_middle),
        (("a", "b"), ("out",), chunk_attend(0, width // LANES // 2)),
        (("a", "b"), (), chunk_attend(width // LANES // 2, width // LANES // 2)),
        (("a", "b"), (), chunk_weights),
        (("core", "a", "b"), (), chunk_last),
        (("h", "a0", "in", "small"), ("a",), None),
        (("h", "a1", "small"), ("a0", "in"), None),
        (("h", "b", "small"), ("a1",), chunk_spread(0, "a")),
        (("h", "b", "small"), (), None),
        (("h", "b0", "b1", "small"), ("b",), None),
        (("h",), ("b0", "b1"), chunk_spread(1, "b")),
    ]
    held = ahead
    for sent, arrived, chunk in plan:
        for name in sent:
            if name not in units:
                units[name] = Once(units[name[0]].pieces[int(name[1])], swap_cores)
        active, landed = [units[name] for name in sent], [units[name] for name in arrived]
        outgoing, received, held = lax.optimization_barrier(
            (tuple(unit.outgoing for unit in active), tuple(unit.received for unit in landed), held)
        )
        for unit, values in zip(landed, received):
            unit.land(values)
        for unit, values in zip(active, outgoing):
            unit.outgoing = values
            unit.start()
        if chunk:
            held = chunk(held)
        for unit in active:
            unit.finish()

    small = units["small"]
    while small.stages:
        small.start()
        small.finish()
    share = width // 4
    small = lax.dynamic_slice_in_dim(small.outgoing, group * share, share, 1)
    heads = jnp.concatenate(units["h"].pieces, axis=0)
    heads = [
        lax.dynamic_index_in_dim(heads, index ^ (2 * x_bit + z_bit), 0, keepdims=False).astype(F32)
        for index in range(4)
    ]
    qkv_grad = jnp.stack(heads[:3]).transpose(2, 0, 1)
    out_grad = heads[3]
    down_grad, in_grad = found["spread"]
    return (
        own_tokens(found["output"], units["out"].received),
        own_tokens(found["input_grad"], units["in"].received),
        small[9],
        small[10],
        qkv_grad,
        small[:9].reshape(3, 3, share),
        out_grad,
        small[11],
        small[12],
        in_grad,
        down_grad,
    )


def solution(mesh):
    placed = (
        P(None, ("dp", "mp"), None),
        P(None, "dp"),
        P(),
        P(),
        P(),
        P(None, None, "mp"),
        P(),
        P(),
        P(),
        P(),
        P(),
        P(None, ("dp", "mp"), None),
    )
    dp_bits = mesh.shape["dp"].bit_length() - 1
    return jax.shard_map(
        functools.partial(local, dp_bits),
        mesh=mesh,
        in_specs=placed,
        out_specs=(
            P(None, ("dp", "mp"), None),
            P(None, ("dp", "mp"), None),
            P("mp"),
            P("mp"),
            P(None, None, "mp"),
            P(None, None, "mp"),
            P("mp", None),
            P("mp"),
            P("mp"),
            P(),
            P(),
        ),
        check_vma=False,
    )
```

```python
import functools
import math

import jax
import jax.numpy as jnp
from jax import lax
from jax.experimental import pallas as pl
from jax.experimental.pallas import tpu as pltpu
from jax.sharding import PartitionSpec as P

HEAD_DIM = 64
LEN = 1024
LANES = 128
BLOCK = 256
FEED_ROWS = 256
EPSILON = 1e-05
MASKED = -1e30
F32 = jnp.float32
BF16 = jnp.bfloat16


def dot(a, b, dims):
    return lax.dot_general(a, b, (dims, ((), ())), preferred_element_type=F32)


def normalize(values, norm_gain, norm_bias):
    centred = values - jnp.mean(values, axis=-1, keepdims=True)
    rstd_row = lax.rsqrt(jnp.mean(centred * centred, axis=-1, keepdims=True) + EPSILON)
    scaled = centred * rstd_row
    return (scaled * norm_gain + norm_bias, scaled, rstd_row)


def normalize_back(gradient, scaled, rstd_row, norm_gain):
    grad_scaled = gradient * norm_gain
    inner_term = (
        grad_scaled
        - jnp.mean(grad_scaled, axis=-1, keepdims=True)
        - scaled * jnp.mean(grad_scaled * scaled, axis=-1, keepdims=True)
    )
    return (rstd_row * inner_term, jnp.sum(gradient * scaled, axis=0), jnp.sum(gradient, axis=0))


def attend_kernel(
    place, proj_q, proj_k, proj_v, taps, segments, mixed_out, attended, lse, same, seg_col, seg_row, bias
):
    q_out, k_out, v_out = mixed_out.at[0], mixed_out.at[1], mixed_out.at[2]

    @pl.when(pl.program_id(0) == 0)
    def _():
        numbers = jnp.where(place[0] == 0, segments[0:1, :], segments[1:2, :])
        seg_row[...] = jnp.broadcast_to(numbers, seg_row.shape)
        column = jnp.broadcast_to(numbers.astype(F32), (LANES, LEN)).T
        seg_col[...] = column.astype(jnp.int32)
        at = lax.broadcasted_iota(jnp.int32, (LEN, LANES), 0)
        for shift in (1, 2):
            equal = (at >= shift) & (pltpu.roll(column, shift, 0) == column)
            same[shift - 1] = jnp.where(equal, 1.0, 0.0)
        for first in range(0, LEN, BLOCK):
            width = first + BLOCK
            rows = first + lax.broadcasted_iota(jnp.int32, (BLOCK, width), 0)
            cols = lax.broadcasted_iota(jnp.int32, (BLOCK, width), 1)
            mine = jnp.concatenate([seg_col[first:width, :]] * (width // LANES), axis=1)
            allowed = (cols <= rows) & (mine == seg_row[0:1, :width])
            bias[first:width, :width] = jnp.where(allowed, 0.0, MASKED)

    same_one, same_two = same[0], same[1]
    for which, (source, target) in enumerate(((proj_q, q_out), (proj_k, k_out), (proj_v, v_out))):
        values = source[...].astype(F32)
        mixed = (
            values * taps[3 * which : 3 * which + 1, :]
            + pltpu.roll(values, 1, 0) * same_one * taps[3 * which + 1 : 3 * which + 2, :]
            + pltpu.roll(values, 2, 0) * same_two * taps[3 * which + 2 : 3 * which + 3, :]
        )
        target[...] = mixed.astype(BF16)
    scaling = 1.0 / math.sqrt(HEAD_DIM)
    lane = lax.broadcasted_iota(jnp.int32, (1, LANES), 1)
    for first in range(0, LEN, BLOCK):
        width = first + BLOCK
        queries = q_out[first:width, :] * jnp.asarray(scaling, BF16)
        parts = []
        for head in range(2):
            chosen = (lane >= HEAD_DIM) if head else (lane < HEAD_DIM)
            mine = jnp.where(chosen, queries, jnp.zeros_like(queries))
            scores = dot(mine, k_out[:width, :], ((1,), (1,))) + bias[first:width, :width]
            top = jnp.max(scores, axis=1, keepdims=True)
            weights = jnp.exp(scores - top)
            total = jnp.sum(weights, axis=1, keepdims=True)
            product = dot(weights.astype(BF16), v_out[:width, :], ((1,), (0,)))
            parts.append((product * (1.0 / total), top + jnp.log(total)))
        left = lane < HEAD_DIM
        attended[first:width, :] = jnp.where(left, parts[0][0], parts[1][0]).astype(BF16)
        logs = jnp.where(left, parts[0][1], parts[1][1])
        flipped = logs.T
        lse[0:1, first:width] = flipped[0:1, :]
        lse[1:2, first:width] = flipped[HEAD_DIM : HEAD_DIM + 1, :]


def attend_back_kernel(
    continued,
    *refs,
):
    attend_back_body(*(refs[2:] if continued else refs))


def attend_back_body(
    mixed_in,
    grads,
    attended,
    lse,
    proj_q,
    proj_k,
    proj_v,
    taps,
    same,
    seg_col,
    seg_row,
    back,
    tap_grads,
    bias,
    grad_k,
    grad_v,
    grad_qt,
    keys_t,
    inner,
):
    q_in, k_in, v_in = mixed_in.at[0], mixed_in.at[1], mixed_in.at[2]
    back_q, back_k, back_v = back.at[0], back.at[1], back.at[2]

    @pl.when(pl.program_id(0) == 0)
    def _():
        for first in range(0, LEN, BLOCK):
            width = first + BLOCK
            rows = lax.broadcasted_iota(jnp.int32, (width, BLOCK), 0)
            cols = first + lax.broadcasted_iota(jnp.int32, (width, BLOCK), 1)
            theirs = jnp.concatenate([seg_col[:width, :]] * (BLOCK // LANES), axis=1)
            allowed = (rows <= cols) & (theirs == seg_row[0:1, first:width])
            bias[:width, first:width] = jnp.where(allowed, 0.0, MASKED)

    scaling = 1.0 / math.sqrt(HEAD_DIM)
    lane = lax.broadcasted_iota(jnp.int32, (1, LANES), 1)
    keys_t[...] = k_in[...].T
    inner[...] = (grads[...].astype(F32) * attended[...].astype(F32)).T
    grad_k[...] = jnp.zeros_like(grad_k)
    grad_v[...] = jnp.zeros_like(grad_v)

    def one_head(head, _):
        low = pl.multiple_of(head * HEAD_DIM, HEAD_DIM)
        mine = pl.ds(low, HEAD_DIM)
        chosen = (lane >= low) & (lane < low + HEAD_DIM)
        inner_row = jnp.sum(inner[mine, :], axis=0, keepdims=True)
        for first in range(0, LEN, BLOCK):
            width = first + BLOCK
            queries = q_in[first:width, :] * jnp.asarray(scaling, BF16)
            queries = jnp.where(chosen, queries, jnp.zeros_like(queries))
            outer = grads[first:width, :]
            outer = jnp.where(chosen, outer, jnp.zeros_like(outer))
            scores = dot(k_in[:width, :], queries, ((1,), (1,))) + bias[:width, first:width]
            probs = jnp.exp(scores - lse[pl.ds(head, 1), first:width])
            grad_probs = dot(v_in[:width, :], outer, ((1,), (1,)))
            grad_scores = (probs * (grad_probs - inner_row[:, first:width])).astype(BF16)
            grad_v[:width, :] += dot(probs.astype(BF16), outer, ((1,), (0,)))
            grad_k[:width, :] += dot(grad_scores, queries, ((1,), (0,)))
            grad_qt[mine, first:width] = dot(keys_t[mine, :width], grad_scores, ((1,), (0,)))
        return 0

    lax.fori_loop(0, 2, one_head, 0)
    same_one, same_two = same[0], same[1]
    grad_q = grad_qt[...].T * scaling
    for which, (gradient, source, target) in enumerate(
        ((grad_q, proj_q, back_q), (grad_k[...], proj_k, back_k), (grad_v[...], proj_v, back_v))
    ):
        values = source[...].astype(F32)
        row = 3 * which
        after_one = pltpu.roll(gradient * same_one, LEN - 1, 0)
        after_two = pltpu.roll(gradient * same_two, LEN - 2, 0)
        tap_grads[row : row + 1, :] = jnp.sum(gradient * values, axis=0, keepdims=True)
        tap_grads[row + 1 : row + 2, :] = jnp.sum(after_one * values, axis=0, keepdims=True)
        tap_grads[row + 2 : row + 3, :] = jnp.sum(after_two * values, axis=0, keepdims=True)
        target[...] = (
            gradient * taps[row : row + 1, :]
            + after_one * taps[row + 1 : row + 2, :]
            + after_two * taps[row + 2 : row + 3, :]
        ).astype(BF16)


def whole(shape):
    return pl.BlockSpec(shape, lambda *_: (0,) * len(shape))


def cost(flops, moved, exps=0):
    return pl.CostEstimate(flops=int(flops), transcendentals=int(exps), bytes_accessed=int(moved))


def attend(place, projected, taps, segments):
    width = projected.shape[1] // 3
    pairs = width // LANES

    def column(offset):
        return pl.BlockSpec((LEN, LANES), lambda h, s, offset=offset: (0, offset + h))

    return pl.pallas_call(
        attend_kernel,
        grid_spec=pltpu.PrefetchScalarGridSpec(
            num_scalar_prefetch=1,
            grid=(pairs,),
            in_specs=[
                column(0),
                column(pairs),
                column(2 * pairs),
                pl.BlockSpec((9, LANES), lambda h, s: (0, h)),
                pl.BlockSpec((2, LEN), lambda h, s: (0, s[3])),
            ],
            out_specs=[
                pl.BlockSpec((3, LEN, LANES), lambda h, s: (0, 0, h)),
                column(0),
                pl.BlockSpec((None, 2, LEN), lambda h, s: (h, 0, 0)),
                whole((2, LEN, LANES)),
                whole((LEN, LANES)),
                whole((8, LEN)),
            ],
            scratch_shapes=[pltpu.VMEM((LEN, LEN), F32)],
        ),
        out_shape=[
            jax.ShapeDtypeStruct((3, LEN, width), BF16),
            jax.ShapeDtypeStruct((LEN, width), BF16),
            jax.ShapeDtypeStruct((pairs, 2, LEN), F32),
            jax.ShapeDtypeStruct((2, LEN, LANES), F32),
            jax.ShapeDtypeStruct((LEN, LANES), jnp.int32),
            jax.ShapeDtypeStruct((8, LEN), jnp.int32),
        ],
        cost_estimate=cost(4 * LEN * LEN * width, 16 * LEN * width, LEN * LEN * pairs),
        name="attend",
    )(place, projected, projected, projected, taps, segments)


def attend_back(first_pair, pairs, so_far, mixed, grads, attended, lse, projected, taps, same, seg_col, seg_row):
    width = grads.shape[1]
    all_pairs = width // LANES

    def column(offset):
        return pl.BlockSpec((LEN, LANES), lambda h, offset=offset: (0, first_pair + offset + h))

    stack = pl.BlockSpec((3, LEN, LANES), lambda h: (0, 0, first_pair + h))
    rows = pl.BlockSpec((9, LANES), lambda h: (0, first_pair + h))
    there = [pl.BlockSpec(memory_space=pl.ANY)] * 2 if so_far else []
    taken = pairs * LANES
    return pl.pallas_call(
        functools.partial(attend_back_kernel, bool(so_far)),
        grid=(pairs,),
        in_specs=there
        + [
            stack,
            column(0),
            column(0),
            pl.BlockSpec((None, 2, LEN), lambda h: (first_pair + h, 0, 0)),
            column(0),
            column(all_pairs),
            column(2 * all_pairs),
            rows,
            whole((2, LEN, LANES)),
            whole((LEN, LANES)),
            whole((8, LEN)),
        ],
        out_specs=[stack, rows],
        out_shape=[
            jax.ShapeDtypeStruct((3, LEN, width), BF16),
            jax.ShapeDtypeStruct((9, width), F32),
        ],
        scratch_shapes=[
            pltpu.VMEM((LEN, LEN), F32),
            pltpu.VMEM((LEN, LANES), F32),
            pltpu.VMEM((LEN, LANES), F32),
            pltpu.VMEM((LANES, LEN), F32),
            pltpu.VMEM((LANES, LEN), BF16),
            pltpu.VMEM((LANES, LEN), F32),
        ],
        input_output_aliases={0: 0, 1: 1} if so_far else {},
        cost_estimate=cost(10 * LEN * LEN * taken, 22 * LEN * taken, LEN * LEN * pairs),
        name="attend_back",
    )(*so_far, mixed, grads, attended, lse, projected, projected, projected, taps, same, seg_col, seg_row)


def front_kernel(continued, place, *refs):
    tokens, gain, offset, weights, projected, normed, rows_out = refs[3:] if continued else refs

    @pl.when(pl.program_id(0) == 0)
    def _():
        rows_out[...] = tokens[...]
        value, _, _ = normalize(tokens[...].astype(F32), row_of(gain), row_of(offset))
        normed[...] = value.astype(BF16)

    projected[...] = dot(normed[...], weights[...], ((1,), (0,))).astype(BF16)


def row_of(vector):
    return vector[...].reshape(1, vector.shape[0])


def front(place, tokens, gain, offset, weights, so_far):
    _, half, width = tokens.shape
    other = int(bool(so_far))
    mine = pl.BlockSpec((half, width), lambda j, s: (s[0] ^ other, 0))
    return pl.pallas_call(
        functools.partial(front_kernel, bool(so_far)),
        grid_spec=pltpu.PrefetchScalarGridSpec(
            num_scalar_prefetch=1,
            grid=(3,),
            in_specs=[pl.BlockSpec(memory_space=pl.ANY)] * len(so_far)
            + [
                pl.BlockSpec((None, half, width), lambda j, s: (s[0], 0, 0)),
                whole((width,)),
                whole((width,)),
                pl.BlockSpec((None, width, width), lambda j, s: (j, 0, 0)),
            ],
            out_specs=[pl.BlockSpec((half, width), lambda j, s: (s[0] ^ other, j)), mine, mine],
        ),
        out_shape=[
            jax.ShapeDtypeStruct((2 * half, 3 * width), BF16),
            jax.ShapeDtypeStruct((2 * half, width), BF16),
            jax.ShapeDtypeStruct((2 * half, width), BF16),
        ],
        input_output_aliases={1: 0, 2: 1, 3: 2} if so_far else {},
        cost_estimate=cost(6 * half * width * width, 14 * half * width + 6 * width * width),
        name="front",
    )(place, *so_far, tokens, gain, offset, weights)


def feed_kernel(number, other, first, last, place, *refs):
    core, here = place[0], place[1 + other]
    square = 2 * number + (core ^ other)
    if first:
        gain, offset, tokens, attended, w_out, mine, theirs, w_in, w_down = refs[:9]
        resid_out, normed_out, grads_out, parts_out, out, back_out = refs[9:15]
        tokens_held, attended_held, weights_held = refs[-3:]
        scratch = refs[15:-3]
    else:
        normed_in, out_in, back_in, grads_in, w_in, w_down = refs[:6]
        if last:
            parts_out, out_theirs, out_mine, back_out = refs[6:10]
            result_low = refs[-1]
            scratch = refs[10:-1]
        else:
            parts_out, out, back_out = refs[6:9]
            scratch = refs[9:]
    lefts, rights, in_block, down_block, total, back, parts, sems, row_sems = scratch
    hidden, normed, grads, grad_pre = lefts.at[0], lefts.at[1], rights.at[0], rights.at[1]
    count = normed.shape[0]
    width = in_block.shape[1]
    half = normed.shape[0] // 2
    columns = pl.ds(pl.multiple_of(square * width, width), width)
    my_rows = pl.ds(pl.multiple_of(core * half, half), half)
    their_rows = pl.ds(pl.multiple_of((1 - core) * half, half), half)
    flights = []

    def copy(source, target):
        flight = pltpu.make_async_copy(source, target, sems.at[len(flights)])
        flights.append(flight)
        flight.start()
        return flight

    if first:
        early = [copy(attended, attended_held), copy(w_out, weights_held), copy(tokens, tokens_held)]
        for flight in early:
            flight.wait()
        later = [
            copy(w_in.at[:, columns], in_block),
            copy(mine.at[core], grads.at[my_rows, :]),
            copy(theirs.at[core], grads.at[their_rows, :]),
            copy(w_down.at[columns, :], down_block),
        ]
    else:
        later = [
            copy(normed_in, normed),
            copy(w_in.at[:, columns], in_block),
            copy(grads_in, grads),
            copy(w_down.at[columns, :], down_block),
        ]
    writes = []
    if first:

        def begin(step, _):
            at = pl.ds(pl.multiple_of(step * BLOCK, BLOCK), BLOCK)
            product = dot(attended_held[at, :], weights_held[...], ((1,), (0,)))
            value = tokens_held[at, :].astype(F32) + product
            total[at, :] = value
            value, _, _ = normalize(value, row_of(gain), row_of(offset))
            normed[at, :] = value.astype(BF16)
            return 0

        lax.fori_loop(0, count // BLOCK, begin, 0)
        resid_flight = copy(total, resid_out)
        writes.append(copy(normed, normed_out))
    for flight in later:
        flight.wait()
    if not first:
        total_in = copy(out_in, total)
        back_so_far = copy(back_in, back)
    if first:
        writes.append(copy(grads, grads_out))
    size = FEED_ROWS

    def inner(step, _):
        at = pl.ds(pl.multiple_of(step * size, size), size)
        active = jnp.maximum(dot(normed[at, :], in_block[...], ((1,), (0,))), 0.0)
        hidden[at, :] = (active * active).astype(BF16)
        grad_hidden = dot(grads[at, :], down_block[...], ((1,), (1,)))
        grad_pre[at, :] = (grad_hidden * 2.0 * active).astype(BF16)
        return 0

    lax.fori_loop(0, count // size, inner, 0)
    blocks, _, rows, _ = parts.shape
    taken = width // 2

    def weigh(step, _):
        which, half_at = step // 2, step % 2
        at = pl.ds(pl.multiple_of(half_at * taken, taken), taken)
        product = dot(lefts[which, :, at], rights[which], ((0,), (0,))).astype(BF16)
        for index in range(blocks // 2):
            target = (half_at * (blocks // 2) + index) ^ here
            parts[target, which, :, :] = product[index * rows : (index + 1) * rows, :]
        return 0

    lax.fori_loop(0, 4, weigh, 0)
    writes.append(copy(parts, parts_out))
    if first:
        resid_flight.wait()
    else:
        total_in.wait()
        back_so_far.wait()

    def row_copies(step):
        at = pl.ds(pl.multiple_of(step * size, size), size)
        flights = [pltpu.make_async_copy(back.at[at, :], back_out.at[at, :], row_sems.at[0, step])]
        if not last:
            flights.append(pltpu.make_async_copy(total.at[at, :], out.at[at, :], row_sems.at[1, step]))
        return flights

    def outer(step, _):
        at = pl.ds(pl.multiple_of(step * size, size), size)
        value = total[at, :] + dot(hidden[at, :], down_block[...], ((1,), (0,)))
        if last:
            result_low[at, :] = value.astype(BF16)
        else:
            total[at, :] = value
        product = dot(grad_pre[at, :], in_block[...], ((1,), (1,)))
        back[at, :] = product if first else back[at, :] + product
        for flight in row_copies(step):
            flight.start()
        return 0

    lax.fori_loop(0, count // size, outer, 0)
    if last:
        writes.append(copy(result_low.at[their_rows, :], out_theirs))
        writes.append(copy(result_low.at[my_rows, :], out_mine))
    for step in range(count // size):
        for flight in row_copies(step):
            flight.wait()
    for flight in writes:
        flight.wait()


def feed(number, other, last, place, ahead, w_in, w_down):
    first = len(ahead) == 7
    rows, width = ahead[2].shape
    sums = jax.ShapeDtypeStruct((rows, width), F32)
    low = jax.ShapeDtypeStruct((rows, width), BF16)
    half = jax.ShapeDtypeStruct((rows // 2, width), BF16)
    out_shape = [jax.ShapeDtypeStruct((8, 2, width // 8, width), BF16)]
    if first:
        out_shape = [sums, low, low] + out_shape
    out_shape += [half, half, sums] if last else [sums, sums]
    anywhere = pl.BlockSpec(memory_space=pl.ANY)
    in_specs = [anywhere] * (len(ahead) + 2)
    if first:
        in_specs[:2] = [whole((width,))] * 2
    held = [
        pltpu.VMEM((2, rows, width), BF16),
        pltpu.VMEM((2, rows, width), BF16),
        pltpu.VMEM((width, width), BF16),
        pltpu.VMEM((width, width), BF16),
        pltpu.VMEM((rows, width), F32),
        pltpu.VMEM((rows, width), F32),
        pltpu.VMEM((8, 2, width // 8, width), BF16),
        pltpu.SemaphoreType.DMA((16,)),
        pltpu.SemaphoreType.DMA((2, rows // FEED_ROWS)),
    ]
    if first:
        held += [
            pltpu.VMEM((rows, width), BF16),
            pltpu.VMEM((rows, width), BF16),
            pltpu.VMEM((width, width), BF16),
        ]
    if last:
        held.append(pltpu.VMEM((rows, width), BF16))
    return pl.pallas_call(
        functools.partial(feed_kernel, number, int(other), first, last),
        grid_spec=pltpu.PrefetchScalarGridSpec(
            num_scalar_prefetch=1,
            grid=(1,),
            in_specs=in_specs,
            out_specs=[anywhere] * len(out_shape),
            scratch_shapes=held,
        ),
        out_shape=out_shape,
        cost_estimate=cost(12 * rows * width * width, 16 * rows * width + 8 * width * width),
        name="feed",
    )(place, *ahead, w_in, w_down)


def middle_kernel(
    resid, gradient, grads, w_out, gain, grad_resid, branch_out, grad_attended, norm_grads
):
    _, scaled, rstd = normalize(resid[...], 1.0, 0.0)
    inner, gain_part, bias_part = normalize_back(gradient[...], scaled, rstd, row_of(gain))
    sums = jnp.concatenate([gain_part[None], bias_part[None]], axis=0)
    whole_grad = grads[...].astype(F32) + inner
    grad_resid[...] = whole_grad
    branch = whole_grad.astype(BF16)
    branch_out[...] = branch
    grad_attended[...] = dot(branch, w_out[...], ((1,), (1,))).astype(BF16)
    before = jnp.where(pl.program_id(0) == 0, 0.0, norm_grads[...])
    norm_grads[...] = jnp.where(pl.program_id(0) == 0, sums, before + sums)


def middle(resid, gradient, grads, w_out, gain):
    rows, width = resid.shape
    block = pl.BlockSpec((BLOCK, width), lambda j: (j, 0))
    return pl.pallas_call(
        middle_kernel,
        grid=(rows // BLOCK,),
        in_specs=[block] * 3 + [whole((width, width)), whole((width,))],
        out_specs=[block, block, block, whole((2, width))],
        out_shape=[
            jax.ShapeDtypeStruct((rows, width), F32),
            jax.ShapeDtypeStruct((rows, width), BF16),
            jax.ShapeDtypeStruct((rows, width), BF16),
            jax.ShapeDtypeStruct((2, width), F32),
        ],
        cost_estimate=cost(2 * rows * width * width, 18 * rows * width),
        name="middle",
    )(resid, gradient, grads, w_out, gain)


def weight_kernel(place, back, normed, attended, branch, mine, theirs):
    step = pl.program_id(0)
    core = place[0]

    def write(left, right):
        product = dot(left[...], right[...], ((0,), (0,))).astype(BF16)
        share = product.shape[0] // 4
        for half in range(2):
            for target, owner, here in ((mine, core, place[1]), (theirs, 1 - core, place[2])):
                high, low = step >> 1, step & 1
                even, odd = 4 * high + 2 * half + low, 4 * half + 2 * high + low
                at = ((1 - owner) * even + owner * odd) ^ here
                first = product[2 * half * share : (2 * half + 1) * share]
                second = product[(2 * half + 1) * share : (2 * half + 2) * share]
                target[at, :, :] = jnp.where(owner == 0, first, second)

    pl.when(step < 3)(lambda: write(back, normed))
    pl.when(step >= 3)(lambda: write(attended, branch))


def weight_grad(place, back, normed, attended, branch):
    _, rows, width = back.shape
    share = width // 4
    return pl.pallas_call(
        weight_kernel,
        grid_spec=pltpu.PrefetchScalarGridSpec(
            num_scalar_prefetch=1,
            grid=(4,),
            in_specs=[pl.BlockSpec((None, rows, width), lambda t, s: (jnp.minimum(t, 2), 0, 0))]
            + [whole((rows, width))] * 3,
            out_specs=[whole((8, share, width))] * 2,
        ),
        out_shape=[jax.ShapeDtypeStruct((8, share, width), BF16)] * 2,
        cost_estimate=cost(8 * rows * width * width, 20 * rows * width),
        name="weight_grad",
    )(place, back, normed, attended, branch)


def spread_kernel(place, *refs):
    pieces, (down, into) = refs[:4], refs[-2:]
    step = pl.program_id(0)
    rows = pieces[0].shape[2]
    odd = place[1 + step // 4] & 1
    parts = 2
    size = rows // parts
    for number, piece in enumerate(pieces):

        @pl.when(step // 2 == number)
        def _():
            def move(number, _):
                index, part = number // parts, number % parts
                source = pl.ds(pl.multiple_of(part * size, size), size)
                target = pl.ds(pl.multiple_of((index ^ odd) * rows + part * size, size), size)
                down[target, :] = piece[index, 0, source, :].astype(F32)
                into[target, :] = piece[index, 1, source, :].astype(F32)
                return 0

            lax.fori_loop(0, 2 * parts, move, 0)


def spread(place, square, units, pieces, so_far):
    _, _, rows, width = pieces[0].shape

    def taken(number):
        return pl.BlockSpec(
            (2, 2, rows, width), lambda t, s: (jnp.clip(t - 2 * number, 0, 1), 0, 0, 0)
        )

    def pair(t, s):
        return (t & 3) ^ (jnp.where(t < 4, s[1], s[2]) >> 1)

    def column(t, s):
        return 2 * square + (s[0] ^ (t >> 2))

    return pl.pallas_call(
        spread_kernel,
        grid_spec=pltpu.PrefetchScalarGridSpec(
            num_scalar_prefetch=1,
            grid=(8,),
            in_specs=[taken(number) for number in range(4)]
            + [pl.BlockSpec(memory_space=pl.ANY)] * len(so_far),
            out_specs=[
                pl.BlockSpec((2 * rows, width), lambda t, s: (4 * column(t, s) + pair(t, s), 0)),
                pl.BlockSpec((2 * rows, width), lambda t, s: (pair(t, s), column(t, s))),
            ],
        ),
        out_shape=[
            jax.ShapeDtypeStruct((units, width), F32),
            jax.ShapeDtypeStruct((width, units), F32),
        ],
        input_output_aliases={5: 0, 6: 1} if so_far else {},
        cost_estimate=cost(0, 24 * width * width),
        name="spread",
    )(place, *pieces, *so_far)


def last_kernel(place, back, weights, tokens, grad_resid, gain, theirs, mine, norm_grads):
    step = pl.program_id(0)
    gradient = dot(back[0], weights[0], ((1,), (1,)))
    gradient += dot(back[1], weights[1], ((1,), (1,)))
    gradient += dot(back[2], weights[2], ((1,), (1,)))
    _, scaled, rstd = normalize(tokens[...].astype(F32), 1.0, 0.0)
    inner, gain_part, bias_part = normalize_back(gradient, scaled, rstd, row_of(gain))
    sums = jnp.concatenate([gain_part[None], bias_part[None]], axis=0)
    result = grad_resid[...] + inner
    half = pl.num_programs(0) // 2

    @pl.when(step < half)
    def _():
        theirs[...] = result.astype(BF16)

    @pl.when(step >= half)
    def _():
        mine[...] = result

    before = jnp.where(step == 0, 0.0, norm_grads[...])
    norm_grads[...] = jnp.where(step == 0, sums, before + sums)


def last(place, back, weights, tokens, grad_resid, gain):
    rows, width = tokens.shape
    steps = rows // BLOCK
    half = steps // 2

    def turn(j, s):
        return (j + half * (1 - s[0])) % steps

    block = pl.BlockSpec((BLOCK, width), lambda j, s: (turn(j, s), 0))
    return pl.pallas_call(
        last_kernel,
        grid_spec=pltpu.PrefetchScalarGridSpec(
            num_scalar_prefetch=1,
            grid=(steps,),
            in_specs=[
                pl.BlockSpec((3, BLOCK, width), lambda j, s: (0, turn(j, s), 0)),
                whole((3, width, width)),
                block,
                block,
                whole((width,)),
            ],
            out_specs=[
                pl.BlockSpec((BLOCK, width), lambda j, s: (jnp.minimum(j, half - 1), 0)),
                pl.BlockSpec((BLOCK, width), lambda j, s: (jnp.maximum(j - half, 0), 0)),
                whole((2, width)),
            ],
        ),
        out_shape=[
            jax.ShapeDtypeStruct((rows // 2, width), BF16),
            jax.ShapeDtypeStruct((rows // 2, width), F32),
            jax.ShapeDtypeStruct((2, width), F32),
        ],
        cost_estimate=cost(6 * rows * width * width, 16 * rows * width + 6 * width * width),
        name="last",
    )(place, back, weights, tokens, grad_resid, gain)


def bit_of(axis, bit):
    return (lax.axis_index(axis) >> bit) & 1


def swap(values, axis, bit):
    count = lax.axis_size(axis)
    return lax.ppermute(values, axis, [(i, i ^ (1 << bit)) for i in range(count)])


class Stage:
    def __init__(self, dp_bits, even, odd):
        flips = [1 << (bit + 2 if axis == "dp" else bit) for axis, bit in (even, odd)]
        self.pairs = [(index, index ^ flips[index & 1]) for index in range(4 << dp_bits)]

    def send(self, values):
        return lax.ppermute(values, ("dp", "mp"), self.pairs)


class Sum:
    def __init__(self, terms, halving, adding, doubling):
        self.terms = terms
        self.count = terms[0].shape[0]
        self.halving, self.adding, self.doubling = list(halving), list(adding), list(doubling)
        self.pieces = None
        self.prepare()

    def total(self, low, high):
        if len(self.terms) == 2:
            return self.terms[0][low:high] + self.terms[1][low:high]
        result = None
        for term in self.terms:
            term = term[low:high].astype(F32)
            result = term if result is None else result + term
        return result.astype(BF16)

    def land(self, values):
        self.received = self.pieces[1] = values

    def prepare(self):
        if self.halving:
            self.outgoing = self.total(self.count // 2, self.count)
        elif self.terms:
            self.outgoing = self.total(0, self.count)

    def start(self):
        stage = (self.halving or self.adding or self.doubling)[0]
        self.received = stage.send(self.outgoing)

    def finish(self):
        if self.halving:
            self.halving.pop(0)
            self.count //= 2
            self.terms.append(self.received)
            self.prepare()
        elif self.adding:
            self.adding.pop(0)
            self.terms = [self.outgoing, self.received]
            self.prepare()
            if self.adding:
                self.start()
                self.finish()
        else:
            self.doubling.pop(0)
            self.terms = []
            self.pieces = [self.outgoing, self.received]
            if self.doubling:
                self.outgoing = jnp.concatenate(self.pieces, axis=0)


class Whole:
    def __init__(self, values, stages):
        self.outgoing, self.stages = values, list(stages)

    def start(self):
        self.received = self.stages.pop(0).send(self.outgoing)

    def finish(self):
        self.outgoing = self.outgoing + self.received


class Once:
    def __init__(self, values, stage):
        self.outgoing, self.stage = values, stage

    def start(self):
        self.received = self.stage.send(self.outgoing)

    def finish(self):
        pass

    def land(self, values):
        self.received = values


def local(
    dp_bits,
    tokens,
    segment_ids,
    norm1_gain,
    norm1_bias,
    w_qkv,
    conv_weight,
    w_out,
    norm2_gain,
    norm2_bias,
    w_in,
    w_down,
    cotangent,
):
    width = tokens.shape[2]
    core = bit_of("mp", 0)
    group = lax.axis_index("mp")
    rows = tokens.shape[1]

    def own_tokens(mine, theirs):
        at = lax.broadcasted_iota(jnp.int32, (2, 1, 1), 0)
        return jnp.where(at == core, mine[None], theirs.astype(mine.dtype)[None])

    dp = [("dp", bit) for bit in range(dp_bits)]
    y, cores = ("mp", 1), ("mp", 0)
    swap_cores = Stage(dp_bits, cores, cores)
    first, second = Stage(dp_bits, dp[0], y), Stage(dp_bits, y, dp[0])
    third = Stage(dp_bits, dp[1], dp[1])
    across = Stage(dp_bits, dp[0], dp[0])
    adding = [Stage(dp_bits, axis, axis) for axis in dp[2:]]
    x_bit, y_bit, z_bit = bit_of(*dp[0]), bit_of(*y), bit_of(*dp[1])
    here_even, here_odd = 4 * x_bit + 2 * y_bit + z_bit, 4 * y_bit + 2 * x_bit + z_bit
    here = jnp.where(core == 0, here_even, here_odd)
    here_theirs = jnp.where(core == 0, here_odd, here_even)
    place = jnp.stack([core, here, here_theirs, y_bit])

    their_tokens = swap(tokens, "mp", 0)
    taps_local, their_tokens = lax.optimization_barrier(
        (conv_weight.reshape(9, conv_weight.shape[2]), their_tokens)
    )
    their_cotangent = swap(cotangent, "mp", 0)
    pieces = [taps_local]
    for offset in range(1, 4):
        pieces.append(lax.ppermute(taps_local, "mp", [(i, i ^ offset) for i in range(4)]))
    stacked = jnp.stack(pieces, axis=0)
    taps = jnp.concatenate(
        [lax.dynamic_index_in_dim(stacked, group ^ i, 0, keepdims=False) for i in range(4)], axis=1
    )

    weights = w_qkv.transpose(1, 0, 2)
    so_far = front(place, tokens, norm1_gain, norm1_bias, weights, ())
    projected, normed_one, token_rows = front(
        place, their_tokens, norm1_gain, norm1_bias, weights, so_far
    )
    projected, their_cotangent = lax.optimization_barrier((projected, their_cotangent))
    mixed, attended, lse, *masks = attend(place, projected, taps, segment_ids)
    masks = (taps, *masks)

    def feed_square(number, other, ahead):
        final = number == squares - 1 and not other
        return feed(number, other, final, place, ahead, w_in, w_down)

    squares = w_in.shape[1] // width // 2
    names = "abcdefgh"[:squares]
    found, units = {}, {}
    resid, normed_two, grad_output, other, *ahead = feed_square(
        0, True, (norm2_gain, norm2_bias, token_rows, attended, w_out, cotangent, their_cotangent)
    )
    units["core" + names[0]] = Once(other, swap_cores)

    def chunk_own(number):
        name = names[number]

        def run(ahead):
            own, *ahead = feed_square(number, False, (normed_two, *ahead, grad_output))
            units[name] = Sum(
                [own, units["core" + name].received], [first, second, third], adding, [third, second, first]
            )
            if number == squares - 1:
                theirs, found["output"], *ahead = ahead
                units["out"] = Once(theirs, swap_cores)
            return ahead

        return run

    def chunk_other(number):
        def run(ahead):
            other, *ahead = feed_square(number, True, (normed_two, *ahead, grad_output))
            units["core" + names[number]] = Once(other, swap_cores)
            return ahead

        return run

    def chunk_middle(ahead):
        back_sum = ahead[-1]
        grad_resid, branch, grad_attended, norm_two = middle(
            resid, back_sum, grad_output, w_out, norm2_gain
        )
        found.update(grad_resid=grad_resid, branch=branch, norm_two=norm_two, back=())
        return grad_attended

    def chunk_attend(first_pair, pairs):
        def run(held):
            grads = held[0] if isinstance(held, tuple) else held
            found["back"] = attend_back(
                first_pair, pairs, found["back"], mixed, grads, attended, lse, projected, *masks
            )
            found["grads"] = grads
            return (grads, found["back"][0])

        return run

    def chunk_weights(held):
        mine, theirs = weight_grad(place, held[1], normed_one, attended, found["branch"])
        found["mine"] = mine
        units["core"] = Once(theirs, swap_cores)
        return held[1]

    def chunk_last(back):
        theirs, found["input_grad"], found["norm_one"] = last(
            place, back, weights, token_rows, found["grad_resid"], norm1_gain
        )
        units["h"] = Sum(
            [found["mine"], units["core"].received], [first, second, third], adding, [third, across]
        )
        small = jnp.concatenate([found["back"][1], found["norm_one"], found["norm_two"]], axis=0)
        units["small"] = Whole(small, [Stage(dp_bits, axis, axis) for axis in [cores, y] + dp])
        units["in"] = Once(theirs, swap_cores)
        return found["input_grad"]

    def chunk_spread(square, name):
        def run(held):
            pieces = list(units[name].pieces) + [units[name + str(i)].received for i in range(2)]
            found["spread"] = spread(
                place, square, w_in.shape[1], pieces, found.get("spread", ())
            )
            return found["spread"]

        return run

    plan = [
        (("corea",), (), chunk_own(0)),
        (("a",), (), chunk_other(1)),
        (("a", "coreb"), (), chunk_own(1)),
        (("a", "b", "out"), (), chunk_middle),
        (("a", "b"), ("out",), chunk_attend(0, width // LANES // 2)),
        (("a", "b"), (), chunk_attend(width // LANES // 2, width // LANES // 2)),
        (("a", "b"), (), chunk_weights),
        (("core", "a", "b"), (), chunk_last),
        (("h", "a0", "in", "small"), ("a",), None),
        (("h", "a1", "small"), ("a0", "in"), None),
        (("h", "b", "small"), ("a1",), None),
        (("h", "b", "small"), (), chunk_spread(0, "a")),
        (("h", "b0", "b1", "small"), ("b",), None),
        (("h",), ("b0", "b1"), chunk_spread(1, "b")),
    ]
    held = ahead
    for sent, arrived, chunk in plan:
        for name in sent:
            if name not in units:
                units[name] = Once(units[name[0]].pieces[int(name[1])], swap_cores)
        active, landed = [units[name] for name in sent], [units[name] for name in arrived]
        outgoing, received, held = lax.optimization_barrier(
            (tuple(unit.outgoing for unit in active), tuple(unit.received for unit in landed), held)
        )
        for unit, values in zip(landed, received):
            unit.land(values)
        for unit, values in zip(active, outgoing):
            unit.outgoing = values
            unit.start()
        if chunk:
            held = chunk(held)
        for unit in active:
            unit.finish()

    small = units["small"]
    while small.stages:
        small.start()
        small.finish()
    share = width // 4
    small = lax.dynamic_slice_in_dim(small.outgoing, group * share, share, 1)
    heads = jnp.concatenate(units["h"].pieces, axis=0)
    heads = [
        lax.dynamic_index_in_dim(heads, index ^ (2 * x_bit + z_bit), 0, keepdims=False).astype(F32)
        for index in range(4)
    ]
    qkv_grad = jnp.stack(heads[:3]).transpose(2, 0, 1)
    out_grad = heads[3]
    down_grad, in_grad = found["spread"]
    return (
        own_tokens(found["output"], units["out"].received),
        own_tokens(found["input_grad"], units["in"].received),
        small[9],
        small[10],
        qkv_grad,
        small[:9].reshape(3, 3, share),
        out_grad,
        small[11],
        small[12],
        in_grad,
        down_grad,
    )


def solution(mesh):
    placed = (
        P(None, ("dp", "mp"), None),
        P(None, "dp"),
        P(),
        P(),
        P(),
        P(None, None, "mp"),
        P(),
        P(),
        P(),
        P(),
        P(),
        P(None, ("dp", "mp"), None),
    )
    dp_bits = mesh.shape["dp"].bit_length() - 1
    return jax.shard_map(
        functools.partial(local, dp_bits),
        mesh=mesh,
        in_specs=placed,
        out_specs=(
            P(None, ("dp", "mp"), None),
            P(None, ("dp", "mp"), None),
            P("mp"),
            P("mp"),
            P(None, None, "mp"),
            P(None, None, "mp"),
            P("mp", None),
            P("mp"),
            P("mp"),
            P(),
            P(),
        ),
        check_vma=False,
    )
```
